256 devices in a mesh: mem: 8 (over y, x_lo), grid: 32 (over z, x_hi, core).
Axes of the slice: x: 4 (x_hi: 2, x_lo: 2; x = x_hi * 2 + x_lo), y: 4, z: 8, core: 2. Of those that a mesh axis runs over, the one named last changes fastest.
Arguments:
- ens_state: bfloat16 [80, 512, 512], P('mem', 'grid'), may hold values from -6 to 6
- obs_prior: bfloat16 [80, 12288, 128], P('mem', 'grid'), may hold values from -6 to 6
- obs_value: float32 [12288, 128], P('grid'), may hold values from -6 to 6
- obs_prec: float32 [12288, 128], P('grid'), may hold values from 0.01 to 0.2
- obs_len: int32 [12288], P('grid'), may hold values from 1 to 128, as said below
- pair_block: int32 [512, 256], P('grid'), may hold values from 0 to 12287, as said below
- obs_pos: float32 [12288, 128], P('grid'), may hold values from 0 to 512, as said below
Outputs:
- analysis: bfloat16 [80, 512, 512], P('mem', 'grid')
The draws below stay inside these ranges and needn't reach their ends.
Inputs may be any that keep to these rules, and one draw needn't show every extreme that they name: `obs_len`: count of valid slots of each observation block; slots at or past it are padding. Row b lists 256 distinct observation blocks; for each, pair_block[b,p] // 384 - b // 16 is -1, 0 or 1 modulo 12288 // 384. `obs_pos`: positions along the cyclic band of 512 state blocks.
All inputs are finite; a program needn't handle non-finite values. Where the reference program divides by a largest or mean magnitude, that divisor is 1e-20 or more.
Results may differ from the reference program's by a relative error of at most 0.0058.
Values may be sent and summed in bfloat16 or wider, within the bound.
No kernel may reach another device: no remote copies, remote signals or barrier semaphores. Data moves between devices by JAX's collectives and lax.ppermute only.
A program may use at most 128 MiB of HBM per device.

```python
import math
import jax
import jax.numpy as jnp
from jax import lax

K = 80
OW = 128
NB_DEV = 16
OB_DEV = 384
P_SIZE = 256
NSIT = 3
L = 512
NB = 512
NOB = 12288
LOCR = 8


def draw_obs_len(key, part):
    counts = jax.random.randint(key, (NOB,), 1, OW + 1, dtype=jnp.int32)
    spot = jax.random.randint(jax.random.fold_in(key, 7), (), 0, NOB, dtype=jnp.int32)
    return counts.at[spot].set(OW)


def draw_pair_block(key, part):
    blocks = jnp.arange(NB, dtype=jnp.int32)
    home = blocks // NB_DEV
    keys = jax.random.split(jax.random.fold_in(key, 11), NB)
    picks = jax.vmap(lambda one: jax.random.permutation(one, 3 * OB_DEV)[:P_SIZE])(keys).astype(jnp.int32)
    return ((home[:, None] - 1) * OB_DEV + picks) % NOB


def draw_obs_pos(key, part):
    frac = jax.random.uniform(jax.random.fold_in(key, 13), (NOB, OW), jnp.float32)
    start = jnp.arange(NOB, dtype=jnp.float32)[:, None]
    return (start + frac) * (NB / NOB)


def steps_of(own_key, shape, cuts, least, top_value):
    loudness = 1.0
    for dim, parts in cuts:
        steps = jax.random.uniform(jax.random.fold_in(jax.random.fold_in(own_key, 6), dim), (parts,), jnp.float32, least / len(cuts), top_value / len(cuts))
        loudness = loudness * jnp.repeat(jnp.exp(steps), shape[dim] // parts).reshape((-1,) + (1,) * (len(shape) - 1 - dim))
    return loudness


def scatter_about(own_key, dims, scale, most, pieces=(), kind=jnp.bfloat16):
    gain = steps_of(own_key, dims, pieces, -0.22, 0.18) if pieces else 1.0
    entries = jax.random.normal(own_key, dims, jnp.float32) * scale * gain
    return jnp.minimum(jnp.maximum(entries, -most), most).astype(kind)


def setup_inputs(seed: int = 0) -> dict:
    seeds = jax.random.split(jax.random.key(seed), 8)
    return {
        "ens_state": scatter_about(seeds[0], (K, NB, L), 1.0, 6.0, ((0, 8), (1, 32))),
        "obs_prior": scatter_about(seeds[1], (K, NOB, OW), 1.0, 6.0, ((0, 8), (1, 32))),
        "obs_value": scatter_about(seeds[2], (NOB, OW), 1.0, 6.0, ((0, 32),), jnp.float32),
        "obs_prec": jnp.clip(jnp.exp(math.log(0.2) - 2.9957323 * jax.random.uniform(seeds[3], (NOB, OW), jnp.float32) ** steps_of(seeds[3], (NOB, OW), ((0, 32),), -0.2, 0.2)), 0.01, 0.2),
        "obs_len": draw_obs_len(jax.random.fold_in(seeds[7], 71), 0),
        "pair_block": draw_pair_block(jax.random.fold_in(seeds[7], 71), 0),
        "obs_pos": draw_obs_pos(jax.random.fold_in(seeds[7], 71), 0),
    }


inflation = 1.1

def finish(gram_matrix, forcing):
    members = gram_matrix.shape[0]
    highest = lax.Precision.HIGHEST
    identity = jnp.eye(members, dtype=jnp.float32)
    system = gram_matrix + (members - 1) / inflation * identity
    bound_sum = jnp.max(lax.optimization_barrier(jnp.sum(jnp.abs(system), axis=1)))
    y_iter = system / bound_sum
    z_iter = identity
    for sweep in range(NSIT):
        factor = 1.5 * identity - 0.5 * jnp.dot(z_iter, y_iter, precision=highest)
        y_iter = jnp.dot(y_iter, factor, precision=highest)
        z_iter = jnp.dot(factor, z_iter, precision=highest)
    root_inv = z_iter / jnp.sqrt(bound_sum)
    mean_weight = jnp.dot(root_inv, jnp.dot(root_inv, forcing, precision=highest), precision=highest)
    return (math.sqrt(members - 1) * root_inv + mean_weight[:, None]).astype(jnp.bfloat16)

def block_transform(perturb, departure, obs_prec, obs_pos, block_ids, center, nb_total):
    highest = lax.Precision.HIGHEST
    chosen = jnp.take(perturb, block_ids, axis=1)
    position = jnp.take(obs_pos, block_ids, axis=0)
    distance = jnp.abs(position - center)
    distance = jnp.minimum(distance, nb_total - distance)
    relative = distance / LOCR
    weight = jnp.take(obs_prec, block_ids, axis=0) * jnp.exp(-0.5 * relative * relative)
    scaled = (chosen.astype(jnp.float32) * weight).astype(jnp.bfloat16)
    gram_matrix = jnp.einsum('ipk,jpk->ij', scaled.astype(jnp.float32), chosen.astype(jnp.float32), precision=highest)
    forcing = jnp.einsum('ipk,pk->i', scaled.astype(jnp.float32), jnp.take(departure, block_ids, axis=0), precision=highest)
    return finish(gram_matrix, forcing)

def reference(ens_state, obs_prior, obs_value, obs_prec, obs_len, pair_block, obs_pos):
    members = ens_state.shape[0]
    nb_total = ens_state.shape[1]
    obs_mean = lax.optimization_barrier(jnp.sum(obs_prior, axis=0, dtype=jnp.float32)) / members
    valid = lax.broadcasted_iota(jnp.int32, obs_mean.shape, 1) < obs_len[:, None]
    perturb = jnp.where(valid, obs_prior.astype(jnp.float32) - obs_mean, 0.0).astype(jnp.bfloat16)
    departure = jnp.where(valid, obs_value - obs_mean, 0.0)
    state_mean = lax.optimization_barrier(jnp.sum(ens_state, axis=0, dtype=jnp.float32)) / members
    deviation = (ens_state.astype(jnp.float32) - state_mean).astype(jnp.bfloat16)
    centers = jnp.arange(nb_total, dtype=jnp.float32) + 0.5

    def one_block(items):
        return block_transform(perturb, departure, obs_prec, obs_pos, items[0], items[1], nb_total)
    transforms = lax.map(one_block, (pair_block, centers))

    def one_update(items):
        return jnp.einsum('il,ij->jl', items[0].astype(jnp.float32), items[1].astype(jnp.float32), precision=lax.Precision.HIGHEST)
    moved = lax.map(one_update, (jnp.transpose(deviation, (1, 0, 2)), transforms))
    return (state_mean[None, :, :] + jnp.transpose(moved, (1, 0, 2))).astype(jnp.bfloat16)
```

```python
import functools
import math

import jax
import jax.numpy as jnp
from jax import lax
from jax.experimental import pallas as pl
from jax.experimental.pallas import tpu as pltpu
from jax.sharding import PartitionSpec as P

NSIT = 3
LOCR = 8
LANES = 128

inflation = 1.1


def shift(value, axis, step):
    count = lax.axis_size(axis)
    return lax.ppermute(value, axis, [(i, (i + step) % count) for i in range(count)])


def weight_kernel(nb_total, obs, base_ref, pairs_ref, centers_ref, prec_ref, pos_ref, out_ref):
    pairs = pairs_ref[...] - base_ref[0]
    centers = centers_ref[...]
    for o in range(obs):
        hit = jnp.max(jnp.where(pairs == o, 1.0, 0.0), axis=1, keepdims=True)
        gap = jnp.abs(pos_ref[o : o + 1, :] - centers)
        distance = jnp.minimum(gap, nb_total - gap)
        relative = distance * (1.0 / LOCR)
        weight = prec_ref[o : o + 1, :] * jnp.exp(-0.5 * relative * relative)
        out_ref[:, o * LANES : (o + 1) * LANES] = jnp.where(hit > 0.0, weight, 0.0)


def gram_kernel(members, obs, rows, blocks, chunk, batch, prior_ref, len_ref, value_ref, w_ref, out_ref, dev_ref, d_ref, acc_ref):
    total = prior_ref[0].astype(jnp.float32)
    for i in range(1, members):
        total = total + prior_ref[i].astype(jnp.float32)
    mean = total / members
    valid = lax.broadcasted_iota(jnp.int32, mean.shape, 1) < len_ref[...]
    for i in range(members):
        dev_ref[i * obs : (i + 1) * obs, :] = jnp.where(
            valid, prior_ref[i].astype(jnp.float32) - mean, 0.0
        )
    departure = jnp.where(valid, value_ref[...] - mean, 0.0)
    high = departure.astype(jnp.bfloat16).astype(jnp.float32)
    dev_ref[members * obs : (members + 1) * obs, :] = high
    dev_ref[(members + 1) * obs : (members + 2) * obs, :] = departure - high
    dev_ref[(members + 2) * obs : rows * obs, :] = jnp.zeros(((rows - members - 2) * obs, LANES), jnp.float32)
    for o in range(obs):
        d_ref[:, o * LANES : (o + 1) * LANES] = dev_ref[pl.ds(o, rows, stride=obs), :].astype(jnp.bfloat16)
    acc_ref[...] = jnp.zeros(acc_ref.shape, jnp.float32)
    width = chunk * LANES

    def step(c, carry):
        start = pl.multiple_of(c * width, width)
        full = d_ref[:, pl.ds(start, width)]
        d = full[:members]
        for b0 in range(0, blocks, batch):
            parts = []
            for b in range(b0, b0 + batch):
                w = jnp.broadcast_to(w_ref[b : b + 1, pl.ds(start, width)], (16, width)).astype(jnp.bfloat16)
                parts.append((d.reshape(members // 16, 16, width) * w[None]).reshape(members, width))
            scaled = jnp.concatenate(parts, axis=0)
            got = lax.dot_general(scaled, full, (((1,), (1,)), ((), ())), preferred_element_type=jnp.float32)
            acc_ref[b0 * members : (b0 + batch) * members, :] += got
        return carry

    lax.fori_loop(0, obs // chunk, step, 0)
    got = acc_ref[...]
    force = got[:, members : members + 1] + got[:, members + 1 : members + 2]
    high = force.astype(jnp.bfloat16).astype(jnp.float32)
    lane = lax.broadcasted_iota(jnp.int32, got.shape, 1)
    got = jnp.where(lane == members, high, jnp.where(lane == members + 1, force - high, got))
    out_ref[...] = got.astype(jnp.bfloat16)


def finish(gram_matrix, forcing):
    members = gram_matrix.shape[0]
    highest = lax.Precision.HIGHEST
    identity = jnp.eye(members, dtype=jnp.float32)
    system = gram_matrix + (members - 1) / inflation * identity
    bound_sum = jnp.max(jnp.sum(jnp.abs(system), axis=1))
    y_iter = system / bound_sum
    z_iter = identity
    for sweep in range(NSIT):
        factor = 1.5 * identity - 0.5 * jnp.dot(z_iter, y_iter, precision=highest)
        y_iter = jnp.dot(y_iter, factor, precision=highest)
        z_iter = jnp.dot(factor, z_iter, precision=highest)
    root_inv = z_iter / jnp.sqrt(bound_sum)
    mean_weight = jnp.dot(
        root_inv, jnp.dot(root_inv, forcing, precision=highest), precision=highest
    )
    return (math.sqrt(members - 1) * root_inv + mean_weight[:, None]).astype(jnp.bfloat16)


def per_device(ens_state, obs_prior, obs_value, obs_prec, obs_len, pair_block, obs_pos):
    mem_count = lax.axis_size("mem")
    grid_count = lax.axis_size("grid")
    local = ens_state.shape[0]
    members = mem_count * local
    blocks_dev = ens_state.shape[1]
    obs_blocks = obs_prior.shape[1]
    owned = blocks_dev // mem_count
    obs = obs_blocks // mem_count
    nb_total = blocks_dev * grid_count
    mem_pos = lax.axis_index("mem")
    grid_pos = lax.axis_index("grid")

    prior = lax.all_to_all(obs_prior, "mem", split_axis=1, concat_axis=0, tiled=True)
    state = lax.all_to_all(ens_state, "mem", split_axis=1, concat_axis=0, tiled=True)
    from_low = shift(pair_block, "grid", 1)
    from_high = shift(pair_block, "grid", -1)

    blocks = 3 * blocks_dev
    pairs = jnp.stack([from_low, pair_block, from_high])
    pairs = pairs.reshape(3, mem_count, owned, -1).transpose(1, 0, 2, 3).reshape(blocks, -1)
    places = (grid_pos + jnp.arange(-1, 2, dtype=jnp.int32)) % grid_count
    ids = places[None, :, None] * blocks_dev + (
        jnp.arange(mem_count, dtype=jnp.int32)[:, None, None] * owned
        + jnp.arange(owned, dtype=jnp.int32)[None, None, :]
    )
    centers = ids.reshape(blocks, 1).astype(jnp.float32) + 0.5

    def mine(value):
        return lax.dynamic_slice_in_dim(value, mem_pos * obs, obs, 0)

    base = (grid_pos * obs_blocks + mem_pos * obs).reshape(1)
    vmem = pl.BlockSpec(memory_space=pltpu.VMEM)
    weights = pl.pallas_call(
        functools.partial(weight_kernel, float(nb_total), obs),
        out_shape=jax.ShapeDtypeStruct((blocks, obs * LANES), jnp.float32),
        in_specs=[pl.BlockSpec(memory_space=pltpu.SMEM), vmem, vmem, vmem, vmem],
        out_specs=vmem,
        name="weights",
    )(base, pairs, centers, mine(obs_prec), mine(obs_pos))

    rows = -(-(members + 2) // 16) * 16
    partial = pl.pallas_call(
        functools.partial(gram_kernel, members, obs, rows, blocks, 2, 8),
        out_shape=jax.ShapeDtypeStruct((blocks * members, rows), jnp.bfloat16),
        in_specs=[vmem, vmem, vmem, vmem],
        out_specs=vmem,
        scratch_shapes=[
            pltpu.VMEM((rows * obs, LANES), jnp.float32),
            pltpu.VMEM((rows, obs * LANES), jnp.bfloat16),
            pltpu.VMEM((blocks * members, rows), jnp.float32),
        ],
        name="gram",
    )(prior, mine(obs_len)[:, None], mine(obs_value), weights)

    partial = partial.reshape(mem_count, 3 * owned, members, rows)
    swapped = lax.all_to_all(partial, "mem", split_axis=0, concat_axis=0, tiled=True)
    summed = jnp.sum(swapped.reshape(mem_count, 3, owned, members, rows), axis=0, dtype=jnp.float32)
    total = summed[1] + shift(summed[0], "grid", -1) + shift(summed[2], "grid", 1)
    forcing = total[:, :, members] + total[:, :, members + 1]
    transforms = jax.vmap(finish)(total[:, :, :members], forcing)

    state = state.astype(jnp.float32)
    state_mean = jnp.sum(state, axis=0) / members
    deviation = (state - state_mean).astype(jnp.bfloat16)
    product = lax.dot_general(
        transforms, deviation, (((1,), (0,)), ((0,), (1,))), preferred_element_type=jnp.float32
    )
    analysis = (state_mean[:, None, :] + product).astype(jnp.bfloat16)
    return lax.all_to_all(
        jnp.transpose(analysis, (1, 0, 2)), "mem", split_axis=0, concat_axis=1, tiled=True
    )


def solution(mesh):
    placed = (
        P("mem", "grid", None),
        P("mem", "grid", None),
        P("grid", None),
        P("grid", None),
        P("grid"),
        P("grid", None),
        P("grid", None),
    )
    return jax.shard_map(
        per_device, mesh=mesh, in_specs=placed, out_specs=P("mem", "grid", None), check_vma=False
    )
```

```python
import functools
import math

import jax
import jax.numpy as jnp
from jax import lax
from jax.experimental import pallas as pl
from jax.experimental.pallas import tpu as pltpu
from jax.sharding import PartitionSpec as P

NSIT = 3
LOCR = 8
LANES = 128

inflation = 1.1


def shift(value, axis, step):
    count = lax.axis_size(axis)
    return lax.ppermute(value, axis, [(i, (i + step) % count) for i in range(count)])


def pack_kernel(parts, size, src_ref, out_ref, sems):
    copies = [
        pltpu.make_async_copy(src_ref.at[:, m * size : (m + 1) * size, :], out_ref.at[m], sems.at[m])
        for m in range(parts)
    ]
    for copy in copies:
        copy.start()
    for copy in copies:
        copy.wait()


def weight_kernel(nb_total, obs, base_ref, pairs_ref, centers_ref, prec_ref, pos_ref, out_ref):
    pairs = pairs_ref[...] - base_ref[0]
    centers = centers_ref[...]
    for o in range(obs):
        hit = jnp.max(jnp.where(pairs == o, 1.0, 0.0), axis=1, keepdims=True)
        gap = jnp.abs(pos_ref[o : o + 1, :] - centers)
        distance = jnp.minimum(gap, nb_total - gap)
        relative = distance * (1.0 / LOCR)
        weight = prec_ref[o : o + 1, :] * jnp.exp(-0.5 * relative * relative)
        out_ref[:, o * LANES : (o + 1) * LANES] = jnp.where(hit > 0.0, weight, 0.0)


def accumulate(members, obs, first, blocks, chunk, batch, d_ref, w_ref, acc_ref):
    acc_ref[...] = jnp.zeros(acc_ref.shape, jnp.float32)
    width = chunk * LANES

    def step(c, carry):
        start = pl.multiple_of(c * width, width)
        full = d_ref[:, pl.ds(start, width)]
        d = full[:members].reshape(members // 16, 16, width)
        for b0 in range(0, blocks, batch):
            parts = []
            for b in range(b0, b0 + batch):
                row = w_ref[first + b : first + b + 1, pl.ds(start, width)]
                w = jnp.broadcast_to(row, (16, width)).astype(jnp.bfloat16)
                parts.append((d * w[None]).reshape(members, width))
            scaled = jnp.concatenate(parts, axis=0)
            acc_ref[b0 * members : (b0 + batch) * members, :] += lax.dot_general(
                scaled, full, (((1,), (1,)), ((), ())), preferred_element_type=jnp.float32
            )
        return carry

    lax.fori_loop(0, obs // chunk, step, 0)


def packed_system(members, blocks, acc_ref, out_ref):
    half = members // 2
    lane = lax.broadcasted_iota(jnp.int32, (half, LANES), 1)
    low = (lane == members + 2) | (lane == members + 3) | (lane >= LANES - half)
    for b in range(blocks):
        top = acc_ref[b * members : b * members + half, :]
        bottom = acc_ref[b * members + half : (b + 1) * members, :]
        out_ref[b * half : (b + 1) * half, :] = jnp.where(low, bottom, top).astype(out_ref.dtype)


def neighbour_kernel(members, obs, blocks, chunk, batch, prior_ref, len_ref, value_ref, w_ref, d_ref, low_ref, high_ref, dev_ref, acc_ref):
    half = members // 2
    total = prior_ref[0].astype(jnp.float32)
    for i in range(1, members):
        total = total + prior_ref[i].astype(jnp.float32)
    mean = total / members
    valid = lax.broadcasted_iota(jnp.int32, mean.shape, 1) < len_ref[...]
    for i in range(members):
        one = jnp.where(valid, prior_ref[i].astype(jnp.float32) - mean, 0.0)
        dev_ref[i * obs : (i + 1) * obs, :] = one
        if i >= half:
            at = LANES - members + i
            dev_ref[at * obs : (at + 1) * obs, :] = one
    departure = jnp.where(valid, value_ref[...] - mean, 0.0)
    high = departure.astype(jnp.bfloat16).astype(jnp.float32)
    for k in range(LANES - half - members):
        piece = (high, departure - high)[k % 2] if k < 4 else jnp.zeros(mean.shape, jnp.float32)
        dev_ref[(members + k) * obs : (members + k + 1) * obs, :] = piece
    for o in range(obs):
        d_ref[:, o * LANES : (o + 1) * LANES] = dev_ref[pl.ds(o, LANES, stride=obs), :].astype(jnp.bfloat16)
    for first, out_ref in ((0, low_ref), (2 * blocks, high_ref)):
        accumulate(members, obs, first, blocks, chunk, batch, d_ref, w_ref, acc_ref)
        packed_system(members, blocks, acc_ref, out_ref)


def own_kernel(members, obs, blocks, chunk, batch, d_ref, w_ref, out_ref, acc_ref):
    accumulate(members, obs, blocks, blocks, chunk, batch, d_ref, w_ref, acc_ref)
    packed_system(members, blocks, acc_ref, out_ref)


def finish_kernel(members, owned, parts, system_ref, state_ref, out_ref):
    half = members // 2
    highest = lax.Precision.HIGHEST
    total = system_ref[0].astype(jnp.float32)
    for m in range(1, parts):
        total = total + system_ref[m].astype(jnp.float32)
    rows = lax.broadcasted_iota(jnp.int32, (members, members), 0)
    cols = lax.broadcasted_iota(jnp.int32, (members, members), 1)
    identity = jnp.where(rows == cols, 1.0, 0.0)
    lane = lax.broadcasted_iota(jnp.int32, (half, LANES), 1)

    def dot(a, b):
        return jnp.dot(a, b, precision=highest, preferred_element_type=jnp.float32)

    y_iter, z_iter, bound, force = [], [], [], []
    for r in range(owned):
        part = total[r * half : (r + 1) * half]
        square = jnp.concatenate([part, jnp.zeros((LANES - half, LANES), jnp.float32)], axis=0)
        below = jnp.transpose(square)[half : 2 * half]
        right = pltpu.roll(part, members, 1)
        bottom = jnp.where(lane < half, below, right)
        system = jnp.concatenate([part, bottom], axis=0)[:, :members]
        system = system + (members - 1) / inflation * identity
        sums = jnp.sum(jnp.abs(system), axis=1, keepdims=True)
        bound.append(jnp.max(sums, axis=0, keepdims=True))
        y_iter.append(system / bound[r])
        f_top = part[:, members : members + 1] + part[:, members + 1 : members + 2]
        f_low = part[:, members + 2 : members + 3] + part[:, members + 3 : members + 4]
        force.append(jnp.concatenate([f_top, f_low], axis=0))
    for sweep in range(NSIT):
        if sweep == 0:
            factor = [1.5 * identity - 0.5 * y for y in y_iter]
            z_next = factor
        else:
            factor = [1.5 * identity - 0.5 * dot(z, y) for z, y in zip(z_iter, y_iter)]
            z_next = [dot(f, z) for f, z in zip(factor, z_iter)]
        if sweep + 1 < NSIT:
            y_iter = [dot(y, f) for y, f in zip(y_iter, factor)]
        z_iter = z_next
    for r in range(owned):
        root = z_iter[r] / jnp.sqrt(bound[r])
        first = dot(root, jnp.broadcast_to(force[r], (members, LANES)))
        shiftu = dot(root, first)[:, :1]
        transform = math.sqrt(members - 1) * root + shiftu
        state = state_ref[r].astype(jnp.float32)
        mean = jnp.sum(state, axis=0, keepdims=True) / members
        dev = (state - mean).astype(jnp.bfloat16)
        moved = jnp.dot(jnp.transpose(transform).astype(jnp.bfloat16), dev, preferred_element_type=jnp.float32)
        out_ref[r] = (mean + moved).astype(jnp.bfloat16)


def per_device(ens_state, obs_prior, obs_value, obs_prec, obs_len, pair_block, obs_pos):
    mem_count = lax.axis_size("mem")
    grid_count = lax.axis_size("grid")
    local = ens_state.shape[0]
    members = mem_count * local
    blocks_dev = ens_state.shape[1]
    obs_blocks = obs_prior.shape[1]
    owned = blocks_dev // mem_count
    obs = obs_blocks // mem_count
    half = members // 2
    nb_total = blocks_dev * grid_count
    mem_pos = lax.axis_index("mem")
    grid_pos = lax.axis_index("grid")
    vmem = pl.BlockSpec(memory_space=pltpu.VMEM)
    anywhere = pl.BlockSpec(memory_space=pl.ANY)

    packed = pl.pallas_call(
        functools.partial(pack_kernel, mem_count, obs),
        out_shape=jax.ShapeDtypeStruct((mem_count, local, obs, LANES), obs_prior.dtype),
        in_specs=[anywhere],
        out_specs=anywhere,
        scratch_shapes=[pltpu.SemaphoreType.DMA((mem_count,))],
        name="pack",
    )(obs_prior)
    prior = lax.all_to_all(packed, "mem", split_axis=0, concat_axis=0, tiled=True)
    prior = prior.reshape(members, obs, LANES)
    state = lax.all_to_all(ens_state, "mem", split_axis=1, concat_axis=0, tiled=True)
    from_low = shift(pair_block, "grid", 1)
    from_high = shift(pair_block, "grid", -1)

    pairs = jnp.concatenate([from_low, pair_block, from_high], axis=0)
    places = (grid_pos + jnp.arange(-1, 2, dtype=jnp.int32)) % grid_count
    ids = places[:, None] * blocks_dev + jnp.arange(blocks_dev, dtype=jnp.int32)[None, :]
    blocks = 3 * blocks_dev
    centers = ids.reshape(blocks, 1).astype(jnp.float32) + 0.5

    def mine(value):
        return lax.dynamic_slice_in_dim(value, mem_pos * obs, obs, 0)

    base = (grid_pos * obs_blocks + mem_pos * obs).reshape(1)
    weights = pl.pallas_call(
        functools.partial(weight_kernel, float(nb_total), obs),
        out_shape=jax.ShapeDtypeStruct((blocks, obs * LANES), jnp.float32),
        in_specs=[pl.BlockSpec(memory_space=pltpu.SMEM), vmem, vmem, vmem, vmem],
        out_specs=vmem,
        name="weights",
    )(base, pairs, centers, mine(obs_prec), mine(obs_pos))

    chunk, batch = 6, 4
    system = jax.ShapeDtypeStruct((blocks_dev * half, LANES), jnp.bfloat16)
    d_all, to_low, to_high = pl.pallas_call(
        functools.partial(neighbour_kernel, members, obs, blocks_dev, chunk, batch),
        out_shape=(jax.ShapeDtypeStruct((LANES, obs * LANES), jnp.bfloat16), system, system),
        in_specs=[vmem, vmem, vmem, vmem],
        out_specs=(vmem, vmem, vmem),
        scratch_shapes=[
            pltpu.VMEM((LANES * obs, LANES), jnp.float32),
            pltpu.VMEM((blocks_dev * members, LANES), jnp.float32),
        ],
        name="neighbours",
    )(prior, mine(obs_len)[:, None], mine(obs_value), weights)
    from_high = shift(to_low, "grid", -1)
    from_low = shift(to_high, "grid", 1)
    own = pl.pallas_call(
        functools.partial(own_kernel, members, obs, blocks_dev, chunk, batch),
        out_shape=jax.ShapeDtypeStruct(system.shape, jnp.float32),
        in_specs=[vmem, vmem],
        out_specs=vmem,
        scratch_shapes=[pltpu.VMEM((blocks_dev * members, LANES), jnp.float32)],
        name="own",
    )(d_all, weights)
    partial = own + from_low.astype(jnp.float32) + from_high.astype(jnp.float32)
    partial = partial.astype(jnp.bfloat16).reshape(mem_count, owned * half, LANES)
    swapped = lax.all_to_all(partial, "mem", split_axis=0, concat_axis=0, tiled=True)
    analysis = pl.pallas_call(
        functools.partial(finish_kernel, members, owned, mem_count),
        out_shape=jax.ShapeDtypeStruct((owned, members, ens_state.shape[2]), jnp.bfloat16),
        in_specs=[vmem, vmem],
        out_specs=vmem,
        name="finish",
    )(swapped, jnp.transpose(state, (1, 0, 2)))
    return lax.all_to_all(
        jnp.transpose(analysis, (1, 0, 2)), "mem", split_axis=0, concat_axis=1, tiled=True
    )


def solution(mesh):
    placed = (
        P("mem", "grid", None),
        P("mem", "grid", None),
        P("grid", None),
        P("grid", None),
        P("grid"),
        P("grid", None),
        P("grid", None),
    )
    return jax.shard_map(
        per_device, mesh=mesh, in_specs=placed, out_specs=P("mem", "grid", None), check_vma=False
    )
```

```python
import functools
import math

import jax
import jax.numpy as jnp
from jax import lax
from jax.experimental import pallas as pl
from jax.experimental.pallas import tpu as pltpu
from jax.sharding import PartitionSpec as P

NSIT = 3
LOCR = 8
LANES = 128

inflation = 1.1


def shift(value, axis, step):
    count = lax.axis_size(axis)
    return lax.ppermute(value, axis, [(i, (i + step) % count) for i in range(count)])


def pack_kernel(parts, size, owned, src_ref, state_ref, out_ref, stage_ref, sems):
    local = state_ref.shape[0]
    pieces = state_ref.shape[2] // LANES
    inward = [
        pltpu.make_async_copy(
            src_ref.at[:, m * size : (m + 1) * size, :], stage_ref.at[m, :, 0:size, :], sems.at[0, m]
        )
        for m in range(parts)
    ]
    outward = [
        pltpu.make_async_copy(stage_ref.at[m], out_ref.at[m], sems.at[1, m]) for m in range(parts)
    ]
    for copy in inward:
        copy.start()
    for i in range(local):
        value = state_ref[i].astype(jnp.float32)
        for m in range(parts):
            rows = value[m * owned : (m + 1) * owned]
            rows = jnp.concatenate(
                [rows[:, q * LANES : (q + 1) * LANES] for q in range(pieces)], axis=0
            )
            stage_ref[m, i, size : size + pieces * owned, :] = rows.astype(stage_ref.dtype)
    for m in range(parts):
        inward[m].wait()
        outward[m].start()
    for copy in outward:
        copy.wait()


def weight_kernel(nb_total, obs, len_ref, low_ref, mid_ref, high_ref, prec_all, pos_all, value_all, out_ref, aux_ref, prec_ref, pos_ref, sems):
    place = lax.axis_index("mem")
    grid_pos = lax.axis_index("grid")
    grid_count = lax.axis_size("grid")
    obs_blocks = prec_all.shape[0]
    blocks_dev = mid_ref.shape[0]
    mine = pl.ds(pl.multiple_of(place * obs, 8), obs)
    copies = [
        pltpu.make_async_copy(prec_all.at[mine], prec_ref, sems.at[0]),
        pltpu.make_async_copy(pos_all.at[mine], pos_ref, sems.at[1]),
        pltpu.make_async_copy(value_all.at[mine], aux_ref.at[obs : 2 * obs], sems.at[2]),
    ]
    for copy in copies:
        copy.start()
    row = lax.broadcasted_iota(jnp.int32, (obs, LANES), 0)
    count = jnp.zeros((obs, LANES), jnp.int32)
    for o in range(obs):
        count = jnp.where(row == o, len_ref[place * obs + o], count)
    lane = lax.broadcasted_iota(jnp.int32, (obs, LANES), 1)
    aux_ref[0:obs, :] = jnp.where(lane < count, 1.0, 0.0)
    base = grid_pos * obs_blocks + place * obs
    pairs = jnp.concatenate([low_ref[...], mid_ref[...], high_ref[...]], axis=0) - base
    index = lax.broadcasted_iota(jnp.int32, (blocks_dev, LANES), 0)
    centers = jnp.concatenate(
        [
            index + lax.rem(grid_pos + grid_count + step, grid_count) * blocks_dev
            for step in (-1, 0, 1)
        ],
        axis=0,
    ).astype(jnp.float32) + 0.5
    for copy in copies:
        copy.wait()
    for o in range(obs):
        hit = jnp.max(jnp.where(pairs == o, 1.0, 0.0), axis=1, keepdims=True)
        gap = jnp.abs(pos_ref[o : o + 1, :] - centers)
        distance = jnp.minimum(gap, nb_total - gap)
        relative = distance * (1.0 / LOCR)
        weight = prec_ref[o : o + 1, :] * jnp.exp(-0.5 * relative * relative)
        out_ref[:, o * LANES : (o + 1) * LANES] = jnp.where(hit > 0.0, weight, 0.0)


def accumulate(members, obs, first, blocks, chunk, batch, d_ref, w_ref, acc_ref):
    acc_ref[...] = jnp.zeros(acc_ref.shape, jnp.float32)
    width = chunk * LANES

    def step(c, carry):
        start = pl.multiple_of(c * width, width)
        full = d_ref[:, pl.ds(start, width)]
        d = full[:members].reshape(members // 16, 16, width)
        for b0 in range(0, blocks, batch):
            parts = []
            for b in range(b0, b0 + batch):
                row = w_ref[first + b : first + b + 1, pl.ds(start, width)]
                w = jnp.broadcast_to(row, (16, width)).astype(jnp.bfloat16)
                parts.append((d * w[None]).reshape(members, width))
            scaled = jnp.concatenate(parts, axis=0)
            acc_ref[b0 * members : (b0 + batch) * members, :] += lax.dot_general(
                scaled, full, (((1,), (1,)), ((), ())), preferred_element_type=jnp.float32
            )
        return carry

    lax.fori_loop(0, obs // chunk, step, 0)


def packed_system(members, blocks, acc_ref, out_ref):
    half = members // 2
    lane = lax.broadcasted_iota(jnp.int32, (half, LANES), 1)
    low = (lane == members + 2) | (lane == members + 3) | (lane >= LANES - half)
    for b in range(blocks):
        top = acc_ref[b * members : b * members + half, :]
        bottom = acc_ref[b * members + half : (b + 1) * members, :]
        out_ref[b * half : (b + 1) * half, :] = jnp.where(low, bottom, top).astype(out_ref.dtype)


def neighbour_kernel(members, obs, blocks, chunk, batch, prior_ref, aux_ref, w_ref, d_ref, low_ref, high_ref, dev_ref, acc_ref):
    half = members // 2
    total = prior_ref[0].astype(jnp.float32)
    for i in range(1, members):
        total = total + prior_ref[i].astype(jnp.float32)
    mean = total / members
    valid = aux_ref[0:obs, :] > 0.0
    for i in range(members):
        one = jnp.where(valid, prior_ref[i].astype(jnp.float32) - mean, 0.0)
        dev_ref[i * obs : (i + 1) * obs, :] = one
        if i >= half:
            at = LANES - members + i
            dev_ref[at * obs : (at + 1) * obs, :] = one
    departure = jnp.where(valid, aux_ref[obs : 2 * obs, :] - mean, 0.0)
    high = departure.astype(jnp.bfloat16).astype(jnp.float32)
    for k in range(LANES - half - members):
        piece = (high, departure - high)[k % 2] if k < 4 else jnp.zeros(mean.shape, jnp.float32)
        dev_ref[(members + k) * obs : (members + k + 1) * obs, :] = piece
    for o in range(obs):
        d_ref[:, o * LANES : (o + 1) * LANES] = dev_ref[pl.ds(o, LANES, stride=obs), :].astype(jnp.bfloat16)
    for first, out_ref in ((0, low_ref), (2 * blocks, high_ref)):
        accumulate(members, obs, first, blocks, chunk, batch, d_ref, w_ref, acc_ref)
        packed_system(members, blocks, acc_ref, out_ref)


def own_kernel(members, obs, blocks, chunk, batch, d_ref, w_ref, out_ref, acc_ref):
    accumulate(members, obs, blocks, blocks, chunk, batch, d_ref, w_ref, acc_ref)
    packed_system(members, blocks, acc_ref, out_ref)


def state_kernel(members, part_ref, dev_ref, mean_ref, wide_ref):
    rows = part_ref.shape[1]
    total = part_ref[0].astype(jnp.float32)
    for i in range(1, members):
        total = total + part_ref[i].astype(jnp.float32)
    mean = total / members
    mean_ref[...] = mean
    for i in range(members):
        wide_ref[i * rows : (i + 1) * rows, :] = part_ref[i].astype(jnp.float32) - mean
    for k in range(rows):
        dev_ref[:, k * LANES : (k + 1) * LANES] = wide_ref[pl.ds(k, members, stride=rows), :].astype(jnp.bfloat16)


def finish_kernel(members, owned, parts, system_ref, dev_ref, mean_ref, out_ref, wide_ref):
    half = members // 2
    rows_out = mean_ref.shape[0]
    highest = lax.Precision.HIGHEST
    total = system_ref[0].astype(jnp.float32)
    for m in range(1, parts):
        total = total + system_ref[m].astype(jnp.float32)
    rows = lax.broadcasted_iota(jnp.int32, (members, members), 0)
    cols = lax.broadcasted_iota(jnp.int32, (members, members), 1)
    identity = jnp.where(rows == cols, 1.0, 0.0)
    lane = lax.broadcasted_iota(jnp.int32, (half, LANES), 1)

    def dot(a, b):
        return jnp.dot(a, b, precision=highest, preferred_element_type=jnp.float32)

    y_iter, z_iter, bound, force = [], [], [], []
    for r in range(owned):
        part = total[r * half : (r + 1) * half]
        square = jnp.concatenate([part, jnp.zeros((LANES - half, LANES), jnp.float32)], axis=0)
        below = jnp.transpose(square)[half : 2 * half]
        right = pltpu.roll(part, members, 1)
        bottom = jnp.where(lane < half, below, right)
        system = jnp.concatenate([part, bottom], axis=0)[:, :members]
        system = system + (members - 1) / inflation * identity
        sums = jnp.sum(jnp.abs(system), axis=1, keepdims=True)
        bound.append(jnp.max(sums, axis=0, keepdims=True))
        y_iter.append(system / bound[r])
        f_top = part[:, members : members + 1] + part[:, members + 1 : members + 2]
        f_low = part[:, members + 2 : members + 3] + part[:, members + 3 : members + 4]
        force.append(jnp.concatenate([f_top, f_low], axis=0))
    for sweep in range(NSIT):
        if sweep == 0:
            factor = [1.5 * identity - 0.5 * y for y in y_iter]
            z_next = factor
        else:
            factor = [1.5 * identity - 0.5 * dot(z, y) for z, y in zip(z_iter, y_iter)]
            z_next = [dot(f, z) for f, z in zip(factor, z_iter)]
        if sweep + 1 < NSIT:
            y_iter = [dot(y, f) for y, f in zip(y_iter, factor)]
        z_iter = z_next
    for r in range(owned):
        root = z_iter[r] / jnp.sqrt(bound[r])
        first = dot(root, jnp.broadcast_to(force[r], (members, LANES)))
        shiftu = dot(root, first)[:, :1]
        transform = math.sqrt(members - 1) * root + shiftu
        turned = jnp.transpose(transform).astype(jnp.bfloat16)
        for k in range(r, rows_out, owned):
            moved = jnp.dot(
                turned, dev_ref[:, k * LANES : (k + 1) * LANES], preferred_element_type=jnp.float32
            )
            wide_ref[pl.ds(k, members, stride=rows_out), :] = mean_ref[k : k + 1, :] + moved
    out_ref[...] = wide_ref[...].astype(jnp.bfloat16)


def unpack_kernel(owned, part_ref, out_ref):
    parts, local, rows, _ = part_ref.shape
    for i in range(local):
        groups = []
        for m in range(parts):
            value = part_ref[m, i].astype(jnp.float32)
            groups.append(
                jnp.concatenate([value[k : k + owned] for k in range(0, rows, owned)], axis=1)
            )
        out_ref[i] = jnp.concatenate(groups, axis=0).astype(out_ref.dtype)


def per_device(ens_state, obs_prior, obs_value, obs_prec, obs_len, pair_block, obs_pos):
    mem_count = lax.axis_size("mem")
    grid_count = lax.axis_size("grid")
    local = ens_state.shape[0]
    members = mem_count * local
    blocks_dev = ens_state.shape[1]
    obs_blocks = obs_prior.shape[1]
    owned = blocks_dev // mem_count
    obs = obs_blocks // mem_count
    half = members // 2
    nb_total = blocks_dev * grid_count
    vmem = pl.BlockSpec(memory_space=pltpu.VMEM)
    anywhere = pl.BlockSpec(memory_space=pl.ANY)

    pieces = ens_state.shape[2] // LANES
    extra = pieces * owned
    packed = pl.pallas_call(
        functools.partial(pack_kernel, mem_count, obs, owned),
        out_shape=jax.ShapeDtypeStruct((mem_count, local, obs + extra, LANES), obs_prior.dtype),
        in_specs=[anywhere, vmem],
        out_specs=anywhere,
        scratch_shapes=[
            pltpu.VMEM((mem_count, local, obs + extra, LANES), obs_prior.dtype),
            pltpu.SemaphoreType.DMA((2, mem_count)),
        ],
        name="pack",
    )(obs_prior, ens_state)
    prior = lax.all_to_all(packed, "mem", split_axis=0, concat_axis=0, tiled=True)
    prior = prior.reshape(members, obs + extra, LANES)
    from_low = shift(pair_block, "grid", 1)
    from_high = shift(pair_block, "grid", -1)

    blocks = 3 * blocks_dev
    weights, aux = pl.pallas_call(
        functools.partial(weight_kernel, float(nb_total), obs),
        out_shape=(
            jax.ShapeDtypeStruct((blocks, obs * LANES), jnp.float32),
            jax.ShapeDtypeStruct((2 * obs, LANES), jnp.float32),
        ),
        in_specs=[pl.BlockSpec(memory_space=pltpu.SMEM), vmem, vmem, vmem, anywhere, anywhere, anywhere],
        out_specs=(vmem, vmem),
        scratch_shapes=[
            pltpu.VMEM((obs, LANES), jnp.float32),
            pltpu.VMEM((obs, LANES), jnp.float32),
            pltpu.SemaphoreType.DMA((3,)),
        ],
        name="weights",
    )(obs_len, from_low, pair_block, from_high, obs_prec, obs_pos, obs_value)

    chunk, batch = 6, 4
    system = jax.ShapeDtypeStruct((blocks_dev * half, LANES), jnp.bfloat16)
    d_all, to_low, to_high = pl.pallas_call(
        functools.partial(neighbour_kernel, members, obs, blocks_dev, chunk, batch),
        out_shape=(jax.ShapeDtypeStruct((LANES, obs * LANES), jnp.bfloat16), system, system),
        grid=(1,),
        in_specs=[pl.BlockSpec((members, obs, LANES), lambda i: (0, 0, 0)), vmem, vmem],
        out_specs=(vmem, vmem, vmem),
        scratch_shapes=[
            pltpu.VMEM((LANES * obs, LANES), jnp.float32),
            pltpu.VMEM((blocks_dev * members, LANES), jnp.float32),
        ],
        name="neighbours",
    )(prior, aux, weights)
    from_high = shift(to_low, "grid", -1)
    from_low = shift(to_high, "grid", 1)
    own = pl.pallas_call(
        functools.partial(own_kernel, members, obs, blocks_dev, chunk, batch),
        out_shape=jax.ShapeDtypeStruct(system.shape, jnp.float32),
        in_specs=[vmem, vmem],
        out_specs=vmem,
        scratch_shapes=[pltpu.VMEM((blocks_dev * members, LANES), jnp.float32)],
        name="own",
    )(d_all, weights)
    partial = own + from_low.astype(jnp.float32) + from_high.astype(jnp.float32)
    partial = partial.astype(jnp.bfloat16).reshape(mem_count, owned * half, LANES)
    swapped = lax.all_to_all(partial, "mem", split_axis=0, concat_axis=0, tiled=True)
    deviation, mean = pl.pallas_call(
        functools.partial(state_kernel, members),
        out_shape=(
            jax.ShapeDtypeStruct((members, extra * LANES), jnp.bfloat16),
            jax.ShapeDtypeStruct((extra, LANES), jnp.float32),
        ),
        grid=(1,),
        in_specs=[pl.BlockSpec((members, extra, LANES), lambda i: (0, obs // extra, 0))],
        out_specs=(vmem, vmem),
        scratch_shapes=[pltpu.VMEM((members * extra, LANES), jnp.float32)],
        name="state",
    )(prior)
    analysis = pl.pallas_call(
        functools.partial(finish_kernel, members, owned, mem_count),
        out_shape=jax.ShapeDtypeStruct((members * extra, LANES), jnp.bfloat16),
        in_specs=[vmem, vmem, vmem],
        out_specs=vmem,
        scratch_shapes=[pltpu.VMEM((members * extra, LANES), jnp.float32)],
        name="finish",
    )(swapped, deviation, mean)
    analysis = analysis.reshape(mem_count, local, extra, LANES)
    analysis = lax.all_to_all(analysis, "mem", split_axis=0, concat_axis=0, tiled=True)
    return pl.pallas_call(
        functools.partial(unpack_kernel, owned),
        out_shape=jax.ShapeDtypeStruct(ens_state.shape, jnp.bfloat16),
        in_specs=[vmem],
        out_specs=vmem,
        name="unpack",
    )(analysis)


def solution(mesh):
    placed = (
        P("mem", "grid", None),
        P("mem", "grid", None),
        P("grid", None),
        P("grid", None),
        P("grid"),
        P("grid", None),
        P("grid", None),
    )
    return jax.shard_map(
        per_device, mesh=mesh, in_specs=placed, out_specs=P("mem", "grid", None), check_vma=False
    )
```

```python
import functools
import math

import jax
import jax.numpy as jnp
from jax import lax
from jax.experimental import pallas as pl
from jax.experimental.pallas import tpu as pltpu
from jax.sharding import PartitionSpec as P

NSIT = 3
LOCR = 8
LANES = 128

inflation = 1.1


def shift(value, axis, step):
    count = lax.axis_size(axis)
    return lax.ppermute(value, axis, [(i, (i + step) % count) for i in range(count)])


def pack_kernel(parts, size, owned, src_ref, state_ref, out_ref, rows_ref, sems):
    local = state_ref.shape[0]
    pieces = state_ref.shape[2] // LANES
    copies = [
        pltpu.make_async_copy(
            src_ref.at[:, m * size : (m + 1) * size, :], out_ref.at[m, :, 0:size, :], sems.at[m]
        )
        for m in range(parts)
    ]
    for copy in copies:
        copy.start()
    for i in range(local):
        value = state_ref[i].astype(jnp.float32)
        for m in range(parts):
            rows = value[m * owned : (m + 1) * owned]
            rows = jnp.concatenate(
                [rows[:, q * LANES : (q + 1) * LANES] for q in range(pieces)], axis=0
            )
            rows_ref[m, i] = rows.astype(rows_ref.dtype)
    last = pltpu.make_async_copy(rows_ref, out_ref.at[:, :, size:, :], sems.at[parts])
    last.start()
    for copy in copies:
        copy.wait()
    last.wait()


def weight_kernel(nb_total, obs, len_ref, low_ref, mid_ref, high_ref, prec_all, pos_all, value_all, out_ref, aux_ref, prec_ref, pos_ref, sems):
    place = lax.axis_index("mem")
    grid_pos = lax.axis_index("grid")
    grid_count = lax.axis_size("grid")
    obs_blocks = prec_all.shape[0]
    blocks_dev = mid_ref.shape[0]
    mine = pl.ds(pl.multiple_of(place * obs, 8), obs)
    copies = [
        pltpu.make_async_copy(prec_all.at[mine], prec_ref, sems.at[0]),
        pltpu.make_async_copy(pos_all.at[mine], pos_ref, sems.at[1]),
        pltpu.make_async_copy(value_all.at[mine], aux_ref.at[obs : 2 * obs], sems.at[2]),
    ]
    for copy in copies:
        copy.start()
    row = lax.broadcasted_iota(jnp.int32, (obs, LANES), 0)
    count = jnp.zeros((obs, LANES), jnp.int32)
    for o in range(obs):
        count = jnp.where(row == o, len_ref[place * obs + o], count)
    lane = lax.broadcasted_iota(jnp.int32, (obs, LANES), 1)
    aux_ref[0:obs, :] = jnp.where(lane < count, 1.0, 0.0)
    base = grid_pos * obs_blocks + place * obs
    pairs = jnp.concatenate([low_ref[...], mid_ref[...], high_ref[...]], axis=0) - base
    index = lax.broadcasted_iota(jnp.int32, (blocks_dev, LANES), 0)
    centers = jnp.concatenate(
        [
            index + lax.rem(grid_pos + grid_count + step, grid_count) * blocks_dev
            for step in (-1, 0, 1)
        ],
        axis=0,
    ).astype(jnp.float32) + 0.5
    for copy in copies:
        copy.wait()
    for o in range(obs):
        hit = jnp.max(jnp.where(pairs == o, 1.0, 0.0), axis=1, keepdims=True)
        gap = jnp.abs(pos_ref[o : o + 1, :] - centers)
        distance = jnp.minimum(gap, nb_total - gap)
        relative = distance * (1.0 / LOCR)
        weight = prec_ref[o : o + 1, :] * jnp.exp(-0.5 * relative * relative)
        out_ref[:, o * LANES : (o + 1) * LANES] = jnp.where(hit > 0.0, weight, 0.0)


def accumulate(members, obs, first, blocks, chunk, batch, d_ref, w_ref, acc_ref):
    acc_ref[...] = jnp.zeros(acc_ref.shape, jnp.float32)
    width = chunk * LANES

    def step(c, carry):
        start = pl.multiple_of(c * width, width)
        full = d_ref[:, pl.ds(start, width)]
        d = full[:members].reshape(members // 16, 16, width)
        for b0 in range(0, blocks, batch):
            parts = []
            for b in range(b0, b0 + batch):
                row = w_ref[first + b : first + b + 1, pl.ds(start, width)]
                w = jnp.broadcast_to(row, (16, width)).astype(jnp.bfloat16)
                parts.append((d * w[None]).reshape(members, width))
            scaled = jnp.concatenate(parts, axis=0)
            acc_ref[b0 * members : (b0 + batch) * members, :] += lax.dot_general(
                scaled, full, (((1,), (1,)), ((), ())), preferred_element_type=jnp.float32
            )
        return carry

    lax.fori_loop(0, obs // chunk, step, 0)


def packed_system(members, blocks, acc_ref, out_ref):
    half = members // 2
    lane = lax.broadcasted_iota(jnp.int32, (half, LANES), 1)
    low = (lane == members + 2) | (lane == members + 3) | (lane >= LANES - half)
    for b in range(blocks):
        top = acc_ref[b * members : b * members + half, :]
        bottom = acc_ref[b * members + half : (b + 1) * members, :]
        out_ref[b * half : (b + 1) * half, :] = jnp.where(low, bottom, top).astype(out_ref.dtype)


def neighbour_kernel(members, obs, blocks, chunk, batch, prior_ref, aux_ref, w_ref, d_ref, low_ref, high_ref, dev_ref, acc_ref):
    half = members // 2
    total = prior_ref[0, 0:obs].astype(jnp.float32)
    for i in range(1, members):
        total = total + prior_ref[i, 0:obs].astype(jnp.float32)
    mean = total / members
    valid = aux_ref[0:obs, :] > 0.0
    for i in range(members):
        one = jnp.where(valid, prior_ref[i, 0:obs].astype(jnp.float32) - mean, 0.0)
        dev_ref[i * obs : (i + 1) * obs, :] = one
        if i >= half:
            at = LANES - members + i
            dev_ref[at * obs : (at + 1) * obs, :] = one
    departure = jnp.where(valid, aux_ref[obs : 2 * obs, :] - mean, 0.0)
    high = departure.astype(jnp.bfloat16).astype(jnp.float32)
    for k in range(LANES - half - members):
        piece = (high, departure - high)[k % 2] if k < 4 else jnp.zeros(mean.shape, jnp.float32)
        dev_ref[(members + k) * obs : (members + k + 1) * obs, :] = piece
    for o in range(obs):
        d_ref[:, o * LANES : (o + 1) * LANES] = dev_ref[pl.ds(o, LANES, stride=obs), :].astype(jnp.bfloat16)
    for first, out_ref in ((0, low_ref), (2 * blocks, high_ref)):
        accumulate(members, obs, first, blocks, chunk, batch, d_ref, w_ref, acc_ref)
        packed_system(members, blocks, acc_ref, out_ref)


def own_kernel(members, obs, blocks, chunk, batch, d_ref, w_ref, out_ref, acc_ref):
    accumulate(members, obs, blocks, blocks, chunk, batch, d_ref, w_ref, acc_ref)
    packed_system(members, blocks, acc_ref, out_ref)


def state_kernel(members, part_ref, dev_ref, mean_ref, wide_ref):
    rows = mean_ref.shape[0]
    first = part_ref.shape[1] - rows
    total = part_ref[0, first:].astype(jnp.float32)
    for i in range(1, members):
        total = total + part_ref[i, first:].astype(jnp.float32)
    mean = total / members
    mean_ref[...] = mean
    for i in range(members):
        wide_ref[i * rows : (i + 1) * rows, :] = part_ref[i, first:].astype(jnp.float32) - mean
    for k in range(rows):
        dev_ref[:, k * LANES : (k + 1) * LANES] = wide_ref[pl.ds(k, members, stride=rows), :].astype(jnp.bfloat16)


def merge_kernel(own_ref, low_ref, high_ref, out_ref):
    total = own_ref[...] + low_ref[...].astype(jnp.float32) + high_ref[...].astype(jnp.float32)
    out_ref[...] = total.astype(jnp.bfloat16)


def finish_kernel(members, owned, parts, system_ref, dev_ref, mean_ref, out_ref, wide_ref):
    half = members // 2
    rows_out = mean_ref.shape[0]
    highest = lax.Precision.HIGHEST
    total = system_ref[0].astype(jnp.float32)
    for m in range(1, parts):
        total = total + system_ref[m].astype(jnp.float32)
    rows = lax.broadcasted_iota(jnp.int32, (members, members), 0)
    cols = lax.broadcasted_iota(jnp.int32, (members, members), 1)
    identity = jnp.where(rows == cols, 1.0, 0.0)
    lane = lax.broadcasted_iota(jnp.int32, (half, LANES), 1)

    def dot(a, b):
        return jnp.dot(a, b, precision=highest, preferred_element_type=jnp.float32)

    y_iter, z_iter, bound, force = [], [], [], []
    for r in range(owned):
        part = total[r * half : (r + 1) * half]
        square = jnp.concatenate([part, jnp.zeros((LANES - half, LANES), jnp.float32)], axis=0)
        below = jnp.transpose(square)[half : 2 * half]
        right = pltpu.roll(part, members, 1)
        bottom = jnp.where(lane < half, below, right)
        system = jnp.concatenate([part, bottom], axis=0)[:, :members]
        system = system + (members - 1) / inflation * identity
        sums = jnp.sum(jnp.abs(system), axis=1, keepdims=True)
        bound.append(jnp.max(sums, axis=0, keepdims=True))
        y_iter.append(system / bound[r])
        f_top = part[:, members : members + 1] + part[:, members + 1 : members + 2]
        f_low = part[:, members + 2 : members + 3] + part[:, members + 3 : members + 4]
        force.append(jnp.concatenate([f_top, f_low], axis=0))
    for sweep in range(NSIT):
        if sweep == 0:
            factor = [1.5 * identity - 0.5 * y for y in y_iter]
            z_next = factor
        else:
            factor = [1.5 * identity - 0.5 * dot(z, y) for z, y in zip(z_iter, y_iter)]
            z_next = [dot(f, z) for f, z in zip(factor, z_iter)]
        if sweep + 1 < NSIT:
            y_iter = [dot(y, f) for y, f in zip(y_iter, factor)]
        z_iter = z_next
    for r in range(owned):
        root = z_iter[r] / jnp.sqrt(bound[r])
        first = dot(root, jnp.broadcast_to(force[r], (members, LANES)))
        shiftu = dot(root, first)[:, :1]
        transform = math.sqrt(members - 1) * root + shiftu
        turned = jnp.transpose(transform).astype(jnp.bfloat16)
        for k in range(r, rows_out, owned):
            moved = jnp.dot(
                turned, dev_ref[:, k * LANES : (k + 1) * LANES], preferred_element_type=jnp.float32
            )
            wide_ref[pl.ds(k, members, stride=rows_out), :] = mean_ref[k : k + 1, :] + moved
    out_ref[...] = wide_ref[...].astype(jnp.bfloat16)


def unpack_kernel(owned, part_ref, out_ref):
    parts, local, rows, _ = part_ref.shape
    for i in range(local):
        groups = []
        for m in range(parts):
            value = part_ref[m, i].astype(jnp.float32)
            groups.append(
                jnp.concatenate([value[k : k + owned] for k in range(0, rows, owned)], axis=1)
            )
        out_ref[i] = jnp.concatenate(groups, axis=0).astype(out_ref.dtype)


def per_device(ens_state, obs_prior, obs_value, obs_prec, obs_len, pair_block, obs_pos):
    mem_count = lax.axis_size("mem")
    grid_count = lax.axis_size("grid")
    local = ens_state.shape[0]
    members = mem_count * local
    blocks_dev = ens_state.shape[1]
    obs_blocks = obs_prior.shape[1]
    owned = blocks_dev // mem_count
    obs = obs_blocks // mem_count
    half = members // 2
    nb_total = blocks_dev * grid_count
    vmem = pl.BlockSpec(memory_space=pltpu.VMEM)
    anywhere = pl.BlockSpec(memory_space=pl.ANY)

    pieces = ens_state.shape[2] // LANES

    def near(value):
        return pltpu.with_memory_space_constraint(value, pltpu.VMEM)

    extra = pieces * owned
    packed = pl.pallas_call(
        functools.partial(pack_kernel, mem_count, obs, owned),
        out_shape=jax.ShapeDtypeStruct((mem_count, local, obs + extra, LANES), obs_prior.dtype),
        in_specs=[vmem, vmem],
        out_specs=anywhere,
        scratch_shapes=[
            pltpu.VMEM((mem_count, local, extra, LANES), ens_state.dtype),
            pltpu.SemaphoreType.DMA((mem_count + 1,)),
        ],
        compiler_params=pltpu.CompilerParams(vmem_limit_bytes=16 * 2**20),
        name="pack",
    )(near(obs_prior), near(ens_state))
    prior = lax.all_to_all(packed, "mem", split_axis=0, concat_axis=0, tiled=True)
    prior = prior.reshape(members, obs + extra, LANES)
    from_low = shift(pair_block, "grid", 1)
    from_high = shift(pair_block, "grid", -1)

    blocks = 3 * blocks_dev
    weights, aux = pl.pallas_call(
        functools.partial(weight_kernel, float(nb_total), obs),
        out_shape=(
            pltpu.VMEM((blocks, obs * LANES), jnp.float32),
            pltpu.VMEM((2 * obs, LANES), jnp.float32),
        ),
        in_specs=[pl.BlockSpec(memory_space=pltpu.SMEM), vmem, vmem, vmem, anywhere, anywhere, anywhere],
        out_specs=(vmem, vmem),
        scratch_shapes=[
            pltpu.VMEM((obs, LANES), jnp.float32),
            pltpu.VMEM((obs, LANES), jnp.float32),
            pltpu.SemaphoreType.DMA((3,)),
        ],
        compiler_params=pltpu.CompilerParams(vmem_limit_bytes=16 * 2**20),
        name="weights",
    )(obs_len, near(from_low), pair_block, near(from_high), obs_prec, obs_pos, obs_value)

    chunk, batch = 6, 4
    system = pltpu.VMEM((blocks_dev * half, LANES), jnp.bfloat16)
    d_all, to_low, to_high = pl.pallas_call(
        functools.partial(neighbour_kernel, members, obs, blocks_dev, chunk, batch),
        out_shape=(pltpu.VMEM((LANES, obs * LANES), jnp.bfloat16), system, system),
        in_specs=[vmem, vmem, vmem],
        out_specs=(vmem, vmem, vmem),
        scratch_shapes=[
            pltpu.VMEM((LANES * obs, LANES), jnp.float32),
            pltpu.VMEM((blocks_dev * members, LANES), jnp.float32),
        ],
        compiler_params=pltpu.CompilerParams(vmem_limit_bytes=16 * 2**20),
        name="neighbours",
    )(near(prior), near(aux), near(weights))
    from_high = shift(to_low, "grid", -1)
    from_low = shift(to_high, "grid", 1)
    own = pl.pallas_call(
        functools.partial(own_kernel, members, obs, blocks_dev, chunk, batch),
        out_shape=pltpu.VMEM((blocks_dev * half, LANES), jnp.float32),
        in_specs=[vmem, vmem],
        out_specs=vmem,
        scratch_shapes=[pltpu.VMEM((blocks_dev * members, LANES), jnp.float32)],
        compiler_params=pltpu.CompilerParams(vmem_limit_bytes=16 * 2**20),
        name="own",
    )(near(d_all), near(weights))
    partial = pl.pallas_call(
        merge_kernel,
        out_shape=pltpu.VMEM((blocks_dev * half, LANES), jnp.bfloat16),
        in_specs=[vmem, vmem, vmem],
        out_specs=vmem,
        compiler_params=pltpu.CompilerParams(vmem_limit_bytes=16 * 2**20),
        name="merge",
    )(near(own), near(from_low), near(from_high))
    partial = partial.reshape(mem_count, owned * half, LANES)
    swapped = lax.all_to_all(partial, "mem", split_axis=0, concat_axis=0, tiled=True)
    deviation, mean = pl.pallas_call(
        functools.partial(state_kernel, members),
        out_shape=(
            pltpu.VMEM((members, extra * LANES), jnp.bfloat16),
            pltpu.VMEM((extra, LANES), jnp.float32),
        ),
        in_specs=[vmem],
        out_specs=(vmem, vmem),
        scratch_shapes=[pltpu.VMEM((members * extra, LANES), jnp.float32)],
        compiler_params=pltpu.CompilerParams(vmem_limit_bytes=16 * 2**20),
        name="state",
    )(near(prior))
    analysis = pl.pallas_call(
        functools.partial(finish_kernel, members, owned, mem_count),
        out_shape=jax.ShapeDtypeStruct((members * extra, LANES), jnp.bfloat16),
        in_specs=[vmem, vmem, vmem],
        out_specs=vmem,
        scratch_shapes=[pltpu.VMEM((members * extra, LANES), jnp.float32)],
        compiler_params=pltpu.CompilerParams(vmem_limit_bytes=16 * 2**20),
        name="finish",
    )(near(swapped), near(deviation), near(mean))
    analysis = analysis.reshape(mem_count, local, extra, LANES)
    analysis = lax.all_to_all(analysis, "mem", split_axis=0, concat_axis=0, tiled=True)
    return pl.pallas_call(
        functools.partial(unpack_kernel, owned),
        out_shape=jax.ShapeDtypeStruct(ens_state.shape, jnp.bfloat16),
        in_specs=[vmem],
        out_specs=vmem,
        compiler_params=pltpu.CompilerParams(vmem_limit_bytes=16 * 2**20),
        name="unpack",
    )(near(analysis))


def solution(mesh):
    placed = (
        P("mem", "grid", None),
        P("mem", "grid", None),
        P("grid", None),
        P("grid", None),
        P("grid"),
        P("grid", None),
        P("grid", None),
    )
    return jax.shard_map(
        per_device, mesh=mesh, in_specs=placed, out_specs=P("mem", "grid", None), check_vma=False
    )
```

```python
import functools
import math

import jax
import jax.numpy as jnp
from jax import lax
from jax.experimental import pallas as pl
from jax.experimental.pallas import tpu as pltpu
from jax.sharding import PartitionSpec as P

NSIT = 3
LOCR = 8
LANES = 128

inflation = 1.1


def shift(value, axis, step):
    count = lax.axis_size(axis)
    return lax.ppermute(value, axis, [(i, (i + step) % count) for i in range(count)])


def pack_kernel(parts, size, owned, src_ref, state_all, out_ref, stage_ref, state_ref, rows_ref, sems, last):
    local = state_all.shape[0]
    pieces = state_all.shape[2] // LANES
    inward = [
        pltpu.make_async_copy(src_ref.at[:, m * size : (m + 1) * size, :], stage_ref.at[m], sems.at[0, m])
        for m in range(parts)
    ]
    outward = [
        pltpu.make_async_copy(stage_ref.at[m], out_ref.at[m, :, 0:size, :], sems.at[1, m])
        for m in range(parts)
    ]
    state_in = pltpu.make_async_copy(state_all, state_ref, last.at[0])
    state_out = pltpu.make_async_copy(rows_ref, out_ref.at[:, :, size:, :], last.at[1])
    state_in.start()
    for copy in inward:
        copy.start()
    state_in.wait()
    for i in range(local):
        value = state_ref[i].astype(jnp.float32)
        for m in range(parts):
            rows = value[m * owned : (m + 1) * owned]
            rows = jnp.concatenate(
                [rows[:, q * LANES : (q + 1) * LANES] for q in range(pieces)], axis=0
            )
            rows_ref[m, i] = rows.astype(rows_ref.dtype)
    for m in range(parts):
        inward[m].wait()
        outward[m].start()
    state_out.start()
    for copy in outward:
        copy.wait()
    state_out.wait()


def weight_kernel(nb_total, obs, len_ref, low_ref, mid_ref, high_ref, prec_all, pos_all, value_all, out_ref, aux_ref, prec_ref, pos_ref, sems):
    place = lax.axis_index("mem")
    grid_pos = lax.axis_index("grid")
    grid_count = lax.axis_size("grid")
    obs_blocks = prec_all.shape[0]
    blocks_dev = mid_ref.shape[0]
    mine = pl.ds(pl.multiple_of(place * obs, 8), obs)
    copies = [
        pltpu.make_async_copy(prec_all.at[mine], prec_ref, sems.at[0]),
        pltpu.make_async_copy(pos_all.at[mine], pos_ref, sems.at[1]),
        pltpu.make_async_copy(value_all.at[mine], aux_ref.at[obs : 2 * obs], sems.at[2]),
    ]
    for copy in copies:
        copy.start()
    row = lax.broadcasted_iota(jnp.int32, (obs, LANES), 0)
    count = jnp.zeros((obs, LANES), jnp.int32)
    for o in range(obs):
        count = jnp.where(row == o, len_ref[place * obs + o], count)
    lane = lax.broadcasted_iota(jnp.int32, (obs, LANES), 1)
    aux_ref[0:obs, :] = jnp.where(lane < count, 1.0, 0.0)
    base = grid_pos * obs_blocks + place * obs
    pairs = jnp.concatenate([low_ref[...], mid_ref[...], high_ref[...]], axis=0) - base
    index = lax.broadcasted_iota(jnp.int32, (blocks_dev, LANES), 0)
    centers = jnp.concatenate(
        [
            index + lax.rem(grid_pos + grid_count + step, grid_count) * blocks_dev
            for step in (-1, 0, 1)
        ],
        axis=0,
    ).astype(jnp.float32) + 0.5
    for copy in copies:
        copy.wait()
    for o in range(obs):
        hit = jnp.max(jnp.where(pairs == o, 1.0, 0.0), axis=1, keepdims=True)
        gap = jnp.abs(pos_ref[o : o + 1, :] - centers)
        distance = jnp.minimum(gap, nb_total - gap)
        relative = distance * (1.0 / LOCR)
        weight = prec_ref[o : o + 1, :] * jnp.exp(-0.5 * relative * relative)
        out_ref[:, o * LANES : (o + 1) * LANES] = jnp.where(hit > 0.0, weight, 0.0)


def accumulate(members, obs, first, blocks, chunk, batch, d_ref, w_ref, acc_ref):
    acc_ref[...] = jnp.zeros(acc_ref.shape, jnp.float32)
    width = chunk * LANES

    def step(c, carry):
        start = pl.multiple_of(c * width, width)
        full = d_ref[:, pl.ds(start, width)]
        d = full[:members].reshape(members // 16, 16, width)
        for b0 in range(0, blocks, batch):
            parts = []
            for b in range(b0, b0 + batch):
                row = w_ref[first + b : first + b + 1, pl.ds(start, width)]
                w = jnp.broadcast_to(row, (16, width)).astype(jnp.bfloat16)
                parts.append((d * w[None]).reshape(members, width))
            scaled = jnp.concatenate(parts, axis=0)
            acc_ref[b0 * members : (b0 + batch) * members, :] += lax.dot_general(
                scaled, full, (((1,), (1,)), ((), ())), preferred_element_type=jnp.float32
            )
        return carry

    lax.fori_loop(0, obs // chunk, step, 0)


def packed_system(members, blocks, acc_ref, out_ref):
    half = members // 2
    lane = lax.broadcasted_iota(jnp.int32, (half, LANES), 1)
    low = (lane == members + 2) | (lane == members + 3) | (lane >= LANES - half)
    for b in range(blocks):
        top = acc_ref[b * members : b * members + half, :]
        bottom = acc_ref[b * members + half : (b + 1) * members, :]
        out_ref[b * half : (b + 1) * half, :] = jnp.where(low, bottom, top).astype(out_ref.dtype)


def neighbour_kernel(members, obs, blocks, chunk, batch, prior_ref, aux_ref, w_ref, d_ref, low_ref, high_ref, dev_ref, acc_ref):
    half = members // 2
    total = prior_ref[0, 0:obs].astype(jnp.float32)
    for i in range(1, members):
        total = total + prior_ref[i, 0:obs].astype(jnp.float32)
    mean = total / members
    valid = aux_ref[0:obs, :] > 0.0
    for i in range(members):
        one = jnp.where(valid, prior_ref[i, 0:obs].astype(jnp.float32) - mean, 0.0)
        dev_ref[i * obs : (i + 1) * obs, :] = one
        if i >= half:
            at = LANES - members + i
            dev_ref[at * obs : (at + 1) * obs, :] = one
    departure = jnp.where(valid, aux_ref[obs : 2 * obs, :] - mean, 0.0)
    high = departure.astype(jnp.bfloat16).astype(jnp.float32)
    for k in range(LANES - half - members):
        piece = (high, departure - high)[k % 2] if k < 4 else jnp.zeros(mean.shape, jnp.float32)
        dev_ref[(members + k) * obs : (members + k + 1) * obs, :] = piece
    for o in range(obs):
        d_ref[:, o * LANES : (o + 1) * LANES] = dev_ref[pl.ds(o, LANES, stride=obs), :].astype(jnp.bfloat16)
    for first, out_ref in ((0, low_ref), (2 * blocks, high_ref)):
        accumulate(members, obs, first, blocks, chunk, batch, d_ref, w_ref, acc_ref)
        packed_system(members, blocks, acc_ref, out_ref)


def own_kernel(members, obs, blocks, chunk, batch, d_ref, w_ref, out_ref, acc_ref):
    accumulate(members, obs, blocks, blocks, chunk, batch, d_ref, w_ref, acc_ref)
    packed_system(members, blocks, acc_ref, out_ref)


def state_kernel(members, part_ref, dev_ref, mean_ref, wide_ref):
    rows = mean_ref.shape[0]
    first = part_ref.shape[1] - rows
    total = part_ref[0, first:].astype(jnp.float32)
    for i in range(1, members):
        total = total + part_ref[i, first:].astype(jnp.float32)
    mean = total / members
    mean_ref[...] = mean
    for i in range(members):
        wide_ref[i * rows : (i + 1) * rows, :] = part_ref[i, first:].astype(jnp.float32) - mean
    for k in range(rows):
        dev_ref[:, k * LANES : (k + 1) * LANES] = wide_ref[pl.ds(k, members, stride=rows), :].astype(jnp.bfloat16)


def merge_kernel(own_ref, low_ref, high_ref, out_ref):
    total = own_ref[...] + low_ref[...].astype(jnp.float32) + high_ref[...].astype(jnp.float32)
    out_ref[...] = total.astype(jnp.bfloat16)


def finish_kernel(members, owned, parts, system_ref, dev_ref, mean_ref, out_ref, wide_ref):
    half = members // 2
    rows_out = mean_ref.shape[0]
    highest = lax.Precision.HIGHEST
    total = system_ref[0].astype(jnp.float32)
    for m in range(1, parts):
        total = total + system_ref[m].astype(jnp.float32)
    rows = lax.broadcasted_iota(jnp.int32, (members, members), 0)
    cols = lax.broadcasted_iota(jnp.int32, (members, members), 1)
    identity = jnp.where(rows == cols, 1.0, 0.0)
    lane = lax.broadcasted_iota(jnp.int32, (half, LANES), 1)

    def dot(a, b):
        return jnp.dot(a, b, precision=highest, preferred_element_type=jnp.float32)

    y_iter, z_iter, bound, force = [], [], [], []
    for r in range(owned):
        part = total[r * half : (r + 1) * half]
        square = jnp.concatenate([part, jnp.zeros((LANES - half, LANES), jnp.float32)], axis=0)
        below = jnp.transpose(square)[half : 2 * half]
        right = pltpu.roll(part, members, 1)
        bottom = jnp.where(lane < half, below, right)
        system = jnp.concatenate([part, bottom], axis=0)[:, :members]
        system = system + (members - 1) / inflation * identity
        sums = jnp.sum(jnp.abs(system), axis=1, keepdims=True)
        bound.append(jnp.max(sums, axis=0, keepdims=True))
        y_iter.append(system / bound[r])
        f_top = part[:, members : members + 1] + part[:, members + 1 : members + 2]
        f_low = part[:, members + 2 : members + 3] + part[:, members + 3 : members + 4]
        force.append(jnp.concatenate([f_top, f_low], axis=0))
    for sweep in range(NSIT):
        if sweep == 0:
            factor = [1.5 * identity - 0.5 * y for y in y_iter]
            z_next = factor
        else:
            factor = [1.5 * identity - 0.5 * dot(z, y) for z, y in zip(z_iter, y_iter)]
            z_next = [dot(f, z) for f, z in zip(factor, z_iter)]
        if sweep + 1 < NSIT:
            y_iter = [dot(y, f) for y, f in zip(y_iter, factor)]
        z_iter = z_next
    for r in range(owned):
        root = z_iter[r] / jnp.sqrt(bound[r])
        first = dot(root, jnp.broadcast_to(force[r], (members, LANES)))
        shiftu = dot(root, first)[:, :1]
        transform = math.sqrt(members - 1) * root + shiftu
        turned = jnp.transpose(transform).astype(jnp.bfloat16)
        for k in range(r, rows_out, owned):
            moved = jnp.dot(
                turned, dev_ref[:, k * LANES : (k + 1) * LANES], preferred_element_type=jnp.float32
            )
            wide_ref[pl.ds(k, members, stride=rows_out), :] = mean_ref[k : k + 1, :] + moved
    out_ref[...] = wide_ref[...].astype(jnp.bfloat16)


def unpack_kernel(owned, part_ref, out_ref):
    parts, local, rows, _ = part_ref.shape
    for i in range(local):
        groups = []
        for m in range(parts):
            value = part_ref[m, i].astype(jnp.float32)
            groups.append(
                jnp.concatenate([value[k : k + owned] for k in range(0, rows, owned)], axis=1)
            )
        out_ref[i] = jnp.concatenate(groups, axis=0).astype(out_ref.dtype)


def per_device(ens_state, obs_prior, obs_value, obs_prec, obs_len, pair_block, obs_pos):
    mem_count = lax.axis_size("mem")
    grid_count = lax.axis_size("grid")
    local = ens_state.shape[0]
    members = mem_count * local
    blocks_dev = ens_state.shape[1]
    obs_blocks = obs_prior.shape[1]
    owned = blocks_dev // mem_count
    obs = obs_blocks // mem_count
    half = members // 2
    nb_total = blocks_dev * grid_count
    vmem = pl.BlockSpec(memory_space=pltpu.VMEM)
    anywhere = pl.BlockSpec(memory_space=pl.ANY)

    pieces = ens_state.shape[2] // LANES

    def near(value):
        return pltpu.with_memory_space_constraint(value, pltpu.VMEM)

    extra = pieces * owned
    packed = pl.pallas_call(
        functools.partial(pack_kernel, mem_count, obs, owned),
        out_shape=jax.ShapeDtypeStruct((mem_count, local, obs + extra, LANES), obs_prior.dtype),
        in_specs=[pl.BlockSpec(memory_space=pltpu.HBM), pl.BlockSpec(memory_space=pltpu.HBM)],
        out_specs=pl.BlockSpec(memory_space=pltpu.HBM),
        scratch_shapes=[
            pltpu.VMEM((mem_count, local, obs, LANES), obs_prior.dtype),
            pltpu.VMEM(ens_state.shape, ens_state.dtype),
            pltpu.VMEM((mem_count, local, extra, LANES), ens_state.dtype),
            pltpu.SemaphoreType.DMA((2, mem_count)),
            pltpu.SemaphoreType.DMA((2,)),
        ],
        compiler_params=pltpu.CompilerParams(vmem_limit_bytes=16 * 2**20),
        name="pack",
    )(obs_prior, ens_state)
    prior = lax.all_to_all(packed, "mem", split_axis=0, concat_axis=0, tiled=True)
    prior = prior.reshape(members, obs + extra, LANES)
    from_low = shift(pair_block, "grid", 1)
    from_high = shift(pair_block, "grid", -1)

    blocks = 3 * blocks_dev
    weights, aux = pl.pallas_call(
        functools.partial(weight_kernel, float(nb_total), obs),
        out_shape=(
            pltpu.VMEM((blocks, obs * LANES), jnp.float32),
            pltpu.VMEM((2 * obs, LANES), jnp.float32),
        ),
        in_specs=[pl.BlockSpec(memory_space=pltpu.SMEM), vmem, vmem, vmem, anywhere, anywhere, anywhere],
        out_specs=(vmem, vmem),
        scratch_shapes=[
            pltpu.VMEM((obs, LANES), jnp.float32),
            pltpu.VMEM((obs, LANES), jnp.float32),
            pltpu.SemaphoreType.DMA((3,)),
        ],
        compiler_params=pltpu.CompilerParams(vmem_limit_bytes=16 * 2**20),
        name="weights",
    )(obs_len, near(from_low), pair_block, near(from_high), obs_prec, obs_pos, obs_value)

    chunk, batch = 6, 4
    system = pltpu.VMEM((blocks_dev * half, LANES), jnp.bfloat16)
    d_all, to_low, to_high = pl.pallas_call(
        functools.partial(neighbour_kernel, members, obs, blocks_dev, chunk, batch),
        out_shape=(pltpu.VMEM((LANES, obs * LANES), jnp.bfloat16), system, system),
        in_specs=[vmem, vmem, vmem],
        out_specs=(vmem, vmem, vmem),
        scratch_shapes=[
            pltpu.VMEM((LANES * obs, LANES), jnp.float32),
            pltpu.VMEM((blocks_dev * members, LANES), jnp.float32),
        ],
        compiler_params=pltpu.CompilerParams(vmem_limit_bytes=16 * 2**20),
        name="neighbours",
    )(near(prior), near(aux), near(weights))
    from_high = shift(to_low, "grid", -1)
    from_low = shift(to_high, "grid", 1)
    own = pl.pallas_call(
        functools.partial(own_kernel, members, obs, blocks_dev, chunk, batch),
        out_shape=pltpu.VMEM((blocks_dev * half, LANES), jnp.float32),
        in_specs=[vmem, vmem],
        out_specs=vmem,
        scratch_shapes=[pltpu.VMEM((blocks_dev * members, LANES), jnp.float32)],
        compiler_params=pltpu.CompilerParams(vmem_limit_bytes=16 * 2**20),
        name="own",
    )(near(d_all), near(weights))
    partial = pl.pallas_call(
        merge_kernel,
        out_shape=pltpu.VMEM((blocks_dev * half, LANES), jnp.bfloat16),
        in_specs=[vmem, vmem, vmem],
        out_specs=vmem,
        compiler_params=pltpu.CompilerParams(vmem_limit_bytes=16 * 2**20),
        name="merge",
    )(near(own), near(from_low), near(from_high))
    partial = partial.reshape(mem_count, owned * half, LANES)
    swapped = lax.all_to_all(partial, "mem", split_axis=0, concat_axis=0, tiled=True)
    deviation, mean = pl.pallas_call(
        functools.partial(state_kernel, members),
        out_shape=(
            pltpu.VMEM((members, extra * LANES), jnp.bfloat16),
            pltpu.VMEM((extra, LANES), jnp.float32),
        ),
        in_specs=[vmem],
        out_specs=(vmem, vmem),
        scratch_shapes=[pltpu.VMEM((members * extra, LANES), jnp.float32)],
        compiler_params=pltpu.CompilerParams(vmem_limit_bytes=16 * 2**20),
        name="state",
    )(near(prior))
    analysis = pl.pallas_call(
        functools.partial(finish_kernel, members, owned, mem_count),
        out_shape=jax.ShapeDtypeStruct((members * extra, LANES), jnp.bfloat16),
        in_specs=[vmem, vmem, vmem],
        out_specs=vmem,
        scratch_shapes=[pltpu.VMEM((members * extra, LANES), jnp.float32)],
        compiler_params=pltpu.CompilerParams(vmem_limit_bytes=16 * 2**20),
        name="finish",
    )(near(swapped), near(deviation), near(mean))
    analysis = analysis.reshape(mem_count, local, extra, LANES)
    analysis = lax.all_to_all(analysis, "mem", split_axis=0, concat_axis=0, tiled=True)
    return pl.pallas_call(
        functools.partial(unpack_kernel, owned),
        out_shape=jax.ShapeDtypeStruct(ens_state.shape, jnp.bfloat16),
        in_specs=[vmem],
        out_specs=vmem,
        compiler_params=pltpu.CompilerParams(vmem_limit_bytes=16 * 2**20),
        name="unpack",
    )(near(analysis))


def solution(mesh):
    placed = (
        P("mem", "grid", None),
        P("mem", "grid", None),
        P("grid", None),
        P("grid", None),
        P("grid"),
        P("grid", None),
        P("grid", None),
    )
    return jax.shard_map(
        per_device, mesh=mesh, in_specs=placed, out_specs=P("mem", "grid", None), check_vma=False
    )
```

```python
import functools
import math

import jax
import jax.numpy as jnp
from jax import lax
from jax.experimental import pallas as pl
from jax.experimental.pallas import tpu as pltpu
from jax.sharding import PartitionSpec as P

NSIT = 3
LOCR = 8
LANES = 128
COUNT = 127
UNIT = 4

inflation = 1.1


def shift(value, axis, step):
    count = lax.axis_size(axis)
    return lax.ppermute(value, axis, [(i, (i + step) % count) for i in range(count)])


def pack_kernel(parts, size, owned, src_ref, state_all, out_ref, stage_ref, state_ref, rows_ref, sems, last):
    local = state_all.shape[0]
    pieces = state_all.shape[2] // LANES
    inward = [
        pltpu.make_async_copy(src_ref.at[:, m * size : (m + 1) * size, :], stage_ref.at[m], sems.at[0, m])
        for m in range(parts)
    ]
    outward = [
        pltpu.make_async_copy(stage_ref.at[m], out_ref.at[m, :, 0:size, :], sems.at[1, m])
        for m in range(parts)
    ]
    state_in = pltpu.make_async_copy(state_all, state_ref, last.at[0])
    state_out = pltpu.make_async_copy(rows_ref, out_ref.at[:, :, size:, :], last.at[1])
    state_in.start()
    for copy in inward:
        copy.start()
    state_in.wait()
    for i in range(local):
        value = state_ref[i].astype(jnp.float32)
        for m in range(parts):
            rows = value[m * owned : (m + 1) * owned]
            rows = jnp.concatenate(
                [rows[:, q * LANES : (q + 1) * LANES] for q in range(pieces)], axis=0
            )
            rows_ref[m, i] = rows.astype(rows_ref.dtype)
    for m in range(parts):
        inward[m].wait()
        outward[m].start()
    state_out.start()
    for copy in outward:
        copy.wait()
    state_out.wait()


def weight_kernel(nb_total, obs, len_ref, low_ref, mid_ref, high_ref, prec_all, pos_all, value_all, out_ref, aux_ref, list_ref, prec_ref, pos_ref, sems):
    place = lax.axis_index("mem")
    grid_pos = lax.axis_index("grid")
    grid_count = lax.axis_size("grid")
    obs_blocks = prec_all.shape[0]
    blocks_dev = mid_ref.shape[0]
    mine = pl.ds(pl.multiple_of(place * obs, 8), obs)
    copies = [
        pltpu.make_async_copy(prec_all.at[mine], prec_ref, sems.at[0]),
        pltpu.make_async_copy(pos_all.at[mine], pos_ref, sems.at[1]),
        pltpu.make_async_copy(value_all.at[mine], aux_ref.at[obs : 2 * obs], sems.at[2]),
    ]
    for copy in copies:
        copy.start()
    row = lax.broadcasted_iota(jnp.int32, (obs, LANES), 0)
    count = jnp.zeros((obs, LANES), jnp.int32)
    for o in range(obs):
        count = jnp.where(row == o, len_ref[place * obs + o], count)
    lane = lax.broadcasted_iota(jnp.int32, (obs, LANES), 1)
    aux_ref[0:obs, :] = jnp.where(lane < count, 1.0, 0.0)
    base = grid_pos * obs_blocks + place * obs
    pairs = jnp.concatenate([low_ref[...], mid_ref[...], high_ref[...]], axis=0) - base
    index = lax.broadcasted_iota(jnp.int32, (blocks_dev, LANES), 0)
    centers = jnp.concatenate(
        [
            index + lax.rem(grid_pos + grid_count + step, grid_count) * blocks_dev
            for step in (-1, 0, 1)
        ],
        axis=0,
    ).astype(jnp.float32) + 0.5
    for copy in copies:
        copy.wait()
    blocks = 3 * blocks_dev
    slot = lax.broadcasted_iota(jnp.int32, (blocks, LANES), 1)
    found = jnp.zeros((blocks, LANES), jnp.int32)
    chosen = jnp.full((blocks, LANES), obs, jnp.int32)
    for o in range(obs):
        hit = jnp.max(jnp.where(pairs == o, 1.0, 0.0), axis=1, keepdims=True)
        hit = jnp.broadcast_to(hit, (blocks, LANES)).astype(jnp.int32)
        chosen = jnp.where(slot == jnp.where(hit > 0, found, -1), o, chosen)
        found = found + hit
        gap = jnp.abs(pos_ref[o : o + 1, :] - centers)
        distance = jnp.minimum(gap, nb_total - gap)
        relative = distance * (1.0 / LOCR)
        weight = prec_ref[o : o + 1, :] * jnp.exp(-0.5 * relative * relative)
        out_ref[pl.ds(o, blocks, stride=obs), :] = weight
    out_ref[blocks * obs :, :] = jnp.zeros((8, LANES), jnp.float32)
    list_ref[...] = jnp.where(slot == COUNT, found, chosen)


def accumulate(members, obs, first, blocks, list_ref, d_ref, w_ref, acc_ref):
    rows = d_ref.shape[1]
    acc_ref[...] = jnp.zeros(acc_ref.shape, jnp.float32)
    longest = list_ref[first, COUNT]
    for b in range(1, blocks):
        longest = jnp.maximum(longest, list_ref[first + b, COUNT])

    def step(turn, carry):
        for b in range(blocks):
            full, scaled = [], []
            for k in range(UNIT):
                o = list_ref[first + b, turn * UNIT + k]
                d = d_ref[o]
                row = w_ref[pl.ds((first + b) * obs + o, 1), :]
                w = jnp.broadcast_to(row, (16, LANES)).astype(jnp.bfloat16)
                full.append(d)
                scaled.append((d[:members].reshape(members // 16, 16, LANES) * w[None]).reshape(members, LANES))
            acc_ref[b * members : (b + 1) * members, 0:rows] += lax.dot_general(
                jnp.concatenate(scaled, axis=1),
                jnp.concatenate(full, axis=1),
                (((1,), (1,)), ((), ())),
                preferred_element_type=jnp.float32,
            )
        return carry

    lax.fori_loop(0, (longest + UNIT - 1) // UNIT, step, 0)


def packed_system(members, blocks, acc_ref, out_ref):
    half = members // 2
    lane = lax.broadcasted_iota(jnp.int32, (half, LANES), 1)
    for b in range(blocks):
        top = acc_ref[b * members : b * members + half, :]
        bottom = acc_ref[b * members + half : (b + 1) * members, :]
        corner = pltpu.roll(bottom, LANES - members, 1)
        force = pltpu.roll(bottom, 2, 1)
        value = jnp.where(lane >= members + 2, force, top)
        value = jnp.where(lane >= LANES - half, corner, value)
        out_ref[b * half : (b + 1) * half, :] = value.astype(out_ref.dtype)


def neighbour_kernel(members, obs, blocks, list_ref, prior_ref, aux_ref, w_ref, d_ref, low_ref, high_ref, dev_ref, acc_ref):
    rows = d_ref.shape[1]
    total = prior_ref[0, 0:obs].astype(jnp.float32)
    for i in range(1, members):
        total = total + prior_ref[i, 0:obs].astype(jnp.float32)
    mean = total / members
    valid = aux_ref[0:obs, :] > 0.0
    for i in range(members):
        dev_ref[i * obs : (i + 1) * obs, :] = jnp.where(
            valid, prior_ref[i, 0:obs].astype(jnp.float32) - mean, 0.0
        )
    departure = jnp.where(valid, aux_ref[obs : 2 * obs, :] - mean, 0.0)
    high = departure.astype(jnp.bfloat16).astype(jnp.float32)
    dev_ref[members * obs : (members + 1) * obs, :] = high
    dev_ref[(members + 1) * obs : (members + 2) * obs, :] = departure - high
    dev_ref[(members + 2) * obs :, :] = jnp.zeros(((rows - members - 2) * obs, LANES), jnp.float32)
    for o in range(obs):
        d_ref[o] = dev_ref[pl.ds(o, rows, stride=obs), :].astype(jnp.bfloat16)
    d_ref[obs] = jnp.zeros((rows, LANES), jnp.bfloat16)
    for first, out_ref in ((0, low_ref), (2 * blocks, high_ref)):
        accumulate(members, obs, first, blocks, list_ref, d_ref, w_ref, acc_ref)
        packed_system(members, blocks, acc_ref, out_ref)


def own_kernel(members, obs, blocks, list_ref, d_ref, w_ref, out_ref, acc_ref):
    accumulate(members, obs, blocks, blocks, list_ref, d_ref, w_ref, acc_ref)
    packed_system(members, blocks, acc_ref, out_ref)


def state_kernel(members, part_ref, dev_ref, mean_ref, wide_ref):
    rows = mean_ref.shape[0]
    first = part_ref.shape[1] - rows
    total = part_ref[0, first:].astype(jnp.float32)
    for i in range(1, members):
        total = total + part_ref[i, first:].astype(jnp.float32)
    mean = total / members
    mean_ref[...] = mean
    for i in range(members):
        wide_ref[i * rows : (i + 1) * rows, :] = part_ref[i, first:].astype(jnp.float32) - mean
    for k in range(rows):
        dev_ref[:, k * LANES : (k + 1) * LANES] = wide_ref[pl.ds(k, members, stride=rows), :].astype(jnp.bfloat16)


def merge_kernel(own_ref, low_ref, high_ref, out_ref):
    total = own_ref[...] + low_ref[...].astype(jnp.float32) + high_ref[...].astype(jnp.float32)
    out_ref[...] = total.astype(jnp.bfloat16)


def finish_kernel(members, owned, parts, system_ref, dev_ref, mean_ref, out_ref, wide_ref):
    half = members // 2
    rows_out = mean_ref.shape[0]
    highest = lax.Precision.HIGHEST
    total = system_ref[0].astype(jnp.float32)
    for m in range(1, parts):
        total = total + system_ref[m].astype(jnp.float32)
    rows = lax.broadcasted_iota(jnp.int32, (members, members), 0)
    cols = lax.broadcasted_iota(jnp.int32, (members, members), 1)
    identity = jnp.where(rows == cols, 1.0, 0.0)
    lane = lax.broadcasted_iota(jnp.int32, (half, LANES), 1)

    def dot(a, b):
        return jnp.dot(a, b, precision=highest, preferred_element_type=jnp.float32)

    y_iter, z_iter, bound, force = [], [], [], []
    for r in range(owned):
        part = total[r * half : (r + 1) * half]
        square = jnp.concatenate([part, jnp.zeros((LANES - half, LANES), jnp.float32)], axis=0)
        below = jnp.transpose(square)[half : 2 * half]
        right = pltpu.roll(part, members, 1)
        bottom = jnp.where(lane < half, below, right)
        system = jnp.concatenate([part, bottom], axis=0)[:, :members]
        system = system + (members - 1) / inflation * identity
        sums = jnp.sum(jnp.abs(system), axis=1, keepdims=True)
        bound.append(jnp.max(sums, axis=0, keepdims=True))
        y_iter.append(system / bound[r])
        f_top = part[:, members : members + 1] + part[:, members + 1 : members + 2]
        f_low = part[:, members + 2 : members + 3] + part[:, members + 3 : members + 4]
        force.append(jnp.concatenate([f_top, f_low], axis=0))
    for sweep in range(NSIT):
        if sweep == 0:
            factor = [1.5 * identity - 0.5 * y for y in y_iter]
            z_next = factor
        else:
            factor = [1.5 * identity - 0.5 * dot(z, y) for z, y in zip(z_iter, y_iter)]
            z_next = [dot(f, z) for f, z in zip(factor, z_iter)]
        if sweep + 1 < NSIT:
            y_iter = [dot(y, f) for y, f in zip(y_iter, factor)]
        z_iter = z_next
    for r in range(owned):
        root = z_iter[r] / jnp.sqrt(bound[r])
        first = dot(root, jnp.broadcast_to(force[r], (members, LANES)))
        shiftu = dot(root, first)[:, :1]
        transform = math.sqrt(members - 1) * root + shiftu
        turned = jnp.transpose(transform).astype(jnp.bfloat16)
        for k in range(r, rows_out, owned):
            moved = jnp.dot(
                turned, dev_ref[:, k * LANES : (k + 1) * LANES], preferred_element_type=jnp.float32
            )
            wide_ref[pl.ds(k, members, stride=rows_out), :] = mean_ref[k : k + 1, :] + moved
    out_ref[...] = wide_ref[...].astype(jnp.bfloat16)


def unpack_kernel(owned, part_ref, out_ref):
    parts, local, rows, _ = part_ref.shape
    for i in range(local):
        groups = []
        for m in range(parts):
            value = part_ref[m, i].astype(jnp.float32)
            groups.append(
                jnp.concatenate([value[k : k + owned] for k in range(0, rows, owned)], axis=1)
            )
        out_ref[i] = jnp.concatenate(groups, axis=0).astype(out_ref.dtype)


def per_device(ens_state, obs_prior, obs_value, obs_prec, obs_len, pair_block, obs_pos):
    mem_count = lax.axis_size("mem")
    grid_count = lax.axis_size("grid")
    local = ens_state.shape[0]
    members = mem_count * local
    blocks_dev = ens_state.shape[1]
    obs_blocks = obs_prior.shape[1]
    owned = blocks_dev // mem_count
    obs = obs_blocks // mem_count
    half = members // 2
    nb_total = blocks_dev * grid_count
    vmem = pl.BlockSpec(memory_space=pltpu.VMEM)
    anywhere = pl.BlockSpec(memory_space=pl.ANY)

    pieces = ens_state.shape[2] // LANES

    def near(value):
        return pltpu.with_memory_space_constraint(value, pltpu.VMEM)

    extra = pieces * owned

    def far(value):
        return pltpu.with_memory_space_constraint(value, pltpu.HBM)

    packed = pl.pallas_call(
        functools.partial(pack_kernel, mem_count, obs, owned),
        out_shape=jax.ShapeDtypeStruct((mem_count, local, obs + extra, LANES), obs_prior.dtype),
        in_specs=[pl.BlockSpec(memory_space=pltpu.HBM), pl.BlockSpec(memory_space=pltpu.HBM)],
        out_specs=pl.BlockSpec(memory_space=pltpu.HBM),
        scratch_shapes=[
            pltpu.VMEM((mem_count, local, obs, LANES), obs_prior.dtype),
            pltpu.VMEM(ens_state.shape, ens_state.dtype),
            pltpu.VMEM((mem_count, local, extra, LANES), ens_state.dtype),
            pltpu.SemaphoreType.DMA((2, mem_count)),
            pltpu.SemaphoreType.DMA((2,)),
        ],
        compiler_params=pltpu.CompilerParams(vmem_limit_bytes=16 * 2**20),
        name="pack",
    )(far(obs_prior), far(ens_state))
    prior = lax.all_to_all(packed, "mem", split_axis=0, concat_axis=0, tiled=True)
    prior = prior.reshape(members, obs + extra, LANES)
    from_low = shift(pair_block, "grid", 1)
    from_high = shift(pair_block, "grid", -1)

    blocks = 3 * blocks_dev
    weights, aux, lists = pl.pallas_call(
        functools.partial(weight_kernel, float(nb_total), obs),
        out_shape=(
            pltpu.VMEM((blocks * obs + 8, LANES), jnp.float32),
            pltpu.VMEM((2 * obs, LANES), jnp.float32),
            jax.ShapeDtypeStruct((blocks, LANES), jnp.int32),
        ),
        in_specs=[pl.BlockSpec(memory_space=pltpu.SMEM), vmem, vmem, vmem, anywhere, anywhere, anywhere],
        out_specs=(vmem, vmem, vmem),
        scratch_shapes=[
            pltpu.VMEM((obs, LANES), jnp.float32),
            pltpu.VMEM((obs, LANES), jnp.float32),
            pltpu.SemaphoreType.DMA((3,)),
        ],
        compiler_params=pltpu.CompilerParams(vmem_limit_bytes=16 * 2**20),
        name="weights",
    )(obs_len, near(from_low), pair_block, near(from_high), obs_prec, obs_pos, obs_value)

    rows = -(-(members + 2) // 16) * 16
    scalars = pl.BlockSpec(memory_space=pltpu.SMEM)
    system = pltpu.VMEM((blocks_dev * half, LANES), jnp.bfloat16)
    d_all, to_low, to_high = pl.pallas_call(
        functools.partial(neighbour_kernel, members, obs, blocks_dev),
        out_shape=(pltpu.VMEM((obs + 1, rows, LANES), jnp.bfloat16), system, system),
        in_specs=[scalars, vmem, vmem, vmem],
        out_specs=(vmem, vmem, vmem),
        scratch_shapes=[
            pltpu.VMEM((rows * obs, LANES), jnp.float32),
            pltpu.VMEM((blocks_dev * members, LANES), jnp.float32),
        ],
        compiler_params=pltpu.CompilerParams(vmem_limit_bytes=16 * 2**20),
        name="neighbours",
    )(lists, near(prior), near(aux), near(weights))
    from_high = shift(to_low, "grid", -1)
    from_low = shift(to_high, "grid", 1)
    own = pl.pallas_call(
        functools.partial(own_kernel, members, obs, blocks_dev),
        out_shape=pltpu.VMEM((blocks_dev * half, LANES), jnp.float32),
        in_specs=[scalars, vmem, vmem],
        out_specs=vmem,
        scratch_shapes=[pltpu.VMEM((blocks_dev * members, LANES), jnp.float32)],
        compiler_params=pltpu.CompilerParams(vmem_limit_bytes=16 * 2**20),
        name="own",
    )(lists, near(d_all), near(weights))
    partial = pl.pallas_call(
        merge_kernel,
        out_shape=pltpu.VMEM((blocks_dev * half, LANES), jnp.bfloat16),
        in_specs=[vmem, vmem, vmem],
        out_specs=vmem,
        compiler_params=pltpu.CompilerParams(vmem_limit_bytes=16 * 2**20),
        name="merge",
    )(near(own), near(from_low), near(from_high))
    partial = partial.reshape(mem_count, owned * half, LANES)
    swapped = lax.all_to_all(partial, "mem", split_axis=0, concat_axis=0, tiled=True)
    deviation, mean = pl.pallas_call(
        functools.partial(state_kernel, members),
        out_shape=(
            pltpu.VMEM((members, extra * LANES), jnp.bfloat16),
            pltpu.VMEM((extra, LANES), jnp.float32),
        ),
        in_specs=[vmem],
        out_specs=(vmem, vmem),
        scratch_shapes=[pltpu.VMEM((members * extra, LANES), jnp.float32)],
        compiler_params=pltpu.CompilerParams(vmem_limit_bytes=16 * 2**20),
        name="state",
    )(near(prior))
    analysis = pl.pallas_call(
        functools.partial(finish_kernel, members, owned, mem_count),
        out_shape=jax.ShapeDtypeStruct((members * extra, LANES), jnp.bfloat16),
        in_specs=[vmem, vmem, vmem],
        out_specs=vmem,
        scratch_shapes=[pltpu.VMEM((members * extra, LANES), jnp.float32)],
        compiler_params=pltpu.CompilerParams(vmem_limit_bytes=16 * 2**20),
        name="finish",
    )(near(swapped), near(deviation), near(mean))
    analysis = analysis.reshape(mem_count, local, extra, LANES)
    analysis = lax.all_to_all(analysis, "mem", split_axis=0, concat_axis=0, tiled=True)
    return pl.pallas_call(
        functools.partial(unpack_kernel, owned),
        out_shape=jax.ShapeDtypeStruct(ens_state.shape, jnp.bfloat16),
        in_specs=[vmem],
        out_specs=vmem,
        compiler_params=pltpu.CompilerParams(vmem_limit_bytes=16 * 2**20),
        name="unpack",
    )(near(analysis))


def solution(mesh):
    placed = (
        P("mem", "grid", None),
        P("mem", "grid", None),
        P("grid", None),
        P("grid", None),
        P("grid"),
        P("grid", None),
        P("grid", None),
    )
    return jax.shard_map(
        per_device, mesh=mesh, in_specs=placed, out_specs=P("mem", "grid", None), check_vma=False
    )
```

```python
import functools
import math

import jax
import jax.numpy as jnp
from jax import lax
from jax.experimental import pallas as pl
from jax.experimental.pallas import tpu as pltpu
from jax.sharding import PartitionSpec as P

NSIT = 3
LOCR = 8
LANES = 128
COUNT = 127
UNIT = 4

inflation = 1.1


def shift(value, step):
    mem_count = lax.axis_size("mem")
    grid_count = lax.axis_size("grid")
    pairs = []
    for m in range(mem_count):
        for g in range(grid_count):
            crossing = g % 2 == (1 if step > 0 else 0)
            other = m ^ 1 if crossing and mem_count % 2 == 0 else m
            pairs.append((m * grid_count + g, other * grid_count + (g + step) % grid_count))
    return lax.ppermute(value, ("mem", "grid"), pairs)


def pack_kernel(parts, size, owned, src_ref, state_all, out_ref, stage_ref, state_ref, rows_ref, sems, last):
    local = state_all.shape[0]
    pieces = state_all.shape[2] // LANES
    inward = [
        pltpu.make_async_copy(src_ref.at[:, m * size : (m + 1) * size, :], stage_ref.at[m], sems.at[0, m])
        for m in range(parts)
    ]
    outward = [
        pltpu.make_async_copy(stage_ref.at[m], out_ref.at[m, :, 0:size, :], sems.at[1, m])
        for m in range(parts)
    ]
    state_in = pltpu.make_async_copy(state_all, state_ref, last.at[0])
    state_out = pltpu.make_async_copy(rows_ref, out_ref.at[:, :, size:, :], last.at[1])
    state_in.start()
    for copy in inward:
        copy.start()
    state_in.wait()
    for i in range(local):
        value = state_ref[i].astype(jnp.float32)
        for m in range(parts):
            rows = value[m * owned : (m + 1) * owned]
            rows = jnp.concatenate(
                [rows[:, q * LANES : (q + 1) * LANES] for q in range(pieces)], axis=0
            )
            rows_ref[m, i] = rows.astype(rows_ref.dtype)
    for m in range(parts):
        inward[m].wait()
        outward[m].start()
    state_out.start()
    for copy in outward:
        copy.wait()
    state_out.wait()


def weight_kernel(nb_total, obs, len_ref, low_ref, mid_ref, high_ref, prec_all, pos_all, value_all, out_ref, aux_ref, list_ref, prec_ref, pos_ref, table_ref, sems):
    place = lax.axis_index("mem")
    grid_pos = lax.axis_index("grid")
    grid_count = lax.axis_size("grid")
    obs_blocks = prec_all.shape[0]
    blocks_dev = mid_ref.shape[0]
    mine = pl.ds(pl.multiple_of(place * obs, 8), obs)
    copies = [
        pltpu.make_async_copy(prec_all.at[mine], prec_ref, sems.at[0]),
        pltpu.make_async_copy(pos_all.at[mine], pos_ref, sems.at[1]),
        pltpu.make_async_copy(value_all.at[mine], aux_ref.at[obs : 2 * obs], sems.at[2]),
    ]
    for copy in copies:
        copy.start()
    row = lax.broadcasted_iota(jnp.int32, (obs, LANES), 0)
    count = jnp.zeros((obs, LANES), jnp.int32)
    for o in range(obs):
        count = jnp.where(row == o, len_ref[place * obs + o], count)
    lane = lax.broadcasted_iota(jnp.int32, (obs, LANES), 1)
    aux_ref[0:obs, :] = jnp.where(lane < count, 1.0, 0.0)
    base = grid_pos * obs_blocks + place * obs
    pairs = jnp.concatenate([low_ref[...], mid_ref[...], high_ref[...]], axis=0) - base
    index = lax.broadcasted_iota(jnp.int32, (blocks_dev, LANES), 0)
    centers = jnp.concatenate(
        [
            index + lax.rem(grid_pos + grid_count + step, grid_count) * blocks_dev
            for step in (-1, 0, 1)
        ],
        axis=0,
    ).astype(jnp.float32) + 0.5
    for copy in copies:
        copy.wait()
    blocks = 3 * blocks_dev
    slot = lax.broadcasted_iota(jnp.int32, (blocks, LANES), 1)
    found = jnp.zeros((blocks, LANES), jnp.int32)
    chosen = jnp.full((blocks, LANES), obs, jnp.int32)
    for o in range(obs):
        hit = jnp.max(jnp.where(pairs == o, 1.0, 0.0), axis=1, keepdims=True)
        hit = jnp.broadcast_to(hit, (blocks, LANES)).astype(jnp.int32)
        chosen = jnp.where(slot == jnp.where(hit > 0, found, -1), o, chosen)
        found = found + hit
        gap = jnp.abs(pos_ref[o : o + 1, :] - centers)
        distance = jnp.minimum(gap, nb_total - gap)
        relative = distance * (1.0 / LOCR)
        weight = prec_ref[o : o + 1, :] * jnp.exp(-0.5 * relative * relative)
        out_ref[pl.ds(o, blocks, stride=obs), :] = weight
    out_ref[blocks * obs :, :] = jnp.zeros((8, LANES), jnp.float32)
    table_ref[...] = jnp.where(slot == COUNT, found, chosen)
    copy = pltpu.make_async_copy(table_ref, list_ref, sems.at[3])
    copy.start()
    copy.wait()


def accumulate(members, obs, first, blocks, list_ref, d_ref, w_ref, acc_ref):
    rows = d_ref.shape[1]
    acc_ref[...] = jnp.zeros(acc_ref.shape, jnp.float32)
    longest = list_ref[first, COUNT]
    for b in range(1, blocks):
        longest = jnp.maximum(longest, list_ref[first + b, COUNT])

    def step(turn, carry):
        for b in range(blocks):
            full, scaled = [], []
            for k in range(UNIT):
                o = list_ref[first + b, turn * UNIT + k]
                d = d_ref[o]
                row = w_ref[pl.ds((first + b) * obs + o, 1), :]
                w = jnp.broadcast_to(row, (16, LANES)).astype(jnp.bfloat16)
                full.append(d)
                scaled.append((d[:members].reshape(members // 16, 16, LANES) * w[None]).reshape(members, LANES))
            acc_ref[b * members : (b + 1) * members, 0:rows] += lax.dot_general(
                jnp.concatenate(scaled, axis=1),
                jnp.concatenate(full, axis=1),
                (((1,), (1,)), ((), ())),
                preferred_element_type=jnp.float32,
            )
        return carry

    lax.fori_loop(0, (longest + UNIT - 1) // UNIT, step, 0)


def packed_system(members, blocks, acc_ref, out_ref):
    half = members // 2
    lane = lax.broadcasted_iota(jnp.int32, (half, LANES), 1)
    for b in range(blocks):
        top = acc_ref[b * members : b * members + half, :]
        bottom = acc_ref[b * members + half : (b + 1) * members, :]
        corner = pltpu.roll(bottom, LANES - members, 1)
        force = pltpu.roll(bottom, 2, 1)
        value = jnp.where(lane >= members + 2, force, top)
        value = jnp.where(lane >= LANES - half, corner, value)
        out_ref[b * half : (b + 1) * half, :] = value.astype(out_ref.dtype)


def neighbour_kernel(members, obs, blocks, list_ref, prior_ref, aux_ref, w_ref, d_ref, low_ref, high_ref, dev_ref, acc_ref):
    rows = d_ref.shape[1]
    total = prior_ref[0, 0:obs].astype(jnp.float32)
    for i in range(1, members):
        total = total + prior_ref[i, 0:obs].astype(jnp.float32)
    mean = total / members
    valid = aux_ref[0:obs, :] > 0.0
    for i in range(members):
        dev_ref[i * obs : (i + 1) * obs, :] = jnp.where(
            valid, prior_ref[i, 0:obs].astype(jnp.float32) - mean, 0.0
        )
    departure = jnp.where(valid, aux_ref[obs : 2 * obs, :] - mean, 0.0)
    high = departure.astype(jnp.bfloat16).astype(jnp.float32)
    dev_ref[members * obs : (members + 1) * obs, :] = high
    dev_ref[(members + 1) * obs : (members + 2) * obs, :] = departure - high
    dev_ref[(members + 2) * obs :, :] = jnp.zeros(((rows - members - 2) * obs, LANES), jnp.float32)
    for o in range(obs):
        d_ref[o] = dev_ref[pl.ds(o, rows, stride=obs), :].astype(jnp.bfloat16)
    d_ref[obs] = jnp.zeros((rows, LANES), jnp.bfloat16)
    for first, out_ref in ((0, low_ref), (2 * blocks, high_ref)):
        accumulate(members, obs, first, blocks, list_ref, d_ref, w_ref, acc_ref)
        packed_system(members, blocks, acc_ref, out_ref)


def own_kernel(members, obs, blocks, list_ref, d_ref, w_ref, out_ref, acc_ref):
    accumulate(members, obs, blocks, blocks, list_ref, d_ref, w_ref, acc_ref)
    packed_system(members, blocks, acc_ref, out_ref)


def state_kernel(members, part_ref, dev_ref, mean_ref, wide_ref):
    rows = mean_ref.shape[0]
    first = part_ref.shape[1] - rows
    total = part_ref[0, first:].astype(jnp.float32)
    for i in range(1, members):
        total = total + part_ref[i, first:].astype(jnp.float32)
    mean = total / members
    mean_ref[...] = mean
    for i in range(members):
        wide_ref[i * rows : (i + 1) * rows, :] = part_ref[i, first:].astype(jnp.float32) - mean
    for k in range(rows):
        dev_ref[:, k * LANES : (k + 1) * LANES] = wide_ref[pl.ds(k, members, stride=rows), :].astype(jnp.bfloat16)


def merge_kernel(own_ref, low_ref, high_ref, out_ref):
    total = own_ref[...] + low_ref[...].astype(jnp.float32) + high_ref[...].astype(jnp.float32)
    out_ref[...] = total.astype(jnp.bfloat16)


def finish_kernel(members, owned, parts, system_ref, dev_ref, mean_ref, out_ref, wide_ref):
    half = members // 2
    rows_out = mean_ref.shape[0]
    highest = lax.Precision.HIGHEST
    total = system_ref[0].astype(jnp.float32)
    for m in range(1, parts):
        total = total + system_ref[m].astype(jnp.float32)
    rows = lax.broadcasted_iota(jnp.int32, (members, members), 0)
    cols = lax.broadcasted_iota(jnp.int32, (members, members), 1)
    identity = jnp.where(rows == cols, 1.0, 0.0)
    lane = lax.broadcasted_iota(jnp.int32, (half, LANES), 1)

    def dot(a, b):
        return jnp.dot(a, b, precision=highest, preferred_element_type=jnp.float32)

    y_iter, z_iter, bound, force = [], [], [], []
    for r in range(owned):
        part = total[r * half : (r + 1) * half]
        square = jnp.concatenate([part, jnp.zeros((LANES - half, LANES), jnp.float32)], axis=0)
        below = jnp.transpose(square)[half : 2 * half]
        right = pltpu.roll(part, members, 1)
        bottom = jnp.where(lane < half, below, right)
        system = jnp.concatenate([part, bottom], axis=0)[:, :members]
        system = system + (members - 1) / inflation * identity
        sums = jnp.sum(jnp.abs(system), axis=1, keepdims=True)
        bound.append(jnp.max(sums, axis=0, keepdims=True))
        y_iter.append(system / bound[r])
        f_top = part[:, members : members + 1] + part[:, members + 1 : members + 2]
        f_low = part[:, members + 2 : members + 3] + part[:, members + 3 : members + 4]
        force.append(jnp.concatenate([f_top, f_low], axis=0))
    for sweep in range(NSIT):
        if sweep == 0:
            factor = [1.5 * identity - 0.5 * y for y in y_iter]
            z_next = factor
        else:
            factor = [1.5 * identity - 0.5 * dot(z, y) for z, y in zip(z_iter, y_iter)]
            z_next = [dot(f, z) for f, z in zip(factor, z_iter)]
        if sweep + 1 < NSIT:
            y_iter = [dot(y, f) for y, f in zip(y_iter, factor)]
        z_iter = z_next
    for r in range(owned):
        root = z_iter[r] / jnp.sqrt(bound[r])
        first = dot(root, jnp.broadcast_to(force[r], (members, LANES)))
        shiftu = dot(root, first)[:, :1]
        transform = math.sqrt(members - 1) * root + shiftu
        turned = jnp.transpose(transform).astype(jnp.bfloat16)
        for k in range(r, rows_out, owned):
            moved = jnp.dot(
                turned, dev_ref[:, k * LANES : (k + 1) * LANES], preferred_element_type=jnp.float32
            )
            wide_ref[pl.ds(k, members, stride=rows_out), :] = mean_ref[k : k + 1, :] + moved
    out_ref[...] = wide_ref[...].astype(jnp.bfloat16)


def unpack_kernel(owned, part_ref, out_ref):
    parts, local, rows, _ = part_ref.shape
    for i in range(local):
        groups = []
        for m in range(parts):
            value = part_ref[m, i].astype(jnp.float32)
            groups.append(
                jnp.concatenate([value[k : k + owned] for k in range(0, rows, owned)], axis=1)
            )
        out_ref[i] = jnp.concatenate(groups, axis=0).astype(out_ref.dtype)


def per_device(ens_state, obs_prior, obs_value, obs_prec, obs_len, pair_block, obs_pos):
    mem_count = lax.axis_size("mem")
    grid_count = lax.axis_size("grid")
    local = ens_state.shape[0]
    members = mem_count * local
    blocks_dev = ens_state.shape[1]
    obs_blocks = obs_prior.shape[1]
    owned = blocks_dev // mem_count
    obs = obs_blocks // mem_count
    half = members // 2
    nb_total = blocks_dev * grid_count
    vmem = pl.BlockSpec(memory_space=pltpu.VMEM)
    anywhere = pl.BlockSpec(memory_space=pl.ANY)

    pieces = ens_state.shape[2] // LANES

    def near(value):
        return pltpu.with_memory_space_constraint(value, pltpu.VMEM)

    extra = pieces * owned

    def far(value):
        return pltpu.with_memory_space_constraint(value, pltpu.HBM)

    packed = pl.pallas_call(
        functools.partial(pack_kernel, mem_count, obs, owned),
        out_shape=jax.ShapeDtypeStruct((mem_count, local, obs + extra, LANES), obs_prior.dtype),
        in_specs=[pl.BlockSpec(memory_space=pltpu.HBM), pl.BlockSpec(memory_space=pltpu.HBM)],
        out_specs=pl.BlockSpec(memory_space=pltpu.HBM),
        scratch_shapes=[
            pltpu.VMEM((mem_count, local, obs, LANES), obs_prior.dtype),
            pltpu.VMEM(ens_state.shape, ens_state.dtype),
            pltpu.VMEM((mem_count, local, extra, LANES), ens_state.dtype),
            pltpu.SemaphoreType.DMA((2, mem_count)),
            pltpu.SemaphoreType.DMA((2,)),
        ],
        compiler_params=pltpu.CompilerParams(vmem_limit_bytes=16 * 2**20),
        name="pack",
    )(far(obs_prior), far(ens_state))
    prior = lax.all_to_all(packed, "mem", split_axis=0, concat_axis=0, tiled=True)
    prior = prior.reshape(members, obs + extra, LANES)
    from_low = shift(pair_block, 1)
    from_high = shift(pair_block, -1)

    blocks = 3 * blocks_dev
    weights, aux, lists = pl.pallas_call(
        functools.partial(weight_kernel, float(nb_total), obs),
        out_shape=(
            pltpu.VMEM((blocks * obs + 8, LANES), jnp.float32),
            pltpu.VMEM((2 * obs, LANES), jnp.float32),
            pltpu.SMEM((blocks, LANES), jnp.int32),
        ),
        in_specs=[pl.BlockSpec(memory_space=pltpu.SMEM), vmem, vmem, vmem, anywhere, anywhere, anywhere],
        out_specs=(vmem, vmem, pl.BlockSpec(memory_space=pltpu.SMEM)),
        scratch_shapes=[
            pltpu.VMEM((obs, LANES), jnp.float32),
            pltpu.VMEM((obs, LANES), jnp.float32),
            pltpu.VMEM((blocks, LANES), jnp.int32),
            pltpu.SemaphoreType.DMA((4,)),
        ],
        compiler_params=pltpu.CompilerParams(vmem_limit_bytes=16 * 2**20),
        name="weights",
    )(obs_len, near(from_low), pair_block, near(from_high), obs_prec, obs_pos, obs_value)

    rows = -(-(members + 2) // 16) * 16
    scalars = pl.BlockSpec(memory_space=pltpu.SMEM)
    system = pltpu.VMEM((blocks_dev * half, LANES), jnp.bfloat16)
    d_all, to_low, to_high = pl.pallas_call(
        functools.partial(neighbour_kernel, members, obs, blocks_dev),
        out_shape=(pltpu.VMEM((obs + 1, rows, LANES), jnp.bfloat16), system, system),
        in_specs=[scalars, vmem, vmem, vmem],
        out_specs=(vmem, vmem, vmem),
        scratch_shapes=[
            pltpu.VMEM((rows * obs, LANES), jnp.float32),
            pltpu.VMEM((blocks_dev * members, LANES), jnp.float32),
        ],
        compiler_params=pltpu.CompilerParams(vmem_limit_bytes=16 * 2**20),
        name="neighbours",
    )(pltpu.with_memory_space_constraint(lists, pltpu.SMEM), near(prior), near(aux), near(weights))
    from_high = shift(to_low, -1)
    from_low = shift(to_high, 1)
    own = pl.pallas_call(
        functools.partial(own_kernel, members, obs, blocks_dev),
        out_shape=pltpu.VMEM((blocks_dev * half, LANES), jnp.float32),
        in_specs=[scalars, vmem, vmem],
        out_specs=vmem,
        scratch_shapes=[pltpu.VMEM((blocks_dev * members, LANES), jnp.float32)],
        compiler_params=pltpu.CompilerParams(vmem_limit_bytes=16 * 2**20),
        name="own",
    )(pltpu.with_memory_space_constraint(lists, pltpu.SMEM), near(d_all), near(weights))
    partial = pl.pallas_call(
        merge_kernel,
        out_shape=pltpu.VMEM((blocks_dev * half, LANES), jnp.bfloat16),
        in_specs=[vmem, vmem, vmem],
        out_specs=vmem,
        compiler_params=pltpu.CompilerParams(vmem_limit_bytes=16 * 2**20),
        name="merge",
    )(near(own), near(from_low), near(from_high))
    partial = partial.reshape(mem_count, owned * half, LANES)
    swapped = lax.all_to_all(partial, "mem", split_axis=0, concat_axis=0, tiled=True)
    deviation, mean = pl.pallas_call(
        functools.partial(state_kernel, members),
        out_shape=(
            pltpu.VMEM((members, extra * LANES), jnp.bfloat16),
            pltpu.VMEM((extra, LANES), jnp.float32),
        ),
        in_specs=[vmem],
        out_specs=(vmem, vmem),
        scratch_shapes=[pltpu.VMEM((members * extra, LANES), jnp.float32)],
        compiler_params=pltpu.CompilerParams(vmem_limit_bytes=16 * 2**20),
        name="state",
    )(near(prior))
    analysis = pl.pallas_call(
        functools.partial(finish_kernel, members, owned, mem_count),
        out_shape=jax.ShapeDtypeStruct((members * extra, LANES), jnp.bfloat16),
        in_specs=[vmem, vmem, vmem],
        out_specs=vmem,
        scratch_shapes=[pltpu.VMEM((members * extra, LANES), jnp.float32)],
        compiler_params=pltpu.CompilerParams(vmem_limit_bytes=16 * 2**20),
        name="finish",
    )(near(swapped), near(deviation), near(mean))
    analysis = analysis.reshape(mem_count, local, extra, LANES)
    analysis = lax.all_to_all(analysis, "mem", split_axis=0, concat_axis=0, tiled=True)
    return pl.pallas_call(
        functools.partial(unpack_kernel, owned),
        out_shape=jax.ShapeDtypeStruct(ens_state.shape, jnp.bfloat16),
        in_specs=[vmem],
        out_specs=vmem,
        compiler_params=pltpu.CompilerParams(vmem_limit_bytes=16 * 2**20),
        name="unpack",
    )(near(analysis))


def solution(mesh):
    placed = (
        P("mem", "grid", None),
        P("mem", "grid", None),
        P("grid", None),
        P("grid", None),
        P("grid"),
        P("grid", None),
        P("grid", None),
    )
    return jax.shard_map(
        per_device, mesh=mesh, in_specs=placed, out_specs=P("mem", "grid", None), check_vma=False
    )
```

```python
import functools
import math

import jax
import jax.numpy as jnp
from jax import lax
from jax.experimental import pallas as pl
from jax.experimental.pallas import tpu as pltpu
from jax.sharding import PartitionSpec as P

NSIT = 3
LOCR = 8
LANES = 128
COUNT = 127
UNIT = 4

inflation = 1.1


def shift(value, step):
    mem_count = lax.axis_size("mem")
    grid_count = lax.axis_size("grid")
    pairs = []
    for m in range(mem_count):
        for g in range(grid_count):
            crossing = g % 2 == (1 if step > 0 else 0)
            other = m ^ 1 if crossing and mem_count % 2 == 0 else m
            pairs.append((m * grid_count + g, other * grid_count + (g + step) % grid_count))
    return lax.ppermute(value, ("mem", "grid"), pairs)


def pack_kernel(parts, size, owned, src_ref, state_all, out_ref, stage_ref, state_ref, rows_ref, sems, last):
    local = state_all.shape[0]
    pieces = state_all.shape[2] // LANES
    inward = [
        pltpu.make_async_copy(src_ref.at[:, m * size : (m + 1) * size, :], stage_ref.at[m], sems.at[0, m])
        for m in range(parts)
    ]
    outward = [
        pltpu.make_async_copy(stage_ref.at[m], out_ref.at[m, :, 0:size, :], sems.at[1, m])
        for m in range(parts)
    ]
    state_in = pltpu.make_async_copy(state_all, state_ref, last.at[0])
    state_out = pltpu.make_async_copy(rows_ref, out_ref.at[:, :, size:, :], last.at[1])
    state_in.start()
    for copy in inward:
        copy.start()
    state_in.wait()
    for i in range(local):
        value = state_ref[i].astype(jnp.float32)
        for m in range(parts):
            rows = value[m * owned : (m + 1) * owned]
            rows = jnp.concatenate(
                [rows[:, q * LANES : (q + 1) * LANES] for q in range(pieces)], axis=0
            )
            rows_ref[m, i] = rows.astype(rows_ref.dtype)
    for m in range(parts):
        inward[m].wait()
        outward[m].start()
    state_out.start()
    for copy in outward:
        copy.wait()
    state_out.wait()


def weight_kernel(nb_total, obs, len_ref, low_ref, mid_ref, high_ref, prec_all, pos_all, value_all, out_ref, aux_ref, list_ref, prec_ref, pos_ref, table_ref, sems):
    place = lax.axis_index("mem")
    grid_pos = lax.axis_index("grid")
    grid_count = lax.axis_size("grid")
    obs_blocks = prec_all.shape[0]
    blocks_dev = mid_ref.shape[0]
    mine = pl.ds(pl.multiple_of(place * obs, 8), obs)
    copies = [
        pltpu.make_async_copy(prec_all.at[mine], prec_ref, sems.at[0]),
        pltpu.make_async_copy(pos_all.at[mine], pos_ref, sems.at[1]),
        pltpu.make_async_copy(value_all.at[mine], aux_ref.at[obs : 2 * obs], sems.at[2]),
    ]
    for copy in copies:
        copy.start()
    row = lax.broadcasted_iota(jnp.int32, (obs, LANES), 0)
    count = jnp.zeros((obs, LANES), jnp.int32)
    for o in range(obs):
        count = jnp.where(row == o, len_ref[place * obs + o], count)
    lane = lax.broadcasted_iota(jnp.int32, (obs, LANES), 1)
    aux_ref[0:obs, :] = jnp.where(lane < count, 1.0, 0.0)
    base = grid_pos * obs_blocks + place * obs
    pairs = jnp.concatenate([low_ref[...], mid_ref[...], high_ref[...]], axis=0) - base
    index = lax.broadcasted_iota(jnp.int32, (blocks_dev, LANES), 0)
    centers = jnp.concatenate(
        [
            index + lax.rem(grid_pos + grid_count + step, grid_count) * blocks_dev
            for step in (-1, 0, 1)
        ],
        axis=0,
    ).astype(jnp.float32) + 0.5
    for copy in copies:
        copy.wait()
    blocks = 3 * blocks_dev
    slot = lax.broadcasted_iota(jnp.int32, (blocks, LANES), 1)
    found = jnp.zeros((blocks, LANES), jnp.int32)
    chosen = jnp.full((blocks, LANES), obs, jnp.int32)
    for o in range(obs):
        hit = jnp.max(jnp.where(pairs == o, 1.0, 0.0), axis=1, keepdims=True)
        hit = jnp.broadcast_to(hit, (blocks, LANES)).astype(jnp.int32)
        chosen = jnp.where(slot == jnp.where(hit > 0, found, -1), o, chosen)
        found = found + hit
        gap = jnp.abs(pos_ref[o : o + 1, :] - centers)
        distance = jnp.minimum(gap, nb_total - gap)
        relative = distance * (1.0 / LOCR)
        weight = prec_ref[o : o + 1, :] * jnp.exp(-0.5 * relative * relative)
        out_ref[pl.ds(o, blocks, stride=obs), :] = weight
    out_ref[blocks * obs :, :] = jnp.zeros((8, LANES), jnp.float32)
    table_ref[...] = jnp.where(slot == COUNT, found, chosen)
    copy = pltpu.make_async_copy(table_ref, list_ref, sems.at[3])
    copy.start()
    copy.wait()


def accumulate(members, obs, first, blocks, list_ref, d_ref, w_ref, acc_ref):
    rows = d_ref.shape[1]
    acc_ref[...] = jnp.zeros(acc_ref.shape, jnp.float32)
    longest = list_ref[first, COUNT]
    for b in range(1, blocks):
        longest = jnp.maximum(longest, list_ref[first + b, COUNT])

    def step(turn, carry):
        for b in range(blocks):
            full, scaled = [], []
            for k in range(UNIT):
                o = list_ref[first + b, turn * UNIT + k]
                d = d_ref[o]
                row = w_ref[pl.ds((first + b) * obs + o, 1), :]
                w = jnp.broadcast_to(row, (16, LANES)).astype(jnp.bfloat16)
                full.append(d)
                scaled.append((d[:members].reshape(members // 16, 16, LANES) * w[None]).reshape(members, LANES))
            acc_ref[b * members : (b + 1) * members, 0:rows] += lax.dot_general(
                jnp.concatenate(scaled, axis=1),
                jnp.concatenate(full, axis=1),
                (((1,), (1,)), ((), ())),
                preferred_element_type=jnp.float32,
            )
        return carry

    lax.fori_loop(0, (longest + UNIT - 1) // UNIT, step, 0)


def packed_system(members, blocks, acc_ref, out_ref):
    half = members // 2
    lane = lax.broadcasted_iota(jnp.int32, (half, LANES), 1)
    for b in range(blocks):
        top = acc_ref[b * members : b * members + half, :]
        bottom = acc_ref[b * members + half : (b + 1) * members, :]
        corner = pltpu.roll(bottom, LANES - members, 1)
        force = pltpu.roll(bottom, 2, 1)
        value = jnp.where(lane >= members + 2, force, top)
        value = jnp.where(lane >= LANES - half, corner, value)
        out_ref[b * half : (b + 1) * half, :] = value.astype(out_ref.dtype)


def low_kernel(members, obs, blocks, list_ref, prior_ref, aux_ref, w_ref, d_ref, low_ref, dev_ref, acc_ref):
    rows = d_ref.shape[1]
    total = prior_ref[0, 0:obs].astype(jnp.float32)
    for i in range(1, members):
        total = total + prior_ref[i, 0:obs].astype(jnp.float32)
    mean = total / members
    valid = aux_ref[0:obs, :] > 0.0
    for i in range(members):
        dev_ref[i * obs : (i + 1) * obs, :] = jnp.where(
            valid, prior_ref[i, 0:obs].astype(jnp.float32) - mean, 0.0
        )
    departure = jnp.where(valid, aux_ref[obs : 2 * obs, :] - mean, 0.0)
    high = departure.astype(jnp.bfloat16).astype(jnp.float32)
    dev_ref[members * obs : (members + 1) * obs, :] = high
    dev_ref[(members + 1) * obs : (members + 2) * obs, :] = departure - high
    dev_ref[(members + 2) * obs :, :] = jnp.zeros(((rows - members - 2) * obs, LANES), jnp.float32)
    for o in range(obs):
        d_ref[o] = dev_ref[pl.ds(o, rows, stride=obs), :].astype(jnp.bfloat16)
    d_ref[obs] = jnp.zeros((rows, LANES), jnp.bfloat16)
    accumulate(members, obs, 0, blocks, list_ref, d_ref, w_ref, acc_ref)
    packed_system(members, blocks, acc_ref, low_ref)


def next_kernel(members, obs, first, blocks, list_ref, d_ref, w_ref, out_ref, acc_ref):
    accumulate(members, obs, first, blocks, list_ref, d_ref, w_ref, acc_ref)
    packed_system(members, blocks, acc_ref, out_ref)


def state_kernel(members, part_ref, dev_ref, mean_ref, wide_ref):
    rows = mean_ref.shape[0]
    first = part_ref.shape[1] - rows
    total = part_ref[0, first:].astype(jnp.float32)
    for i in range(1, members):
        total = total + part_ref[i, first:].astype(jnp.float32)
    mean = total / members
    mean_ref[...] = mean
    for i in range(members):
        wide_ref[i * rows : (i + 1) * rows, :] = part_ref[i, first:].astype(jnp.float32) - mean
    for k in range(rows):
        dev_ref[:, k * LANES : (k + 1) * LANES] = wide_ref[pl.ds(k, members, stride=rows), :].astype(jnp.bfloat16)


def merge_kernel(own_ref, low_ref, high_ref, out_ref):
    total = own_ref[...] + low_ref[...].astype(jnp.float32) + high_ref[...].astype(jnp.float32)
    out_ref[...] = total.astype(jnp.bfloat16)


def finish_kernel(members, owned, parts, system_ref, dev_ref, mean_ref, out_ref, wide_ref):
    half = members // 2
    rows_out = mean_ref.shape[0]
    total = system_ref[0].astype(jnp.float32)
    for m in range(1, parts):
        total = total + system_ref[m].astype(jnp.float32)
    rows = lax.broadcasted_iota(jnp.int32, (members, members), 0)
    cols = lax.broadcasted_iota(jnp.int32, (members, members), 1)
    identity = jnp.where(rows == cols, 1.0, 0.0)
    lane = lax.broadcasted_iota(jnp.int32, (half, LANES), 1)

    def split(value):
        top = value.astype(jnp.bfloat16)
        return top, (value - top.astype(jnp.float32)).astype(jnp.bfloat16)

    def dot(a, b):
        (a_top, a_low), (b_top, b_low) = split(a), split(b)

        def one(x, y):
            return jnp.dot(x, y, preferred_element_type=jnp.float32)

        return one(a_top, b_top) + (one(a_top, b_low) + one(a_low, b_top))

    y_iter, z_iter, bound, force = [], [], [], []
    for r in range(owned):
        part = total[r * half : (r + 1) * half]
        square = jnp.concatenate([part, jnp.zeros((LANES - half, LANES), jnp.float32)], axis=0)
        below = jnp.transpose(square)[half : 2 * half]
        right = pltpu.roll(part, members, 1)
        bottom = jnp.where(lane < half, below, right)
        system = jnp.concatenate([part, bottom], axis=0)[:, :members]
        system = system + (members - 1) / inflation * identity
        sums = jnp.sum(jnp.abs(system), axis=1, keepdims=True)
        bound.append(jnp.max(sums, axis=0, keepdims=True))
        y_iter.append(system / bound[r])
        f_top = part[:, members : members + 1] + part[:, members + 1 : members + 2]
        f_low = part[:, members + 2 : members + 3] + part[:, members + 3 : members + 4]
        force.append(jnp.concatenate([f_top, f_low], axis=0))
    for sweep in range(NSIT):
        if sweep == 0:
            factor = [1.5 * identity - 0.5 * y for y in y_iter]
            z_next = factor
        else:
            factor = [1.5 * identity - 0.5 * dot(z, y) for z, y in zip(z_iter, y_iter)]
            z_next = [dot(f, z) for f, z in zip(factor, z_iter)]
        if sweep + 1 < NSIT:
            y_iter = [dot(y, f) for y, f in zip(y_iter, factor)]
        z_iter = z_next
    for r in range(owned):
        root = z_iter[r] / jnp.sqrt(bound[r])
        first = dot(root, jnp.broadcast_to(force[r], (members, LANES)))
        shiftu = dot(root, first)[:, :1]
        transform = math.sqrt(members - 1) * root + shiftu
        turned = jnp.transpose(transform).astype(jnp.bfloat16)
        for k in range(r, rows_out, owned):
            moved = jnp.dot(
                turned, dev_ref[:, k * LANES : (k + 1) * LANES], preferred_element_type=jnp.float32
            )
            wide_ref[pl.ds(k, members, stride=rows_out), :] = mean_ref[k : k + 1, :] + moved
    out_ref[...] = wide_ref[...].astype(jnp.bfloat16)


def unpack_kernel(owned, part_ref, out_ref):
    parts, local, rows, _ = part_ref.shape
    for i in range(local):
        groups = []
        for m in range(parts):
            value = part_ref[m, i].astype(jnp.float32)
            groups.append(
                jnp.concatenate([value[k : k + owned] for k in range(0, rows, owned)], axis=1)
            )
        out_ref[i] = jnp.concatenate(groups, axis=0).astype(out_ref.dtype)


def per_device(ens_state, obs_prior, obs_value, obs_prec, obs_len, pair_block, obs_pos):
    mem_count = lax.axis_size("mem")
    grid_count = lax.axis_size("grid")
    local = ens_state.shape[0]
    members = mem_count * local
    blocks_dev = ens_state.shape[1]
    obs_blocks = obs_prior.shape[1]
    owned = blocks_dev // mem_count
    obs = obs_blocks // mem_count
    half = members // 2
    nb_total = blocks_dev * grid_count
    vmem = pl.BlockSpec(memory_space=pltpu.VMEM)
    anywhere = pl.BlockSpec(memory_space=pl.ANY)

    pieces = ens_state.shape[2] // LANES

    def near(value):
        return pltpu.with_memory_space_constraint(value, pltpu.VMEM)

    extra = pieces * owned

    def scalar(value):
        return pltpu.with_memory_space_constraint(value, pltpu.SMEM)

    def far(value):
        return pltpu.with_memory_space_constraint(value, pltpu.HBM)

    packed = pl.pallas_call(
        functools.partial(pack_kernel, mem_count, obs, owned),
        out_shape=jax.ShapeDtypeStruct((mem_count, local, obs + extra, LANES), obs_prior.dtype),
        in_specs=[pl.BlockSpec(memory_space=pltpu.HBM), pl.BlockSpec(memory_space=pltpu.HBM)],
        out_specs=pl.BlockSpec(memory_space=pltpu.HBM),
        scratch_shapes=[
            pltpu.VMEM((mem_count, local, obs, LANES), obs_prior.dtype),
            pltpu.VMEM(ens_state.shape, ens_state.dtype),
            pltpu.VMEM((mem_count, local, extra, LANES), ens_state.dtype),
            pltpu.SemaphoreType.DMA((2, mem_count)),
            pltpu.SemaphoreType.DMA((2,)),
        ],
        compiler_params=pltpu.CompilerParams(vmem_limit_bytes=16 * 2**20),
        name="pack",
    )(far(obs_prior), far(ens_state))
    prior = lax.all_to_all(packed, "mem", split_axis=0, concat_axis=0, tiled=True)
    prior = prior.reshape(members, obs + extra, LANES)
    from_low = shift(pair_block, 1)
    from_high = shift(pair_block, -1)

    blocks = 3 * blocks_dev
    weights, aux, lists = pl.pallas_call(
        functools.partial(weight_kernel, float(nb_total), obs),
        out_shape=(
            pltpu.VMEM((blocks * obs + 8, LANES), jnp.float32),
            pltpu.VMEM((2 * obs, LANES), jnp.float32),
            pltpu.SMEM((blocks, LANES), jnp.int32),
        ),
        in_specs=[pl.BlockSpec(memory_space=pltpu.SMEM), vmem, vmem, vmem, anywhere, anywhere, anywhere],
        out_specs=(vmem, vmem, pl.BlockSpec(memory_space=pltpu.SMEM)),
        scratch_shapes=[
            pltpu.VMEM((obs, LANES), jnp.float32),
            pltpu.VMEM((obs, LANES), jnp.float32),
            pltpu.VMEM((blocks, LANES), jnp.int32),
            pltpu.SemaphoreType.DMA((4,)),
        ],
        compiler_params=pltpu.CompilerParams(vmem_limit_bytes=16 * 2**20),
        name="weights",
    )(obs_len, near(from_low), pair_block, near(from_high), obs_prec, obs_pos, obs_value)

    rows = -(-(members + 2) // 16) * 16
    scalars = pl.BlockSpec(memory_space=pltpu.SMEM)
    system = pltpu.VMEM((blocks_dev * half, LANES), jnp.bfloat16)
    d_all, to_low = pl.pallas_call(
        functools.partial(low_kernel, members, obs, blocks_dev),
        out_shape=(pltpu.VMEM((obs + 1, rows, LANES), jnp.bfloat16), system),
        in_specs=[scalars, vmem, vmem, vmem],
        out_specs=(vmem, vmem),
        scratch_shapes=[
            pltpu.VMEM((rows * obs, LANES), jnp.float32),
            pltpu.VMEM((blocks_dev * members, LANES), jnp.float32),
        ],
        compiler_params=pltpu.CompilerParams(vmem_limit_bytes=16 * 2**20),
        name="low",
    )(scalar(lists), near(prior), near(aux), near(weights))
    from_high = shift(to_low, -1)

    def later(first, dtype):
        return pl.pallas_call(
            functools.partial(next_kernel, members, obs, first, blocks_dev),
            out_shape=pltpu.VMEM((blocks_dev * half, LANES), dtype),
            in_specs=[scalars, vmem, vmem],
            out_specs=vmem,
            scratch_shapes=[pltpu.VMEM((blocks_dev * members, LANES), jnp.float32)],
            compiler_params=pltpu.CompilerParams(vmem_limit_bytes=16 * 2**20),
        )(scalar(lists), near(d_all), near(weights))

    to_high = later(2 * blocks_dev, jnp.bfloat16)
    from_low = shift(to_high, 1)
    own = later(blocks_dev, jnp.float32)
    partial = pl.pallas_call(
        merge_kernel,
        out_shape=pltpu.VMEM((blocks_dev * half, LANES), jnp.bfloat16),
        in_specs=[vmem, vmem, vmem],
        out_specs=vmem,
        compiler_params=pltpu.CompilerParams(vmem_limit_bytes=16 * 2**20),
        name="merge",
    )(near(own), near(from_low), near(from_high))
    partial = partial.reshape(mem_count, owned * half, LANES)
    swapped = lax.all_to_all(partial, "mem", split_axis=0, concat_axis=0, tiled=True)
    deviation, mean = pl.pallas_call(
        functools.partial(state_kernel, members),
        out_shape=(
            pltpu.VMEM((members, extra * LANES), jnp.bfloat16),
            pltpu.VMEM((extra, LANES), jnp.float32),
        ),
        in_specs=[vmem],
        out_specs=(vmem, vmem),
        scratch_shapes=[pltpu.VMEM((members * extra, LANES), jnp.float32)],
        compiler_params=pltpu.CompilerParams(vmem_limit_bytes=16 * 2**20),
        name="state",
    )(near(prior))
    analysis = pl.pallas_call(
        functools.partial(finish_kernel, members, owned, mem_count),
        out_shape=pltpu.VMEM((members * extra, LANES), jnp.bfloat16),
        in_specs=[vmem, vmem, vmem],
        out_specs=vmem,
        scratch_shapes=[pltpu.VMEM((members * extra, LANES), jnp.float32)],
        compiler_params=pltpu.CompilerParams(vmem_limit_bytes=16 * 2**20),
        name="finish",
    )(near(swapped), near(deviation), near(mean))
    analysis = analysis.reshape(mem_count, local, extra, LANES)
    analysis = lax.all_to_all(analysis, "mem", split_axis=0, concat_axis=0, tiled=True)
    return pl.pallas_call(
        functools.partial(unpack_kernel, owned),
        out_shape=jax.ShapeDtypeStruct(ens_state.shape, jnp.bfloat16),
        in_specs=[vmem],
        out_specs=vmem,
        compiler_params=pltpu.CompilerParams(vmem_limit_bytes=16 * 2**20),
        name="unpack",
    )(near(analysis))


def solution(mesh):
    placed = (
        P("mem", "grid", None),
        P("mem", "grid", None),
        P("grid", None),
        P("grid", None),
        P("grid"),
        P("grid", None),
        P("grid", None),
    )
    return jax.shard_map(
        per_device, mesh=mesh, in_specs=placed, out_specs=P("mem", "grid", None), check_vma=False
    )
```

```python
import functools
import math

import jax
import jax.numpy as jnp
from jax import lax
from jax.experimental import pallas as pl
from jax.experimental.pallas import tpu as pltpu
from jax.sharding import PartitionSpec as P

NSIT = 3
LOCR = 8
LANES = 128
COUNT = 127
UNIT = 4
TURN = 18
ROOM = 256
SPAN = 16

inflation = 1.1


def shift(value, step):
    mem_count = lax.axis_size("mem")
    grid_count = lax.axis_size("grid")
    pairs = []
    for m in range(mem_count):
        for g in range(grid_count):
            crossing = g % 2 == (1 if step > 0 else 0)
            other = m ^ 1 if crossing and mem_count % 2 == 0 else m
            pairs.append((m * grid_count + g, other * grid_count + (g + step) % grid_count))
    return lax.ppermute(value, ("mem", "grid"), pairs)


def pack_kernel(parts, size, owned, src_ref, state_all, out_ref, stage_ref, state_ref, rows_ref, sems, last):
    local = state_all.shape[0]
    pieces = state_all.shape[2] // LANES
    inward = [
        pltpu.make_async_copy(src_ref.at[:, m * size : (m + 1) * size, :], stage_ref.at[m], sems.at[0, m])
        for m in range(parts)
    ]
    outward = [
        pltpu.make_async_copy(stage_ref.at[m], out_ref.at[m, :, 0:size, :], sems.at[1, m])
        for m in range(parts)
    ]
    state_in = pltpu.make_async_copy(state_all, state_ref, last.at[0])
    state_out = pltpu.make_async_copy(rows_ref, out_ref.at[:, :, size:, :], last.at[1])
    state_in.start()
    for copy in inward:
        copy.start()
    state_in.wait()
    for i in range(local):
        value = state_ref[i].astype(jnp.float32)
        for m in range(parts):
            rows = value[m * owned : (m + 1) * owned]
            rows = jnp.concatenate(
                [rows[:, q * LANES : (q + 1) * LANES] for q in range(pieces)], axis=0
            )
            rows_ref[m, i] = rows.astype(rows_ref.dtype)
    for m in range(parts):
        inward[m].wait()
        outward[m].start()
    state_out.start()
    for copy in outward:
        copy.wait()
    state_out.wait()


def weight_kernel(nb_total, obs, len_ref, low_ref, mid_ref, high_ref, prec_all, pos_all, value_all, out_ref, aux_ref, list_ref, item_ref, prec_ref, pos_ref, table_ref, sems):
    place = lax.axis_index("mem")
    grid_pos = lax.axis_index("grid")
    grid_count = lax.axis_size("grid")
    obs_blocks = prec_all.shape[0]
    blocks_dev = mid_ref.shape[0]
    mine = pl.ds(pl.multiple_of(place * obs, 8), obs)
    copies = [
        pltpu.make_async_copy(prec_all.at[mine], prec_ref, sems.at[0]),
        pltpu.make_async_copy(pos_all.at[mine], pos_ref, sems.at[1]),
        pltpu.make_async_copy(value_all.at[mine], aux_ref.at[obs : 2 * obs], sems.at[2]),
    ]
    for copy in copies:
        copy.start()
    row = lax.broadcasted_iota(jnp.int32, (obs, LANES), 0)
    count = jnp.zeros((obs, LANES), jnp.int32)
    for o in range(obs):
        count = jnp.where(row == o, len_ref[place * obs + o], count)
    lane = lax.broadcasted_iota(jnp.int32, (obs, LANES), 1)
    aux_ref[0:obs, :] = jnp.where(lane < count, 1.0, 0.0)
    base = grid_pos * obs_blocks + place * obs
    pairs = jnp.concatenate([low_ref[...], mid_ref[...], high_ref[...]], axis=0) - base
    index = lax.broadcasted_iota(jnp.int32, (blocks_dev, LANES), 0)
    centers = jnp.concatenate(
        [
            index + lax.rem(grid_pos + grid_count + step, grid_count) * blocks_dev
            for step in (-1, 0, 1)
        ],
        axis=0,
    ).astype(jnp.float32) + 0.5
    for copy in copies:
        copy.wait()
    blocks = 3 * blocks_dev
    slot = lax.broadcasted_iota(jnp.int32, (blocks, LANES), 1)
    found = jnp.zeros((blocks, LANES), jnp.int32)
    chosen = jnp.full((blocks, LANES), obs, jnp.int32)
    for o in range(obs):
        hit = jnp.max(jnp.where(pairs == o, 1.0, 0.0), axis=1, keepdims=True)
        hit = jnp.broadcast_to(hit, (blocks, LANES)).astype(jnp.int32)
        chosen = jnp.where(slot == jnp.where(hit > 0, found, -1), o, chosen)
        found = found + hit
        gap = jnp.abs(pos_ref[o : o + 1, :] - centers)
        distance = jnp.minimum(gap, nb_total - gap)
        relative = distance * (1.0 / LOCR)
        weight = prec_ref[o : o + 1, :] * jnp.exp(-0.5 * relative * relative)
        out_ref[pl.ds(o, blocks, stride=obs), :] = weight
    out_ref[blocks * obs :, :] = jnp.zeros((out_ref.shape[0] - blocks * obs, LANES), jnp.float32)
    table_ref[0:blocks] = jnp.where(slot == COUNT, found, chosen)
    table_ref[blocks:] = jnp.full((table_ref.shape[0] - blocks, LANES), obs, jnp.int32)
    copy = pltpu.make_async_copy(table_ref, list_ref, sems.at[3])
    copy.start()
    copy.wait()
    most = -(-obs // UNIT)
    for group in range(3):
        at = 0
        for b in range(group * blocks_dev, (group + 1) * blocks_dev):
            for k in range(most):
                item_ref[group, at + k] = b * SPAN + k
            at = at + lax.shift_right_logical(list_ref[b, COUNT] + UNIT - 1, 2)
        for k in range(TURN):
            item_ref[group, at + k] = (group + 1) * blocks_dev * SPAN + most
        item_ref[group, ROOM - 1] = at


def accumulate(members, obs, group, blocks, list_ref, item_ref, d_ref, w_ref, acc_ref):
    rows = d_ref.shape[1]
    acc_ref[...] = jnp.zeros(acc_ref.shape, jnp.float32)

    def step(turn, carry):
        for u in range(TURN):
            item = item_ref[group, turn * TURN + u]
            b = lax.shift_right_logical(item, 4)
            first = lax.bitwise_and(item, SPAN - 1) * UNIT
            full, scaled = [], []
            for k in range(UNIT):
                o = list_ref[b, first + k]
                d = d_ref[o]
                row = w_ref[pl.ds(b * obs + o, 1), :]
                w = jnp.broadcast_to(row, (16, LANES)).astype(jnp.bfloat16)
                full.append(d)
                scaled.append((d[:members].reshape(members // 16, 16, LANES) * w[None]).reshape(members, LANES))
            at = pl.multiple_of((b - group * blocks) * members, 16)
            acc_ref[pl.ds(at, members), 0:rows] += lax.dot_general(
                jnp.concatenate(scaled, axis=1),
                jnp.concatenate(full, axis=1),
                (((1,), (1,)), ((), ())),
                preferred_element_type=jnp.float32,
            )
        return carry

    lax.fori_loop(0, (item_ref[group, ROOM - 1] + TURN - 1) // TURN, step, 0)


def packed_system(members, blocks, acc_ref, out_ref):
    half = members // 2
    lane = lax.broadcasted_iota(jnp.int32, (half, LANES), 1)
    for b in range(blocks):
        top = acc_ref[b * members : b * members + half, :]
        bottom = acc_ref[b * members + half : (b + 1) * members, :]
        corner = pltpu.roll(bottom, LANES - members, 1)
        force = pltpu.roll(bottom, 2, 1)
        value = jnp.where(lane >= members + 2, force, top)
        value = jnp.where(lane >= LANES - half, corner, value)
        out_ref[b * half : (b + 1) * half, :] = value.astype(out_ref.dtype)


def low_kernel(members, obs, blocks, list_ref, item_ref, prior_ref, aux_ref, w_ref, d_ref, low_ref, dev_ref, acc_ref):
    rows = d_ref.shape[1]
    total = prior_ref[0, 0:obs].astype(jnp.float32)
    for i in range(1, members):
        total = total + prior_ref[i, 0:obs].astype(jnp.float32)
    mean = total / members
    valid = aux_ref[0:obs, :] > 0.0
    for i in range(members):
        dev_ref[i * obs : (i + 1) * obs, :] = jnp.where(
            valid, prior_ref[i, 0:obs].astype(jnp.float32) - mean, 0.0
        )
    departure = jnp.where(valid, aux_ref[obs : 2 * obs, :] - mean, 0.0)
    high = departure.astype(jnp.bfloat16).astype(jnp.float32)
    dev_ref[members * obs : (members + 1) * obs, :] = high
    dev_ref[(members + 1) * obs : (members + 2) * obs, :] = departure - high
    dev_ref[(members + 2) * obs :, :] = jnp.zeros(((rows - members - 2) * obs, LANES), jnp.float32)
    for o in range(obs):
        d_ref[o] = dev_ref[pl.ds(o, rows, stride=obs), :].astype(jnp.bfloat16)
    d_ref[obs] = jnp.zeros((rows, LANES), jnp.bfloat16)
    accumulate(members, obs, 0, blocks, list_ref, item_ref, d_ref, w_ref, acc_ref)
    packed_system(members, blocks, acc_ref, low_ref)


def next_kernel(members, obs, group, blocks, list_ref, item_ref, d_ref, w_ref, out_ref, acc_ref):
    accumulate(members, obs, group, blocks, list_ref, item_ref, d_ref, w_ref, acc_ref)
    packed_system(members, blocks, acc_ref, out_ref)


def state_kernel(members, part_ref, dev_ref, mean_ref, wide_ref):
    rows = mean_ref.shape[0]
    first = part_ref.shape[1] - rows
    total = part_ref[0, first:].astype(jnp.float32)
    for i in range(1, members):
        total = total + part_ref[i, first:].astype(jnp.float32)
    mean = total / members
    mean_ref[...] = mean
    for i in range(members):
        wide_ref[i * rows : (i + 1) * rows, :] = part_ref[i, first:].astype(jnp.float32) - mean
    for k in range(rows):
        dev_ref[:, k * LANES : (k + 1) * LANES] = wide_ref[pl.ds(k, members, stride=rows), :].astype(jnp.bfloat16)


def merge_kernel(own_ref, low_ref, high_ref, out_ref):
    total = own_ref[...] + low_ref[...].astype(jnp.float32) + high_ref[...].astype(jnp.float32)
    out_ref[...] = total.astype(jnp.bfloat16)


def finish_kernel(members, owned, parts, system_ref, dev_ref, mean_ref, out_ref, wide_ref):
    half = members // 2
    rows_out = mean_ref.shape[0]
    total = system_ref[0].astype(jnp.float32)
    for m in range(1, parts):
        total = total + system_ref[m].astype(jnp.float32)
    rows = lax.broadcasted_iota(jnp.int32, (members, members), 0)
    cols = lax.broadcasted_iota(jnp.int32, (members, members), 1)
    identity = jnp.where(rows == cols, 1.0, 0.0)
    lane = lax.broadcasted_iota(jnp.int32, (half, LANES), 1)

    def split(value):
        top = value.astype(jnp.bfloat16)
        return top, (value - top.astype(jnp.float32)).astype(jnp.bfloat16)

    def dot(a, b):
        (a_top, a_low), (b_top, b_low) = split(a), split(b)

        def one(x, y):
            return jnp.dot(x, y, preferred_element_type=jnp.float32)

        return one(a_top, b_top) + (one(a_top, b_low) + one(a_low, b_top))

    y_iter, z_iter, bound, force = [], [], [], []
    for r in range(owned):
        part = total[r * half : (r + 1) * half]
        square = jnp.concatenate([part, jnp.zeros((LANES - half, LANES), jnp.float32)], axis=0)
        below = jnp.transpose(square)[half : 2 * half]
        right = pltpu.roll(part, members, 1)
        bottom = jnp.where(lane < half, below, right)
        system = jnp.concatenate([part, bottom], axis=0)[:, :members]
        system = system + (members - 1) / inflation * identity
        sums = jnp.sum(jnp.abs(system), axis=1, keepdims=True)
        bound.append(jnp.max(sums, axis=0, keepdims=True))
        y_iter.append(system / bound[r])
        f_top = part[:, members : members + 1] + part[:, members + 1 : members + 2]
        f_low = part[:, members + 2 : members + 3] + part[:, members + 3 : members + 4]
        force.append(jnp.concatenate([f_top, f_low], axis=0))
    for sweep in range(NSIT):
        if sweep == 0:
            factor = [1.5 * identity - 0.5 * y for y in y_iter]
            z_next = factor
        else:
            factor = [1.5 * identity - 0.5 * dot(z, y) for z, y in zip(z_iter, y_iter)]
            z_next = [dot(f, z) for f, z in zip(factor, z_iter)]
        if sweep + 1 < NSIT:
            y_iter = [dot(y, f) for y, f in zip(y_iter, factor)]
        z_iter = z_next
    for r in range(owned):
        root = z_iter[r] / jnp.sqrt(bound[r])
        first = dot(root, jnp.broadcast_to(force[r], (members, LANES)))
        shiftu = dot(root, first)[:, :1]
        transform = math.sqrt(members - 1) * root + shiftu
        turned = jnp.transpose(transform).astype(jnp.bfloat16)
        for k in range(r, rows_out, owned):
            moved = jnp.dot(
                turned, dev_ref[:, k * LANES : (k + 1) * LANES], preferred_element_type=jnp.float32
            )
            wide_ref[pl.ds(k, members, stride=rows_out), :] = mean_ref[k : k + 1, :] + moved
    out_ref[...] = wide_ref[...].astype(jnp.bfloat16)


def unpack_kernel(owned, part_ref, out_ref):
    parts, local, rows, _ = part_ref.shape
    for i in range(local):
        groups = []
        for m in range(parts):
            value = part_ref[m, i].astype(jnp.float32)
            groups.append(
                jnp.concatenate([value[k : k + owned] for k in range(0, rows, owned)], axis=1)
            )
        out_ref[i] = jnp.concatenate(groups, axis=0).astype(out_ref.dtype)


def per_device(ens_state, obs_prior, obs_value, obs_prec, obs_len, pair_block, obs_pos):
    mem_count = lax.axis_size("mem")
    grid_count = lax.axis_size("grid")
    local = ens_state.shape[0]
    members = mem_count * local
    blocks_dev = ens_state.shape[1]
    obs_blocks = obs_prior.shape[1]
    owned = blocks_dev // mem_count
    obs = obs_blocks // mem_count
    half = members // 2
    nb_total = blocks_dev * grid_count
    vmem = pl.BlockSpec(memory_space=pltpu.VMEM)
    anywhere = pl.BlockSpec(memory_space=pl.ANY)
    scalars = pl.BlockSpec(memory_space=pltpu.SMEM)

    pieces = ens_state.shape[2] // LANES

    def near(value):
        return pltpu.with_memory_space_constraint(value, pltpu.VMEM)

    extra = pieces * owned

    def scalar(value):
        return pltpu.with_memory_space_constraint(value, pltpu.SMEM)

    def far(value):
        return pltpu.with_memory_space_constraint(value, pltpu.HBM)

    packed = pl.pallas_call(
        functools.partial(pack_kernel, mem_count, obs, owned),
        out_shape=jax.ShapeDtypeStruct((mem_count, local, obs + extra, LANES), obs_prior.dtype),
        in_specs=[pl.BlockSpec(memory_space=pltpu.HBM), pl.BlockSpec(memory_space=pltpu.HBM)],
        out_specs=pl.BlockSpec(memory_space=pltpu.HBM),
        scratch_shapes=[
            pltpu.VMEM((mem_count, local, obs, LANES), obs_prior.dtype),
            pltpu.VMEM(ens_state.shape, ens_state.dtype),
            pltpu.VMEM((mem_count, local, extra, LANES), ens_state.dtype),
            pltpu.SemaphoreType.DMA((2, mem_count)),
            pltpu.SemaphoreType.DMA((2,)),
        ],
        compiler_params=pltpu.CompilerParams(vmem_limit_bytes=16 * 2**20),
        name="pack",
    )(far(obs_prior), far(ens_state))
    prior = lax.all_to_all(packed, "mem", split_axis=0, concat_axis=0, tiled=True)
    prior = prior.reshape(members, obs + extra, LANES)
    from_low = shift(pair_block, 1)
    from_high = shift(pair_block, -1)

    blocks = 3 * blocks_dev
    weights, aux, lists, items = pl.pallas_call(
        functools.partial(weight_kernel, float(nb_total), obs),
        out_shape=(
            pltpu.VMEM(((blocks + 1) * obs + 8, LANES), jnp.float32),
            pltpu.VMEM((2 * obs, LANES), jnp.float32),
            pltpu.SMEM((blocks + 8, LANES), jnp.int32),
            pltpu.SMEM((3, ROOM), jnp.int32),
        ),
        in_specs=[pl.BlockSpec(memory_space=pltpu.SMEM), vmem, vmem, vmem, anywhere, anywhere, anywhere],
        out_specs=(vmem, vmem, scalars, scalars),
        scratch_shapes=[
            pltpu.VMEM((obs, LANES), jnp.float32),
            pltpu.VMEM((obs, LANES), jnp.float32),
            pltpu.VMEM((blocks + 8, LANES), jnp.int32),
            pltpu.SemaphoreType.DMA((4,)),
        ],
        compiler_params=pltpu.CompilerParams(vmem_limit_bytes=16 * 2**20),
        name="weights",
    )(obs_len, near(from_low), pair_block, near(from_high), obs_prec, obs_pos, obs_value)

    rows = -(-(members + 2) // 16) * 16
    system = pltpu.VMEM((blocks_dev * half, LANES), jnp.bfloat16)
    d_all, to_low = pl.pallas_call(
        functools.partial(low_kernel, members, obs, blocks_dev),
        out_shape=(pltpu.VMEM((obs + 1, rows, LANES), jnp.bfloat16), system),
        in_specs=[scalars, scalars, vmem, vmem, vmem],
        out_specs=(vmem, vmem),
        scratch_shapes=[
            pltpu.VMEM((rows * obs, LANES), jnp.float32),
            pltpu.VMEM(((blocks_dev + 1) * members, LANES), jnp.float32),
        ],
        compiler_params=pltpu.CompilerParams(vmem_limit_bytes=16 * 2**20),
        name="low",
    )(scalar(lists), scalar(items), near(prior), near(aux), near(weights))
    from_high = shift(to_low, -1)

    def later(group, dtype):
        return pl.pallas_call(
            functools.partial(next_kernel, members, obs, group, blocks_dev),
            out_shape=pltpu.VMEM((blocks_dev * half, LANES), dtype),
            in_specs=[scalars, scalars, vmem, vmem],
            out_specs=vmem,
            scratch_shapes=[pltpu.VMEM(((blocks_dev + 1) * members, LANES), jnp.float32)],
            compiler_params=pltpu.CompilerParams(vmem_limit_bytes=16 * 2**20),
        )(scalar(lists), scalar(items), near(d_all), near(weights))

    to_high = later(2, jnp.bfloat16)
    from_low = shift(to_high, 1)
    own = later(1, jnp.float32)
    partial = pl.pallas_call(
        merge_kernel,
        out_shape=pltpu.VMEM((blocks_dev * half, LANES), jnp.bfloat16),
        in_specs=[vmem, vmem, vmem],
        out_specs=vmem,
        compiler_params=pltpu.CompilerParams(vmem_limit_bytes=16 * 2**20),
        name="merge",
    )(near(own), near(from_low), near(from_high))
    partial = partial.reshape(mem_count, owned * half, LANES)
    swapped = lax.all_to_all(partial, "mem", split_axis=0, concat_axis=0, tiled=True)
    deviation, mean = pl.pallas_call(
        functools.partial(state_kernel, members),
        out_shape=(
            pltpu.VMEM((members, extra * LANES), jnp.bfloat16),
            pltpu.VMEM((extra, LANES), jnp.float32),
        ),
        in_specs=[vmem],
        out_specs=(vmem, vmem),
        scratch_shapes=[pltpu.VMEM((members * extra, LANES), jnp.float32)],
        compiler_params=pltpu.CompilerParams(vmem_limit_bytes=16 * 2**20),
        name="state",
    )(near(prior))
    analysis = pl.pallas_call(
        functools.partial(finish_kernel, members, owned, mem_count),
        out_shape=pltpu.VMEM((members * extra, LANES), jnp.bfloat16),
        in_specs=[vmem, vmem, vmem],
        out_specs=vmem,
        scratch_shapes=[pltpu.VMEM((members * extra, LANES), jnp.float32)],
        compiler_params=pltpu.CompilerParams(vmem_limit_bytes=16 * 2**20),
        name="finish",
    )(near(swapped), near(deviation), near(mean))
    analysis = analysis.reshape(mem_count, local, extra, LANES)
    analysis = lax.all_to_all(analysis, "mem", split_axis=0, concat_axis=0, tiled=True)
    return pl.pallas_call(
        functools.partial(unpack_kernel, owned),
        out_shape=jax.ShapeDtypeStruct(ens_state.shape, jnp.bfloat16),
        in_specs=[vmem],
        out_specs=vmem,
        compiler_params=pltpu.CompilerParams(vmem_limit_bytes=16 * 2**20),
        name="unpack",
    )(near(analysis))


def solution(mesh):
    placed = (
        P("mem", "grid", None),
        P("mem", "grid", None),
        P("grid", None),
        P("grid", None),
        P("grid"),
        P("grid", None),
        P("grid", None),
    )
    return jax.shard_map(
        per_device, mesh=mesh, in_specs=placed, out_specs=P("mem", "grid", None), check_vma=False
    )
```

```python
import functools
import math

import jax
import jax.numpy as jnp
from jax import lax
from jax.experimental import pallas as pl
from jax.experimental.pallas import tpu as pltpu
from jax.sharding import PartitionSpec as P

NSIT = 3
LOCR = 8
LANES = 128
COUNT = 127
UNIT = 4
TURN = 18
ROOM = 256
SPAN = 16

inflation = 1.1


def swap(value, crossing):
    mem_count = lax.axis_size("mem")
    grid_count = lax.axis_size("grid")
    pairs = []
    for m in range(mem_count):
        for g in range(grid_count):
            if crossing:
                other = m ^ 1, (g + 1 if g % 2 else g - 1) % grid_count
            else:
                other = m, g ^ 1
            pairs.append((m * grid_count + g, other[0] * grid_count + other[1]))
    return lax.ppermute(value, ("mem", "grid"), pairs)


def pack_kernel(parts, size, owned, src_ref, state_all, out_ref, stage_ref, state_ref, rows_ref, sems, last):
    local = state_all.shape[0]
    pieces = state_all.shape[2] // LANES
    inward = [
        pltpu.make_async_copy(src_ref.at[:, m * size : (m + 1) * size, :], stage_ref.at[m], sems.at[0, m])
        for m in range(parts)
    ]
    outward = [
        pltpu.make_async_copy(stage_ref.at[m], out_ref.at[m, :, 0:size, :], sems.at[1, m])
        for m in range(parts)
    ]
    state_in = pltpu.make_async_copy(state_all, state_ref, last.at[0])
    state_out = pltpu.make_async_copy(rows_ref, out_ref.at[:, :, size:, :], last.at[1])
    state_in.start()
    for copy in inward:
        copy.start()
    state_in.wait()
    for i in range(local):
        value = state_ref[i].astype(jnp.float32)
        for m in range(parts):
            rows = value[m * owned : (m + 1) * owned]
            rows = jnp.concatenate(
                [rows[:, q * LANES : (q + 1) * LANES] for q in range(pieces)], axis=0
            )
            rows_ref[m, i] = rows.astype(rows_ref.dtype)
    for m in range(parts):
        inward[m].wait()
        outward[m].start()
    state_out.start()
    for copy in outward:
        copy.wait()
    state_out.wait()


def weight_kernel(nb_total, obs, len_ref, cross_ref, mid_ref, chip_ref, prec_all, pos_all, value_all, out_ref, aux_ref, list_ref, item_ref, prec_ref, pos_ref, table_ref, sems):
    place = lax.axis_index("mem")
    grid_pos = lax.axis_index("grid")
    grid_count = lax.axis_size("grid")
    obs_blocks = prec_all.shape[0]
    blocks_dev = mid_ref.shape[0]
    mine = pl.ds(pl.multiple_of(place * obs, 8), obs)
    copies = [
        pltpu.make_async_copy(prec_all.at[mine], prec_ref, sems.at[0]),
        pltpu.make_async_copy(pos_all.at[mine], pos_ref, sems.at[1]),
        pltpu.make_async_copy(value_all.at[mine], aux_ref.at[obs : 2 * obs], sems.at[2]),
    ]
    for copy in copies:
        copy.start()
    row = lax.broadcasted_iota(jnp.int32, (obs, LANES), 0)
    count = jnp.zeros((obs, LANES), jnp.int32)
    for o in range(obs):
        count = jnp.where(row == o, len_ref[place * obs + o], count)
    lane = lax.broadcasted_iota(jnp.int32, (obs, LANES), 1)
    aux_ref[0:obs, :] = jnp.where(lane < count, 1.0, 0.0)
    base = grid_pos * obs_blocks + place * obs
    even = jnp.broadcast_to(lax.rem(grid_pos, 2), mid_ref.shape) == 0
    low = jnp.where(even, cross_ref[...], chip_ref[...])
    high = jnp.where(even, chip_ref[...], cross_ref[...])
    pairs = jnp.concatenate([low, mid_ref[...], high], axis=0) - base
    index = lax.broadcasted_iota(jnp.int32, (blocks_dev, LANES), 0)
    centers = jnp.concatenate(
        [
            index + lax.rem(grid_pos + grid_count + step, grid_count) * blocks_dev
            for step in (-1, 0, 1)
        ],
        axis=0,
    ).astype(jnp.float32) + 0.5
    for copy in copies:
        copy.wait()
    blocks = 3 * blocks_dev
    slot = lax.broadcasted_iota(jnp.int32, (blocks, LANES), 1)
    found = jnp.zeros((blocks, LANES), jnp.int32)
    chosen = jnp.full((blocks, LANES), obs, jnp.int32)
    for o in range(obs):
        hit = jnp.max(jnp.where(pairs == o, 1.0, 0.0), axis=1, keepdims=True)
        hit = jnp.broadcast_to(hit, (blocks, LANES)).astype(jnp.int32)
        chosen = jnp.where(slot == jnp.where(hit > 0, found, -1), o, chosen)
        found = found + hit
        gap = jnp.abs(pos_ref[o : o + 1, :] - centers)
        distance = jnp.minimum(gap, nb_total - gap)
        relative = distance * (1.0 / LOCR)
        weight = prec_ref[o : o + 1, :] * jnp.exp(-0.5 * relative * relative)
        out_ref[pl.ds(o, blocks, stride=obs), :] = weight
    out_ref[blocks * obs :, :] = jnp.zeros((out_ref.shape[0] - blocks * obs, LANES), jnp.float32)
    table_ref[0:blocks] = jnp.where(slot == COUNT, found, chosen)
    table_ref[blocks:] = jnp.full((table_ref.shape[0] - blocks, LANES), obs, jnp.int32)
    copy = pltpu.make_async_copy(table_ref, list_ref, sems.at[3])
    copy.start()
    copy.wait()
    most = -(-obs // UNIT)
    for group in range(3):
        at = 0
        for b in range(group * blocks_dev, (group + 1) * blocks_dev):
            for k in range(most):
                item_ref[group, at + k] = b * SPAN + k
            at = at + lax.shift_right_logical(list_ref[b, COUNT] + UNIT - 1, 2)
        for k in range(TURN):
            item_ref[group, at + k] = (group + 1) * blocks_dev * SPAN + most
        item_ref[group, ROOM - 1] = at


def accumulate(members, obs, group, blocks, list_ref, item_ref, d_ref, w_ref, acc_ref):
    rows = d_ref.shape[1]
    acc_ref[...] = jnp.zeros(acc_ref.shape, jnp.float32)

    def step(turn, carry):
        for u in range(TURN):
            item = item_ref[group, turn * TURN + u]
            b = lax.shift_right_logical(item, 4)
            first = lax.bitwise_and(item, SPAN - 1) * UNIT
            full, scaled = [], []
            for k in range(UNIT):
                o = list_ref[b, first + k]
                d = d_ref[o]
                row = w_ref[pl.ds(b * obs + o, 1), :]
                w = jnp.broadcast_to(row, (16, LANES)).astype(jnp.bfloat16)
                full.append(d)
                scaled.append((d[:members].reshape(members // 16, 16, LANES) * w[None]).reshape(members, LANES))
            at = pl.multiple_of((b - group * blocks) * members, 16)
            acc_ref[pl.ds(at, members), 0:rows] += lax.dot_general(
                jnp.concatenate(scaled, axis=1),
                jnp.concatenate(full, axis=1),
                (((1,), (1,)), ((), ())),
                preferred_element_type=jnp.float32,
            )
        return carry

    lax.fori_loop(0, (item_ref[group, ROOM - 1] + TURN - 1) // TURN, step, 0)


def packed_system(members, blocks, acc_ref, out_ref):
    half = members // 2
    lane = lax.broadcasted_iota(jnp.int32, (half, LANES), 1)
    for b in range(blocks):
        top = acc_ref[b * members : b * members + half, :]
        bottom = acc_ref[b * members + half : (b + 1) * members, :]
        corner = pltpu.roll(bottom, LANES - members, 1)
        force = pltpu.roll(bottom, 2, 1)
        value = jnp.where(lane >= members + 2, force, top)
        value = jnp.where(lane >= LANES - half, corner, value)
        out_ref[b * half : (b + 1) * half, :] = value.astype(out_ref.dtype)


def cross_kernel(members, obs, blocks, list_ref, item_ref, prior_ref, aux_ref, w_ref, d_ref, out_ref, dev_ref, acc_ref):
    rows = d_ref.shape[1]
    total = prior_ref[0, 0:obs].astype(jnp.float32)
    for i in range(1, members):
        total = total + prior_ref[i, 0:obs].astype(jnp.float32)
    mean = total / members
    valid = aux_ref[0:obs, :] > 0.0
    for i in range(members):
        dev_ref[i * obs : (i + 1) * obs, :] = jnp.where(
            valid, prior_ref[i, 0:obs].astype(jnp.float32) - mean, 0.0
        )
    departure = jnp.where(valid, aux_ref[obs : 2 * obs, :] - mean, 0.0)
    high = departure.astype(jnp.bfloat16).astype(jnp.float32)
    dev_ref[members * obs : (members + 1) * obs, :] = high
    dev_ref[(members + 1) * obs : (members + 2) * obs, :] = departure - high
    dev_ref[(members + 2) * obs :, :] = jnp.zeros(((rows - members - 2) * obs, LANES), jnp.float32)
    for o in range(obs):
        d_ref[o] = dev_ref[pl.ds(o, rows, stride=obs), :].astype(jnp.bfloat16)
    d_ref[obs] = jnp.zeros((rows, LANES), jnp.bfloat16)
    group = 2 * lax.rem(lax.axis_index("grid"), 2)
    accumulate(members, obs, group, blocks, list_ref, item_ref, d_ref, w_ref, acc_ref)
    packed_system(members, blocks, acc_ref, out_ref)


def next_kernel(members, obs, own, blocks, list_ref, item_ref, d_ref, w_ref, out_ref, acc_ref):
    group = 1 if own else 2 - 2 * lax.rem(lax.axis_index("grid"), 2)
    accumulate(members, obs, group, blocks, list_ref, item_ref, d_ref, w_ref, acc_ref)
    packed_system(members, blocks, acc_ref, out_ref)


def state_kernel(members, part_ref, dev_ref, mean_ref, wide_ref):
    rows = mean_ref.shape[0]
    first = part_ref.shape[1] - rows
    total = part_ref[0, first:].astype(jnp.float32)
    for i in range(1, members):
        total = total + part_ref[i, first:].astype(jnp.float32)
    mean = total / members
    mean_ref[...] = mean
    for i in range(members):
        wide_ref[i * rows : (i + 1) * rows, :] = part_ref[i, first:].astype(jnp.float32) - mean
    for k in range(rows):
        dev_ref[:, k * LANES : (k + 1) * LANES] = wide_ref[pl.ds(k, members, stride=rows), :].astype(jnp.bfloat16)


def merge_kernel(own_ref, low_ref, high_ref, out_ref):
    total = own_ref[...] + low_ref[...].astype(jnp.float32) + high_ref[...].astype(jnp.float32)
    out_ref[...] = total.astype(jnp.bfloat16)


def finish_kernel(members, owned, parts, system_ref, dev_ref, mean_ref, out_ref, wide_ref):
    half = members // 2
    rows_out = mean_ref.shape[0]
    total = system_ref[0].astype(jnp.float32)
    for m in range(1, parts):
        total = total + system_ref[m].astype(jnp.float32)
    rows = lax.broadcasted_iota(jnp.int32, (members, members), 0)
    cols = lax.broadcasted_iota(jnp.int32, (members, members), 1)
    identity = jnp.where(rows == cols, 1.0, 0.0)
    lane = lax.broadcasted_iota(jnp.int32, (half, LANES), 1)

    def split(value):
        top = value.astype(jnp.bfloat16)
        return top, (value - top.astype(jnp.float32)).astype(jnp.bfloat16)

    def dot(a, b):
        (a_top, a_low), (b_top, b_low) = split(a), split(b)

        def one(x, y):
            return jnp.dot(x, y, preferred_element_type=jnp.float32)

        return one(a_top, b_top) + (one(a_top, b_low) + one(a_low, b_top))

    y_iter, z_iter, bound, force = [], [], [], []
    for r in range(owned):
        part = total[r * half : (r + 1) * half]
        square = jnp.concatenate([part, jnp.zeros((LANES - half, LANES), jnp.float32)], axis=0)
        below = jnp.transpose(square)[half : 2 * half]
        right = pltpu.roll(part, members, 1)
        bottom = jnp.where(lane < half, below, right)
        system = jnp.concatenate([part, bottom], axis=0)[:, :members]
        system = system + (members - 1) / inflation * identity
        sums = jnp.sum(jnp.abs(system), axis=1, keepdims=True)
        bound.append(jnp.max(sums, axis=0, keepdims=True))
        y_iter.append(system / bound[r])
        f_top = part[:, members : members + 1] + part[:, members + 1 : members + 2]
        f_low = part[:, members + 2 : members + 3] + part[:, members + 3 : members + 4]
        force.append(jnp.concatenate([f_top, f_low], axis=0))
    for sweep in range(NSIT):
        if sweep == 0:
            factor = [1.5 * identity - 0.5 * y for y in y_iter]
            z_next = factor
        else:
            factor = [1.5 * identity - 0.5 * dot(z, y) for z, y in zip(z_iter, y_iter)]
            z_next = [dot(f, z) for f, z in zip(factor, z_iter)]
        if sweep + 1 < NSIT:
            y_iter = [dot(y, f) for y, f in zip(y_iter, factor)]
        z_iter = z_next
    for r in range(owned):
        root = z_iter[r] / jnp.sqrt(bound[r])
        first = dot(root, jnp.broadcast_to(force[r], (members, LANES)))
        shiftu = dot(root, first)[:, :1]
        transform = math.sqrt(members - 1) * root + shiftu
        turned = jnp.transpose(transform).astype(jnp.bfloat16)
        for k in range(r, rows_out, owned):
            moved = jnp.dot(
                turned, dev_ref[:, k * LANES : (k + 1) * LANES], preferred_element_type=jnp.float32
            )
            wide_ref[pl.ds(k, members, stride=rows_out), :] = mean_ref[k : k + 1, :] + moved
    out_ref[...] = wide_ref[...].astype(jnp.bfloat16)


def unpack_kernel(owned, part_ref, out_ref):
    parts, local, rows, _ = part_ref.shape
    for i in range(local):
        groups = []
        for m in range(parts):
            value = part_ref[m, i].astype(jnp.float32)
            groups.append(
                jnp.concatenate([value[k : k + owned] for k in range(0, rows, owned)], axis=1)
            )
        out_ref[i] = jnp.concatenate(groups, axis=0).astype(out_ref.dtype)


def per_device(ens_state, obs_prior, obs_value, obs_prec, obs_len, pair_block, obs_pos):
    mem_count = lax.axis_size("mem")
    grid_count = lax.axis_size("grid")
    local = ens_state.shape[0]
    members = mem_count * local
    blocks_dev = ens_state.shape[1]
    obs_blocks = obs_prior.shape[1]
    owned = blocks_dev // mem_count
    obs = obs_blocks // mem_count
    half = members // 2
    nb_total = blocks_dev * grid_count
    vmem = pl.BlockSpec(memory_space=pltpu.VMEM)
    anywhere = pl.BlockSpec(memory_space=pl.ANY)
    scalars = pl.BlockSpec(memory_space=pltpu.SMEM)

    pieces = ens_state.shape[2] // LANES

    def near(value):
        return pltpu.with_memory_space_constraint(value, pltpu.VMEM)

    extra = pieces * owned

    def scalar(value):
        return pltpu.with_memory_space_constraint(value, pltpu.SMEM)

    def far(value):
        return pltpu.with_memory_space_constraint(value, pltpu.HBM)

    packed = pl.pallas_call(
        functools.partial(pack_kernel, mem_count, obs, owned),
        out_shape=jax.ShapeDtypeStruct((mem_count, local, obs + extra, LANES), obs_prior.dtype),
        in_specs=[pl.BlockSpec(memory_space=pltpu.HBM), pl.BlockSpec(memory_space=pltpu.HBM)],
        out_specs=pl.BlockSpec(memory_space=pltpu.HBM),
        scratch_shapes=[
            pltpu.VMEM((mem_count, local, obs, LANES), obs_prior.dtype),
            pltpu.VMEM(ens_state.shape, ens_state.dtype),
            pltpu.VMEM((mem_count, local, extra, LANES), ens_state.dtype),
            pltpu.SemaphoreType.DMA((2, mem_count)),
            pltpu.SemaphoreType.DMA((2,)),
        ],
        compiler_params=pltpu.CompilerParams(vmem_limit_bytes=16 * 2**20),
        name="pack",
    )(far(obs_prior), far(ens_state))
    prior = lax.all_to_all(packed, "mem", split_axis=0, concat_axis=0, tiled=True)
    prior = prior.reshape(members, obs + extra, LANES)
    pairs_cross = swap(pair_block, True)
    pairs_chip = swap(pair_block, False)

    blocks = 3 * blocks_dev
    weights, aux, lists, items = pl.pallas_call(
        functools.partial(weight_kernel, float(nb_total), obs),
        out_shape=(
            pltpu.VMEM(((blocks + 1) * obs + 8, LANES), jnp.float32),
            pltpu.VMEM((2 * obs, LANES), jnp.float32),
            pltpu.SMEM((blocks + 8, LANES), jnp.int32),
            pltpu.SMEM((3, ROOM), jnp.int32),
        ),
        in_specs=[pl.BlockSpec(memory_space=pltpu.SMEM), vmem, vmem, vmem, anywhere, anywhere, anywhere],
        out_specs=(vmem, vmem, scalars, scalars),
        scratch_shapes=[
            pltpu.VMEM((obs, LANES), jnp.float32),
            pltpu.VMEM((obs, LANES), jnp.float32),
            pltpu.VMEM((blocks + 8, LANES), jnp.int32),
            pltpu.SemaphoreType.DMA((4,)),
        ],
        compiler_params=pltpu.CompilerParams(vmem_limit_bytes=16 * 2**20),
        name="weights",
    )(obs_len, near(pairs_cross), pair_block, near(pairs_chip), obs_prec, obs_pos, obs_value)

    rows = -(-(members + 2) // 16) * 16
    system = pltpu.VMEM((blocks_dev * half, LANES), jnp.bfloat16)
    d_all, to_cross = pl.pallas_call(
        functools.partial(cross_kernel, members, obs, blocks_dev),
        out_shape=(pltpu.VMEM((obs + 1, rows, LANES), jnp.bfloat16), system),
        in_specs=[scalars, scalars, vmem, vmem, vmem],
        out_specs=(vmem, vmem),
        scratch_shapes=[
            pltpu.VMEM((rows * obs, LANES), jnp.float32),
            pltpu.VMEM(((blocks_dev + 1) * members, LANES), jnp.float32),
        ],
        compiler_params=pltpu.CompilerParams(vmem_limit_bytes=16 * 2**20),
        name="cross",
    )(scalar(lists), scalar(items), near(prior), near(aux), near(weights))
    from_cross = swap(to_cross, True)

    def later(own, dtype):
        return pl.pallas_call(
            functools.partial(next_kernel, members, obs, own, blocks_dev),
            out_shape=pltpu.VMEM((blocks_dev * half, LANES), dtype),
            in_specs=[scalars, scalars, vmem, vmem],
            out_specs=vmem,
            scratch_shapes=[pltpu.VMEM(((blocks_dev + 1) * members, LANES), jnp.float32)],
            compiler_params=pltpu.CompilerParams(vmem_limit_bytes=16 * 2**20),
        )(scalar(lists), scalar(items), near(d_all), near(weights))

    to_chip = later(False, jnp.bfloat16)
    from_chip = swap(to_chip, False)
    own = later(True, jnp.float32)
    partial = pl.pallas_call(
        merge_kernel,
        out_shape=pltpu.VMEM((blocks_dev * half, LANES), jnp.bfloat16),
        in_specs=[vmem, vmem, vmem],
        out_specs=vmem,
        compiler_params=pltpu.CompilerParams(vmem_limit_bytes=16 * 2**20),
        name="merge",
    )(near(own), near(from_cross), near(from_chip))
    partial = partial.reshape(mem_count, owned * half, LANES)
    swapped = lax.all_to_all(partial, "mem", split_axis=0, concat_axis=0, tiled=True)
    deviation, mean = pl.pallas_call(
        functools.partial(state_kernel, members),
        out_shape=(
            pltpu.VMEM((members, extra * LANES), jnp.bfloat16),
            pltpu.VMEM((extra, LANES), jnp.float32),
        ),
        in_specs=[vmem],
        out_specs=(vmem, vmem),
        scratch_shapes=[pltpu.VMEM((members * extra, LANES), jnp.float32)],
        compiler_params=pltpu.CompilerParams(vmem_limit_bytes=16 * 2**20),
        name="state",
    )(near(prior))
    analysis = pl.pallas_call(
        functools.partial(finish_kernel, members, owned, mem_count),
        out_shape=pltpu.VMEM((members * extra, LANES), jnp.bfloat16),
        in_specs=[vmem, vmem, vmem],
        out_specs=vmem,
        scratch_shapes=[pltpu.VMEM((members * extra, LANES), jnp.float32)],
        compiler_params=pltpu.CompilerParams(vmem_limit_bytes=16 * 2**20),
        name="finish",
    )(near(swapped), near(deviation), near(mean))
    analysis = analysis.reshape(mem_count, local, extra, LANES)
    analysis = lax.all_to_all(analysis, "mem", split_axis=0, concat_axis=0, tiled=True)
    return pl.pallas_call(
        functools.partial(unpack_kernel, owned),
        out_shape=jax.ShapeDtypeStruct(ens_state.shape, jnp.bfloat16),
        in_specs=[vmem],
        out_specs=vmem,
        compiler_params=pltpu.CompilerParams(vmem_limit_bytes=16 * 2**20),
        name="unpack",
    )(near(analysis))


def solution(mesh):
    placed = (
        P("mem", "grid", None),
        P("mem", "grid", None),
        P("grid", None),
        P("grid", None),
        P("grid"),
        P("grid", None),
        P("grid", None),
    )
    return jax.shard_map(
        per_device, mesh=mesh, in_specs=placed, out_specs=P("mem", "grid", None), check_vma=False
    )
```

```python
import functools
import math

import jax
import jax.numpy as jnp
from jax import lax
from jax.experimental import pallas as pl
from jax.experimental.pallas import tpu as pltpu
from jax.sharding import PartitionSpec as P

NSIT = 3
LOCR = 8
LANES = 128
COUNT = 127
UNIT = 4
TURN = 28
ROOM = 256
SPAN = 16
PITCH = 49

inflation = 1.1


def swap(value, crossing):
    mem_count = lax.axis_size("mem")
    grid_count = lax.axis_size("grid")
    pairs = []
    for m in range(mem_count):
        for g in range(grid_count):
            if crossing:
                other = m ^ 1, (g + 1 if g % 2 else g - 1) % grid_count
            else:
                other = m, g ^ 1
            pairs.append((m * grid_count + g, other[0] * grid_count + other[1]))
    return lax.ppermute(value, ("mem", "grid"), pairs)


def pack_kernel(parts, size, owned, src_ref, state_all, out_ref, stage_ref, state_ref, rows_ref, sems, last):
    local = state_all.shape[0]
    pieces = state_all.shape[2] // LANES
    inward = [
        pltpu.make_async_copy(src_ref.at[:, m * size : (m + 1) * size, :], stage_ref.at[m], sems.at[0, m])
        for m in range(parts)
    ]
    outward = [
        pltpu.make_async_copy(stage_ref.at[m], out_ref.at[m, :, 0:size, :], sems.at[1, m])
        for m in range(parts)
    ]
    state_in = pltpu.make_async_copy(state_all, state_ref, last.at[0])
    state_out = pltpu.make_async_copy(rows_ref, out_ref.at[:, :, size:, :], last.at[1])
    state_in.start()
    for copy in inward:
        copy.start()
    state_in.wait()
    for i in range(local):
        value = state_ref[i].astype(jnp.float32)
        for m in range(parts):
            rows = value[m * owned : (m + 1) * owned]
            rows = jnp.concatenate(
                [rows[:, q * LANES : (q + 1) * LANES] for q in range(pieces)], axis=0
            )
            rows_ref[m, i] = rows.astype(rows_ref.dtype)
    for m in range(parts):
        inward[m].wait()
        outward[m].start()
    state_out.start()
    for copy in outward:
        copy.wait()
    state_out.wait()


def weight_kernel(nb_total, obs, len_ref, cross_ref, mid_ref, chip_ref, prec_all, pos_all, value_all, out_ref, aux_ref, list_ref, item_ref, prec_ref, pos_ref, table_ref, sems):
    place = lax.axis_index("mem")
    grid_pos = lax.axis_index("grid")
    grid_count = lax.axis_size("grid")
    obs_blocks = prec_all.shape[0]
    blocks_dev = mid_ref.shape[0]
    mine = pl.ds(pl.multiple_of(place * obs, 8), obs)
    copies = [
        pltpu.make_async_copy(prec_all.at[mine], prec_ref, sems.at[0]),
        pltpu.make_async_copy(pos_all.at[mine], pos_ref, sems.at[1]),
        pltpu.make_async_copy(value_all.at[mine], aux_ref.at[obs : 2 * obs], sems.at[2]),
    ]
    for copy in copies:
        copy.start()
    row = lax.broadcasted_iota(jnp.int32, (obs, LANES), 0)
    count = jnp.zeros((obs, LANES), jnp.int32)
    for o in range(obs):
        count = jnp.where(row == o, len_ref[place * obs + o], count)
    lane = lax.broadcasted_iota(jnp.int32, (obs, LANES), 1)
    aux_ref[0:obs, :] = jnp.where(lane < count, 1.0, 0.0)
    base = grid_pos * obs_blocks + place * obs
    even = jnp.broadcast_to(lax.rem(grid_pos, 2), mid_ref.shape) == 0
    low = jnp.where(even, cross_ref[...], chip_ref[...])
    high = jnp.where(even, chip_ref[...], cross_ref[...])
    pairs = jnp.concatenate([low, mid_ref[...], high], axis=0) - base
    index = lax.broadcasted_iota(jnp.int32, (blocks_dev, LANES), 0)
    centers = jnp.concatenate(
        [
            index + lax.rem(grid_pos + grid_count + step, grid_count) * blocks_dev
            for step in (-1, 0, 1)
        ],
        axis=0,
    ).astype(jnp.float32) + 0.5
    for copy in copies:
        copy.wait()
    blocks = 3 * blocks_dev
    slot = lax.broadcasted_iota(jnp.int32, (blocks, LANES), 1)
    found = jnp.zeros((blocks, LANES), jnp.int32)
    chosen = jnp.full((blocks, LANES), obs, jnp.int32)
    for o in range(obs):
        hit = jnp.max(jnp.where(pairs == o, 1.0, 0.0), axis=1, keepdims=True)
        hit = jnp.broadcast_to(hit, (blocks, LANES)).astype(jnp.int32)
        chosen = jnp.where(slot == jnp.where(hit > 0, found, -1), o, chosen)
        found = found + hit
        gap = jnp.abs(pos_ref[o : o + 1, :] - centers)
        distance = jnp.minimum(gap, nb_total - gap)
        relative = distance * (1.0 / LOCR)
        weight = prec_ref[o : o + 1, :] * jnp.exp(-0.5 * relative * relative)
        out_ref[pl.ds(o, blocks, stride=obs), :] = weight
    out_ref[blocks * obs :, :] = jnp.zeros((out_ref.shape[0] - blocks * obs, LANES), jnp.float32)
    table_ref[0:blocks] = jnp.where(slot == COUNT, found, chosen)
    table_ref[blocks:] = jnp.full((table_ref.shape[0] - blocks, LANES), obs, jnp.int32)
    copy = pltpu.make_async_copy(table_ref, list_ref, sems.at[3])
    copy.start()
    copy.wait()
    most = -(-obs // UNIT)
    for group in range(3):
        at = 0
        for b in range(group * blocks_dev, (group + 1) * blocks_dev):
            for k in range(most):
                item_ref[group, at + k] = b * SPAN + k
            at = at + lax.shift_right_logical(list_ref[b, COUNT] + UNIT - 1, 2)
        for k in range(TURN):
            item_ref[group, at + k] = (group + 1) * blocks_dev * SPAN + most
        item_ref[group, ROOM - 1] = at


def accumulate(members, obs, group, blocks, list_ref, item_ref, d_ref, w_ref, acc_ref):
    rows = d_ref.shape[1]
    acc_ref[...] = jnp.zeros(acc_ref.shape, jnp.float32)

    def step(turn, carry):
        for u in range(TURN):
            item = item_ref[group, turn * TURN + u]
            b = lax.shift_right_logical(item, 4)
            first = lax.bitwise_and(item, SPAN - 1) * UNIT
            full, scaled = [], []
            for k in range(UNIT):
                o = list_ref[b, first + k]
                d = d_ref[o]
                row = w_ref[pl.ds(b * obs + o, 1), :]
                w = jnp.broadcast_to(row, (16, LANES)).astype(jnp.bfloat16)
                full.append(d)
                scaled.append((d[:members].reshape(members // 16, 16, LANES) * w[None]).reshape(members, LANES))
            at = pl.multiple_of((b - group * blocks) * members, 16)
            acc_ref[pl.ds(at, members), 0:rows] += lax.dot_general(
                jnp.concatenate(scaled, axis=1),
                jnp.concatenate(full, axis=1),
                (((1,), (1,)), ((), ())),
                preferred_element_type=jnp.float32,
            )
        return carry

    lax.fori_loop(0, (item_ref[group, ROOM - 1] + TURN - 1) // TURN, step, 0)


def packed_system(members, blocks, acc_ref, out_ref):
    half = members // 2
    lane = lax.broadcasted_iota(jnp.int32, (half, LANES), 1)
    for b in range(blocks):
        top = acc_ref[b * members : b * members + half, :]
        bottom = acc_ref[b * members + half : (b + 1) * members, :]
        corner = pltpu.roll(bottom, LANES - members, 1)
        force = pltpu.roll(bottom, 2, 1)
        value = jnp.where(lane >= members + 2, force, top)
        value = jnp.where(lane >= LANES - half, corner, value)
        out_ref[b * half : (b + 1) * half, :] = value.astype(out_ref.dtype)


def cross_kernel(members, obs, blocks, list_ref, item_ref, prior_ref, aux_ref, w_ref, d_ref, out_ref, dev_ref, acc_ref):
    rows = d_ref.shape[1]
    total = prior_ref[0, 0:obs].astype(jnp.float32)
    for i in range(1, members):
        total = total + prior_ref[i, 0:obs].astype(jnp.float32)
    mean = total / members
    valid = aux_ref[0:obs, :] > 0.0
    for i in range(members):
        dev_ref[i * PITCH : i * PITCH + obs, :] = jnp.where(
            valid, prior_ref[i, 0:obs].astype(jnp.float32) - mean, 0.0
        )
    departure = jnp.where(valid, aux_ref[obs : 2 * obs, :] - mean, 0.0)
    high = departure.astype(jnp.bfloat16).astype(jnp.float32)
    dev_ref[members * PITCH : members * PITCH + obs, :] = high
    dev_ref[(members + 1) * PITCH : (members + 1) * PITCH + obs, :] = departure - high
    dev_ref[(members + 2) * PITCH :, :] = jnp.zeros(((rows - members - 2) * PITCH, LANES), jnp.float32)
    for o in range(obs):
        d_ref[o] = dev_ref[pl.ds(o, rows, stride=PITCH), :].astype(jnp.bfloat16)
    d_ref[obs] = jnp.zeros((rows, LANES), jnp.bfloat16)
    group = 2 * lax.rem(lax.axis_index("grid"), 2)
    accumulate(members, obs, group, blocks, list_ref, item_ref, d_ref, w_ref, acc_ref)
    packed_system(members, blocks, acc_ref, out_ref)


def next_kernel(members, obs, own, blocks, list_ref, item_ref, d_ref, w_ref, out_ref, acc_ref):
    group = 1 if own else 2 - 2 * lax.rem(lax.axis_index("grid"), 2)
    accumulate(members, obs, group, blocks, list_ref, item_ref, d_ref, w_ref, acc_ref)
    packed_system(members, blocks, acc_ref, out_ref)


def state_kernel(members, part_ref, dev_ref, mean_ref, wide_ref):
    rows = mean_ref.shape[0]
    first = part_ref.shape[1] - rows
    total = part_ref[0, first:].astype(jnp.float32)
    for i in range(1, members):
        total = total + part_ref[i, first:].astype(jnp.float32)
    mean = total / members
    mean_ref[...] = mean
    for i in range(members):
        wide_ref[i * rows : (i + 1) * rows, :] = part_ref[i, first:].astype(jnp.float32) - mean
    for k in range(rows):
        dev_ref[:, k * LANES : (k + 1) * LANES] = wide_ref[pl.ds(k, members, stride=rows), :].astype(jnp.bfloat16)


def merge_kernel(own_ref, low_ref, high_ref, out_ref):
    total = own_ref[...] + low_ref[...].astype(jnp.float32) + high_ref[...].astype(jnp.float32)
    out_ref[...] = total.astype(jnp.bfloat16)


def finish_kernel(members, owned, parts, system_ref, dev_ref, mean_ref, out_ref, wide_ref):
    half = members // 2
    rows_out = mean_ref.shape[0]
    total = system_ref[0].astype(jnp.float32)
    for m in range(1, parts):
        total = total + system_ref[m].astype(jnp.float32)
    rows = lax.broadcasted_iota(jnp.int32, (members, members), 0)
    cols = lax.broadcasted_iota(jnp.int32, (members, members), 1)
    identity = jnp.where(rows == cols, 1.0, 0.0)
    lane = lax.broadcasted_iota(jnp.int32, (half, LANES), 1)

    def split(value):
        top = value.astype(jnp.bfloat16)
        return top, (value - top.astype(jnp.float32)).astype(jnp.bfloat16)

    def dot(a, b):
        (a_top, a_low), (b_top, b_low) = split(a), split(b)

        def one(x, y):
            return jnp.dot(x, y, preferred_element_type=jnp.float32)

        return one(a_top, b_top) + (one(a_top, b_low) + one(a_low, b_top))

    y_iter, z_iter, bound, force = [], [], [], []
    for r in range(owned):
        part = total[r * half : (r + 1) * half]
        square = jnp.concatenate([part, jnp.zeros((LANES - half, LANES), jnp.float32)], axis=0)
        below = jnp.transpose(square)[half : 2 * half]
        right = pltpu.roll(part, members, 1)
        bottom = jnp.where(lane < half, below, right)
        system = jnp.concatenate([part, bottom], axis=0)[:, :members]
        system = system + (members - 1) / inflation * identity
        sums = jnp.sum(jnp.abs(system), axis=1, keepdims=True)
        bound.append(jnp.max(sums, axis=0, keepdims=True))
        y_iter.append(system / bound[r])
        turned = jnp.transpose(square)
        sums_hl = turned[members : members + 8] + pltpu.roll(turned[members : members + 8], 7, 0)
        low = jnp.broadcast_to(sums_hl[2:3], (8, LANES))
        row = jnp.broadcast_to(sums_hl[0:1], (8, LANES))
        lane8 = lax.broadcasted_iota(jnp.int32, (8, LANES), 1)
        row = jnp.where(lane8 < half, row, pltpu.roll(low, half, 1))
        force.append(row[:, :members])
    for sweep in range(NSIT):
        if sweep == 0:
            factor = [1.5 * identity - 0.5 * y for y in y_iter]
            z_next = factor
        else:
            factor = [1.5 * identity - 0.5 * dot(z, y) for z, y in zip(z_iter, y_iter)]
            z_next = [dot(f, z) for f, z in zip(factor, z_iter)]
        if sweep + 1 < NSIT:
            y_iter = [dot(y, f) for y, f in zip(y_iter, factor)]
        else:
            before = [dot(row, z) for row, z in zip(force, z_iter)]
            before = [dot(row, f) for row, f in zip(before, factor)]
        z_iter = z_next
    for r in range(owned):
        weight = dot(before[r], z_iter[r])[0:1] / bound[r]
        turned = math.sqrt(members - 1) * (z_iter[r] / jnp.sqrt(bound[r])) + weight
        turned = turned.astype(jnp.bfloat16)
        for k in range(r, rows_out, owned):
            moved = jnp.dot(
                turned, dev_ref[:, k * LANES : (k + 1) * LANES], preferred_element_type=jnp.float32
            )
            wide_ref[pl.ds(k, members, stride=rows_out), :] = mean_ref[k : k + 1, :] + moved
    out_ref[...] = wide_ref[...].astype(jnp.bfloat16)


def unpack_kernel(owned, part_ref, out_ref):
    parts, local, rows, _ = part_ref.shape
    for i in range(local):
        groups = []
        for m in range(parts):
            value = part_ref[m, i].astype(jnp.float32)
            groups.append(
                jnp.concatenate([value[k : k + owned] for k in range(0, rows, owned)], axis=1)
            )
        out_ref[i] = jnp.concatenate(groups, axis=0).astype(out_ref.dtype)


def per_device(ens_state, obs_prior, obs_value, obs_prec, obs_len, pair_block, obs_pos):
    mem_count = lax.axis_size("mem")
    grid_count = lax.axis_size("grid")
    local = ens_state.shape[0]
    members = mem_count * local
    blocks_dev = ens_state.shape[1]
    obs_blocks = obs_prior.shape[1]
    owned = blocks_dev // mem_count
    obs = obs_blocks // mem_count
    half = members // 2
    nb_total = blocks_dev * grid_count
    vmem = pl.BlockSpec(memory_space=pltpu.VMEM)
    anywhere = pl.BlockSpec(memory_space=pl.ANY)
    scalars = pl.BlockSpec(memory_space=pltpu.SMEM)

    pieces = ens_state.shape[2] // LANES

    def near(value):
        return pltpu.with_memory_space_constraint(value, pltpu.VMEM)

    extra = pieces * owned

    def scalar(value):
        return pltpu.with_memory_space_constraint(value, pltpu.SMEM)

    def far(value):
        return pltpu.with_memory_space_constraint(value, pltpu.HBM)

    packed = pl.pallas_call(
        functools.partial(pack_kernel, mem_count, obs, owned),
        out_shape=jax.ShapeDtypeStruct((mem_count, local, obs + extra, LANES), obs_prior.dtype),
        in_specs=[pl.BlockSpec(memory_space=pltpu.HBM), pl.BlockSpec(memory_space=pltpu.HBM)],
        out_specs=pl.BlockSpec(memory_space=pltpu.HBM),
        scratch_shapes=[
            pltpu.VMEM((mem_count, local, obs, LANES), obs_prior.dtype),
            pltpu.VMEM(ens_state.shape, ens_state.dtype),
            pltpu.VMEM((mem_count, local, extra, LANES), ens_state.dtype),
            pltpu.SemaphoreType.DMA((2, mem_count)),
            pltpu.SemaphoreType.DMA((2,)),
        ],
        compiler_params=pltpu.CompilerParams(vmem_limit_bytes=16 * 2**20),
        name="pack",
    )(far(obs_prior), far(ens_state))
    prior = lax.all_to_all(packed, "mem", split_axis=0, concat_axis=0, tiled=True)
    prior = prior.reshape(members, obs + extra, LANES)
    pairs_cross = swap(pair_block, True)
    pairs_chip = swap(pair_block, False)

    blocks = 3 * blocks_dev
    weights, aux, lists, items = pl.pallas_call(
        functools.partial(weight_kernel, float(nb_total), obs),
        out_shape=(
            pltpu.VMEM(((blocks + 1) * obs + 8, LANES), jnp.float32),
            pltpu.VMEM((2 * obs, LANES), jnp.float32),
            pltpu.SMEM((blocks + 8, LANES), jnp.int32),
            pltpu.SMEM((3, ROOM), jnp.int32),
        ),
        in_specs=[pl.BlockSpec(memory_space=pltpu.SMEM), vmem, vmem, vmem, anywhere, anywhere, anywhere],
        out_specs=(vmem, vmem, scalars, scalars),
        scratch_shapes=[
            pltpu.VMEM((obs, LANES), jnp.float32),
            pltpu.VMEM((obs, LANES), jnp.float32),
            pltpu.VMEM((blocks + 8, LANES), jnp.int32),
            pltpu.SemaphoreType.DMA((4,)),
        ],
        compiler_params=pltpu.CompilerParams(vmem_limit_bytes=16 * 2**20),
        name="weights",
    )(obs_len, near(pairs_cross), pair_block, near(pairs_chip), obs_prec, obs_pos, obs_value)

    rows = -(-(members + 2) // 16) * 16
    system = pltpu.VMEM((blocks_dev * half, LANES), jnp.bfloat16)
    d_all, to_cross = pl.pallas_call(
        functools.partial(cross_kernel, members, obs, blocks_dev),
        out_shape=(pltpu.VMEM((obs + 1, rows, LANES), jnp.bfloat16), system),
        in_specs=[scalars, scalars, vmem, vmem, vmem],
        out_specs=(vmem, vmem),
        scratch_shapes=[
            pltpu.VMEM((rows * PITCH, LANES), jnp.float32),
            pltpu.VMEM(((blocks_dev + 1) * members, LANES), jnp.float32),
        ],
        compiler_params=pltpu.CompilerParams(vmem_limit_bytes=16 * 2**20),
        name="cross",
    )(scalar(lists), scalar(items), near(prior), near(aux), near(weights))
    from_cross = swap(to_cross, True)

    def later(own, dtype):
        return pl.pallas_call(
            functools.partial(next_kernel, members, obs, own, blocks_dev),
            out_shape=pltpu.VMEM((blocks_dev * half, LANES), dtype),
            in_specs=[scalars, scalars, vmem, vmem],
            out_specs=vmem,
            scratch_shapes=[pltpu.VMEM(((blocks_dev + 1) * members, LANES), jnp.float32)],
            compiler_params=pltpu.CompilerParams(vmem_limit_bytes=16 * 2**20),
        )(scalar(lists), scalar(items), near(d_all), near(weights))

    to_chip = later(False, jnp.bfloat16)
    from_chip = swap(to_chip, False)
    own = later(True, jnp.float32)
    partial = pl.pallas_call(
        merge_kernel,
        out_shape=pltpu.VMEM((blocks_dev * half, LANES), jnp.bfloat16),
        in_specs=[vmem, vmem, vmem],
        out_specs=vmem,
        compiler_params=pltpu.CompilerParams(vmem_limit_bytes=16 * 2**20),
        name="merge",
    )(near(own), near(from_cross), near(from_chip))
    partial = partial.reshape(mem_count, owned * half, LANES)
    swapped = lax.all_to_all(partial, "mem", split_axis=0, concat_axis=0, tiled=True)
    deviation, mean = pl.pallas_call(
        functools.partial(state_kernel, members),
        out_shape=(
            pltpu.VMEM((members, extra * LANES), jnp.bfloat16),
            pltpu.VMEM((extra, LANES), jnp.float32),
        ),
        in_specs=[vmem],
        out_specs=(vmem, vmem),
        scratch_shapes=[pltpu.VMEM((members * extra, LANES), jnp.float32)],
        compiler_params=pltpu.CompilerParams(vmem_limit_bytes=16 * 2**20),
        name="state",
    )(near(prior))
    analysis = pl.pallas_call(
        functools.partial(finish_kernel, members, owned, mem_count),
        out_shape=pltpu.VMEM((members * extra, LANES), jnp.bfloat16),
        in_specs=[vmem, vmem, vmem],
        out_specs=vmem,
        scratch_shapes=[pltpu.VMEM((members * extra, LANES), jnp.float32)],
        compiler_params=pltpu.CompilerParams(vmem_limit_bytes=16 * 2**20),
        name="finish",
    )(near(swapped), near(deviation), near(mean))
    analysis = analysis.reshape(mem_count, local, extra, LANES)
    analysis = lax.all_to_all(analysis, "mem", split_axis=0, concat_axis=0, tiled=True)
    return pl.pallas_call(
        functools.partial(unpack_kernel, owned),
        out_shape=jax.ShapeDtypeStruct(ens_state.shape, jnp.bfloat16),
        in_specs=[vmem],
        out_specs=vmem,
        compiler_params=pltpu.CompilerParams(vmem_limit_bytes=16 * 2**20),
        name="unpack",
    )(near(analysis))


def solution(mesh):
    placed = (
        P("mem", "grid", None),
        P("mem", "grid", None),
        P("grid", None),
        P("grid", None),
        P("grid"),
        P("grid", None),
        P("grid", None),
    )
    return jax.shard_map(
        per_device, mesh=mesh, in_specs=placed, out_specs=P("mem", "grid", None), check_vma=False
    )
```

```python
import functools
import math

import jax
import jax.numpy as jnp
from jax import lax
from jax.experimental import pallas as pl
from jax.experimental.pallas import tpu as pltpu
from jax.sharding import PartitionSpec as P

NSIT = 3
LOCR = 8
LANES = 128
COUNT = 127
UNIT = 4
TURN = 28
ROOM = 256
SPAN = 16
PITCH = 49

inflation = 1.1


def swap(value, crossing):
    mem_count = lax.axis_size("mem")
    grid_count = lax.axis_size("grid")
    pairs = []
    for m in range(mem_count):
        for g in range(grid_count):
            if crossing:
                other = m ^ 1, (g + 1 if g % 2 else g - 1) % grid_count
            else:
                other = m, g ^ 1
            pairs.append((m * grid_count + g, other[0] * grid_count + other[1]))
    return lax.ppermute(value, ("mem", "grid"), pairs)


def pack_kernel(parts, size, owned, src_ref, state_all, out_ref, stage_ref, state_ref, rows_ref, sems, last):
    local = state_all.shape[0]
    pieces = state_all.shape[2] // LANES
    inward = [
        pltpu.make_async_copy(src_ref.at[:, m * size : (m + 1) * size, :], stage_ref.at[m], sems.at[0, m])
        for m in range(parts)
    ]
    outward = [
        pltpu.make_async_copy(stage_ref.at[m], out_ref.at[m, :, 0:size, :], sems.at[1, m])
        for m in range(parts)
    ]
    state_in = pltpu.make_async_copy(state_all, state_ref, last.at[0])
    state_out = pltpu.make_async_copy(rows_ref, out_ref.at[:, :, size:, :], last.at[1])
    state_in.start()
    for copy in inward:
        copy.start()
    state_in.wait()
    for i in range(local):
        value = state_ref[i].astype(jnp.float32)
        for m in range(parts):
            rows = value[m * owned : (m + 1) * owned]
            rows = jnp.concatenate(
                [rows[:, q * LANES : (q + 1) * LANES] for q in range(pieces)], axis=0
            )
            rows_ref[m, i] = rows.astype(rows_ref.dtype)
    for m in range(parts):
        inward[m].wait()
        outward[m].start()
    state_out.start()
    for copy in outward:
        copy.wait()
    state_out.wait()


def weight_kernel(nb_total, obs, len_ref, cross_ref, mid_ref, chip_ref, prec_all, pos_all, value_all, out_ref, aux_ref, list_ref, item_ref, prec_ref, pos_ref, table_ref, sems):
    place = lax.axis_index("mem")
    grid_pos = lax.axis_index("grid")
    grid_count = lax.axis_size("grid")
    obs_blocks = prec_all.shape[0]
    blocks_dev = mid_ref.shape[0]
    mine = pl.ds(pl.multiple_of(place * obs, 8), obs)
    copies = [
        pltpu.make_async_copy(prec_all.at[mine], prec_ref, sems.at[0]),
        pltpu.make_async_copy(pos_all.at[mine], pos_ref, sems.at[1]),
        pltpu.make_async_copy(value_all.at[mine], aux_ref.at[obs : 2 * obs], sems.at[2]),
    ]
    for copy in copies:
        copy.start()
    row = lax.broadcasted_iota(jnp.int32, (obs, LANES), 0)
    count = jnp.zeros((obs, LANES), jnp.int32)
    for o in range(obs):
        count = jnp.where(row == o, len_ref[place * obs + o], count)
    lane = lax.broadcasted_iota(jnp.int32, (obs, LANES), 1)
    aux_ref[0:obs, :] = jnp.where(lane < count, 1.0, 0.0)
    base = grid_pos * obs_blocks + place * obs
    even = jnp.broadcast_to(lax.rem(grid_pos, 2), mid_ref.shape) == 0
    low = jnp.where(even, cross_ref[...], chip_ref[...])
    high = jnp.where(even, chip_ref[...], cross_ref[...])
    pairs = jnp.concatenate([low, mid_ref[...], high], axis=0) - base
    index = lax.broadcasted_iota(jnp.int32, (blocks_dev, LANES), 0)
    centers = jnp.concatenate(
        [
            index + lax.rem(grid_pos + grid_count + step, grid_count) * blocks_dev
            for step in (-1, 0, 1)
        ],
        axis=0,
    ).astype(jnp.float32) + 0.5
    for copy in copies:
        copy.wait()
    blocks = 3 * blocks_dev
    slot = lax.broadcasted_iota(jnp.int32, (blocks, LANES), 1)
    found = jnp.zeros((blocks, LANES), jnp.int32)
    chosen = jnp.full((blocks, LANES), obs, jnp.int32)
    for o in range(obs):
        hit = jnp.max(jnp.where(pairs == o, 1.0, 0.0), axis=1, keepdims=True)
        hit = jnp.broadcast_to(hit, (blocks, LANES)).astype(jnp.int32)
        chosen = jnp.where(slot == jnp.where(hit > 0, found, -1), o, chosen)
        found = found + hit
        gap = jnp.abs(pos_ref[o : o + 1, :] - centers)
        distance = jnp.minimum(gap, nb_total - gap)
        relative = distance * (1.0 / LOCR)
        weight = prec_ref[o : o + 1, :] * jnp.exp(-0.5 * relative * relative)
        out_ref[pl.ds(o, blocks, stride=obs), :] = weight
    out_ref[blocks * obs :, :] = jnp.zeros((out_ref.shape[0] - blocks * obs, LANES), jnp.float32)
    table_ref[0:blocks] = jnp.where(slot == COUNT, found, chosen)
    table_ref[blocks:] = jnp.full((table_ref.shape[0] - blocks, LANES), obs, jnp.int32)
    copy = pltpu.make_async_copy(table_ref, list_ref, sems.at[3])
    copy.start()
    copy.wait()
    most = -(-obs // UNIT)
    for group in range(3):
        at = 0
        for b in range(group * blocks_dev, (group + 1) * blocks_dev):
            for k in range(most):
                item_ref[group, at + k] = b * SPAN + k
            at = at + lax.shift_right_logical(list_ref[b, COUNT] + UNIT - 1, 2)
        for k in range(TURN):
            item_ref[group, at + k] = (group + 1) * blocks_dev * SPAN + most
        item_ref[group, ROOM - 1] = at


def accumulate(members, obs, group, blocks, list_ref, item_ref, d_ref, w_ref, acc_ref):
    rows = d_ref.shape[1]
    acc_ref[...] = jnp.zeros(acc_ref.shape, jnp.float32)

    def step(turn, carry):
        for u in range(TURN):
            item = item_ref[group, turn * TURN + u]
            b = lax.shift_right_logical(item, 4)
            first = lax.bitwise_and(item, SPAN - 1) * UNIT
            full, scaled = [], []
            for k in range(UNIT):
                o = list_ref[b, first + k]
                d = d_ref[o]
                row = w_ref[pl.ds(b * obs + o, 1), :]
                w = jnp.broadcast_to(row, (16, LANES)).astype(jnp.bfloat16)
                full.append(d)
                scaled.append((d[:members].reshape(members // 16, 16, LANES) * w[None]).reshape(members, LANES))
            at = pl.multiple_of((b - group * blocks) * members, 16)
            acc_ref[pl.ds(at, members), 0:rows] += lax.dot_general(
                jnp.concatenate(scaled, axis=1),
                jnp.concatenate(full, axis=1),
                (((1,), (1,)), ((), ())),
                preferred_element_type=jnp.float32,
            )
        return carry

    lax.fori_loop(0, (item_ref[group, ROOM - 1] + TURN - 1) // TURN, step, 0)


def packed_system(members, blocks, acc_ref, out_ref):
    half = members // 2
    lane = lax.broadcasted_iota(jnp.int32, (half, LANES), 1)
    for b in range(blocks):
        top = acc_ref[b * members : b * members + half, :]
        bottom = acc_ref[b * members + half : (b + 1) * members, :]
        corner = pltpu.roll(bottom, LANES - members, 1)
        force = pltpu.roll(bottom, 2, 1)
        value = jnp.where(lane >= members + 2, force, top)
        value = jnp.where(lane >= LANES - half, corner, value)
        out_ref[b * half : (b + 1) * half, :] = value.astype(out_ref.dtype)


def cross_kernel(members, obs, blocks, list_ref, item_ref, prior_ref, aux_ref, w_ref, d_ref, out_ref, early_ref, dev_ref, acc_ref):
    rows = d_ref.shape[1]
    total = prior_ref[0, 0:obs].astype(jnp.float32)
    for i in range(1, members):
        total = total + prior_ref[i, 0:obs].astype(jnp.float32)
    mean = total / members
    valid = aux_ref[0:obs, :] > 0.0
    for i in range(members):
        dev_ref[i * PITCH : i * PITCH + obs, :] = jnp.where(
            valid, prior_ref[i, 0:obs].astype(jnp.float32) - mean, 0.0
        )
    departure = jnp.where(valid, aux_ref[obs : 2 * obs, :] - mean, 0.0)
    high = departure.astype(jnp.bfloat16).astype(jnp.float32)
    dev_ref[members * PITCH : members * PITCH + obs, :] = high
    dev_ref[(members + 1) * PITCH : (members + 1) * PITCH + obs, :] = departure - high
    dev_ref[(members + 2) * PITCH :, :] = jnp.zeros(((rows - members - 2) * PITCH, LANES), jnp.float32)
    for o in range(obs):
        d_ref[o] = dev_ref[pl.ds(o, rows, stride=PITCH), :].astype(jnp.bfloat16)
    d_ref[obs] = jnp.zeros((rows, LANES), jnp.bfloat16)
    place = lax.axis_index("grid")
    group = 2 * lax.rem(place, 2)
    accumulate(members, obs, group, blocks, list_ref, item_ref, d_ref, w_ref, acc_ref)
    packed_system(members, blocks, acc_ref, out_ref)

    @pl.when(place == 0)
    def _():
        accumulate(members, obs, 2 - group, blocks, list_ref, item_ref, d_ref, w_ref, acc_ref)
        packed_system(members, blocks, acc_ref, early_ref)


def chip_kernel(members, obs, blocks, list_ref, item_ref, d_ref, w_ref, early_ref, out_ref, acc_ref):
    place = lax.axis_index("grid")

    @pl.when(place == 0)
    def _():
        out_ref[...] = early_ref[...]

    @pl.when(place != 0)
    def _():
        group = 2 - 2 * lax.rem(place, 2)
        accumulate(members, obs, group, blocks, list_ref, item_ref, d_ref, w_ref, acc_ref)
        packed_system(members, blocks, acc_ref, out_ref)


def own_kernel(members, obs, blocks, list_ref, item_ref, d_ref, w_ref, out_ref, acc_ref):
    accumulate(members, obs, 1, blocks, list_ref, item_ref, d_ref, w_ref, acc_ref)
    packed_system(members, blocks, acc_ref, out_ref)


def state_kernel(members, part_ref, dev_ref, mean_ref, wide_ref):
    rows = mean_ref.shape[0]
    first = part_ref.shape[1] - rows
    total = part_ref[0, first:].astype(jnp.float32)
    for i in range(1, members):
        total = total + part_ref[i, first:].astype(jnp.float32)
    mean = total / members
    mean_ref[...] = mean
    for i in range(members):
        wide_ref[i * rows : (i + 1) * rows, :] = part_ref[i, first:].astype(jnp.float32) - mean
    for k in range(rows):
        dev_ref[:, k * LANES : (k + 1) * LANES] = wide_ref[pl.ds(k, members, stride=rows), :].astype(jnp.bfloat16)


def merge_kernel(own_ref, low_ref, high_ref, out_ref):
    total = own_ref[...] + low_ref[...].astype(jnp.float32) + high_ref[...].astype(jnp.float32)
    out_ref[...] = total.astype(jnp.bfloat16)


def finish_kernel(members, owned, parts, system_ref, dev_ref, mean_ref, out_ref, wide_ref):
    half = members // 2
    rows_out = mean_ref.shape[0]
    total = system_ref[0].astype(jnp.float32)
    for m in range(1, parts):
        total = total + system_ref[m].astype(jnp.float32)
    rows = lax.broadcasted_iota(jnp.int32, (members, members), 0)
    cols = lax.broadcasted_iota(jnp.int32, (members, members), 1)
    identity = jnp.where(rows == cols, 1.0, 0.0)
    lane = lax.broadcasted_iota(jnp.int32, (half, LANES), 1)

    def split(value):
        top = value.astype(jnp.bfloat16)
        return top, (value - top.astype(jnp.float32)).astype(jnp.bfloat16)

    def dot(a, b):
        (a_top, a_low), (b_top, b_low) = split(a), split(b)

        def one(x, y):
            return jnp.dot(x, y, preferred_element_type=jnp.float32)

        return one(a_top, b_top) + (one(a_top, b_low) + one(a_low, b_top))

    y_iter, z_iter, bound, force = [], [], [], []
    for r in range(owned):
        part = total[r * half : (r + 1) * half]
        square = jnp.concatenate([part, jnp.zeros((LANES - half, LANES), jnp.float32)], axis=0)
        below = jnp.transpose(square)[half : 2 * half]
        right = pltpu.roll(part, members, 1)
        bottom = jnp.where(lane < half, below, right)
        system = jnp.concatenate([part, bottom], axis=0)[:, :members]
        system = system + (members - 1) / inflation * identity
        sums = jnp.sum(jnp.abs(system), axis=1, keepdims=True)
        bound.append(jnp.max(sums, axis=0, keepdims=True))
        y_iter.append(system / bound[r])
        turned = jnp.transpose(square)
        sums_hl = turned[members : members + 8] + pltpu.roll(turned[members : members + 8], 7, 0)
        low = jnp.broadcast_to(sums_hl[2:3], (8, LANES))
        row = jnp.broadcast_to(sums_hl[0:1], (8, LANES))
        lane8 = lax.broadcasted_iota(jnp.int32, (8, LANES), 1)
        row = jnp.where(lane8 < half, row, pltpu.roll(low, half, 1))
        force.append(row[:, :members])
    for sweep in range(NSIT):
        if sweep == 0:
            factor = [1.5 * identity - 0.5 * y for y in y_iter]
            z_next = factor
        else:
            factor = [1.5 * identity - 0.5 * dot(z, y) for z, y in zip(z_iter, y_iter)]
            z_next = [dot(f, z) for f, z in zip(factor, z_iter)]
        if sweep + 1 < NSIT:
            y_iter = [dot(y, f) for y, f in zip(y_iter, factor)]
        else:
            before = [dot(row, z) for row, z in zip(force, z_iter)]
            before = [dot(row, f) for row, f in zip(before, factor)]
        z_iter = z_next
    for r in range(owned):
        weight = dot(before[r], z_iter[r])[0:1] / bound[r]
        turned = math.sqrt(members - 1) * (z_iter[r] / jnp.sqrt(bound[r])) + weight
        turned = turned.astype(jnp.bfloat16)
        for k in range(r, rows_out, owned):
            moved = jnp.dot(
                turned, dev_ref[:, k * LANES : (k + 1) * LANES], preferred_element_type=jnp.float32
            )
            wide_ref[pl.ds(k, members, stride=rows_out), :] = mean_ref[k : k + 1, :] + moved
    out_ref[...] = wide_ref[...].astype(jnp.bfloat16)


def unpack_kernel(owned, part_ref, out_ref):
    parts, local, rows, _ = part_ref.shape
    for i in range(local):
        groups = []
        for m in range(parts):
            value = part_ref[m, i].astype(jnp.float32)
            groups.append(
                jnp.concatenate([value[k : k + owned] for k in range(0, rows, owned)], axis=1)
            )
        out_ref[i] = jnp.concatenate(groups, axis=0).astype(out_ref.dtype)


def per_device(ens_state, obs_prior, obs_value, obs_prec, obs_len, pair_block, obs_pos):
    mem_count = lax.axis_size("mem")
    grid_count = lax.axis_size("grid")
    local = ens_state.shape[0]
    members = mem_count * local
    blocks_dev = ens_state.shape[1]
    obs_blocks = obs_prior.shape[1]
    owned = blocks_dev // mem_count
    obs = obs_blocks // mem_count
    half = members // 2
    nb_total = blocks_dev * grid_count
    vmem = pl.BlockSpec(memory_space=pltpu.VMEM)
    anywhere = pl.BlockSpec(memory_space=pl.ANY)
    scalars = pl.BlockSpec(memory_space=pltpu.SMEM)

    pieces = ens_state.shape[2] // LANES

    def near(value):
        return pltpu.with_memory_space_constraint(value, pltpu.VMEM)

    extra = pieces * owned

    def scalar(value):
        return pltpu.with_memory_space_constraint(value, pltpu.SMEM)

    def far(value):
        return pltpu.with_memory_space_constraint(value, pltpu.HBM)

    packed = pl.pallas_call(
        functools.partial(pack_kernel, mem_count, obs, owned),
        out_shape=jax.ShapeDtypeStruct((mem_count, local, obs + extra, LANES), obs_prior.dtype),
        in_specs=[pl.BlockSpec(memory_space=pltpu.HBM), pl.BlockSpec(memory_space=pltpu.HBM)],
        out_specs=pl.BlockSpec(memory_space=pltpu.HBM),
        scratch_shapes=[
            pltpu.VMEM((mem_count, local, obs, LANES), obs_prior.dtype),
            pltpu.VMEM(ens_state.shape, ens_state.dtype),
            pltpu.VMEM((mem_count, local, extra, LANES), ens_state.dtype),
            pltpu.SemaphoreType.DMA((2, mem_count)),
            pltpu.SemaphoreType.DMA((2,)),
        ],
        compiler_params=pltpu.CompilerParams(vmem_limit_bytes=16 * 2**20),
        name="pack",
    )(far(obs_prior), far(ens_state))
    prior = lax.all_to_all(packed, "mem", split_axis=0, concat_axis=0, tiled=True)
    prior = prior.reshape(members, obs + extra, LANES)
    pairs_cross = swap(pair_block, True)
    pairs_chip = swap(pair_block, False)

    blocks = 3 * blocks_dev
    weights, aux, lists, items = pl.pallas_call(
        functools.partial(weight_kernel, float(nb_total), obs),
        out_shape=(
            pltpu.VMEM(((blocks + 1) * obs + 8, LANES), jnp.float32),
            pltpu.VMEM((2 * obs, LANES), jnp.float32),
            pltpu.SMEM((blocks + 8, LANES), jnp.int32),
            pltpu.SMEM((3, ROOM), jnp.int32),
        ),
        in_specs=[pl.BlockSpec(memory_space=pltpu.SMEM), vmem, vmem, vmem, anywhere, anywhere, anywhere],
        out_specs=(vmem, vmem, scalars, scalars),
        scratch_shapes=[
            pltpu.VMEM((obs, LANES), jnp.float32),
            pltpu.VMEM((obs, LANES), jnp.float32),
            pltpu.VMEM((blocks + 8, LANES), jnp.int32),
            pltpu.SemaphoreType.DMA((4,)),
        ],
        compiler_params=pltpu.CompilerParams(vmem_limit_bytes=16 * 2**20),
        name="weights",
    )(obs_len, near(pairs_cross), pair_block, near(pairs_chip), obs_prec, obs_pos, obs_value)

    rows = -(-(members + 2) // 16) * 16
    system = pltpu.VMEM((blocks_dev * half, LANES), jnp.bfloat16)
    d_all, to_cross, early = pl.pallas_call(
        functools.partial(cross_kernel, members, obs, blocks_dev),
        out_shape=(pltpu.VMEM((obs + 1, rows, LANES), jnp.bfloat16), system, system),
        in_specs=[scalars, scalars, vmem, vmem, vmem],
        out_specs=(vmem, vmem, vmem),
        scratch_shapes=[
            pltpu.VMEM((rows * PITCH, LANES), jnp.float32),
            pltpu.VMEM(((blocks_dev + 1) * members, LANES), jnp.float32),
        ],
        compiler_params=pltpu.CompilerParams(vmem_limit_bytes=16 * 2**20),
        name="cross",
    )(scalar(lists), scalar(items), near(prior), near(aux), near(weights))
    from_cross = swap(to_cross, True)

    def later(kernel, more, dtype):
        return pl.pallas_call(
            functools.partial(kernel, members, obs, blocks_dev),
            out_shape=pltpu.VMEM((blocks_dev * half, LANES), dtype),
            in_specs=[scalars, scalars, vmem, vmem] + [vmem] * len(more),
            out_specs=vmem,
            scratch_shapes=[pltpu.VMEM(((blocks_dev + 1) * members, LANES), jnp.float32)],
            compiler_params=pltpu.CompilerParams(vmem_limit_bytes=16 * 2**20),
        )(scalar(lists), scalar(items), near(d_all), near(weights), *(near(value) for value in more))

    to_chip = later(chip_kernel, (early,), jnp.bfloat16)
    from_chip = swap(to_chip, False)
    own = later(own_kernel, (), jnp.float32)
    partial = pl.pallas_call(
        merge_kernel,
        out_shape=pltpu.VMEM((blocks_dev * half, LANES), jnp.bfloat16),
        in_specs=[vmem, vmem, vmem],
        out_specs=vmem,
        compiler_params=pltpu.CompilerParams(vmem_limit_bytes=16 * 2**20),
        name="merge",
    )(near(own), near(from_cross), near(from_chip))
    partial = partial.reshape(mem_count, owned * half, LANES)
    swapped = lax.all_to_all(partial, "mem", split_axis=0, concat_axis=0, tiled=True)
    deviation, mean = pl.pallas_call(
        functools.partial(state_kernel, members),
        out_shape=(
            pltpu.VMEM((members, extra * LANES), jnp.bfloat16),
            pltpu.VMEM((extra, LANES), jnp.float32),
        ),
        in_specs=[vmem],
        out_specs=(vmem, vmem),
        scratch_shapes=[pltpu.VMEM((members * extra, LANES), jnp.float32)],
        compiler_params=pltpu.CompilerParams(vmem_limit_bytes=16 * 2**20),
        name="state",
    )(near(prior))
    analysis = pl.pallas_call(
        functools.partial(finish_kernel, members, owned, mem_count),
        out_shape=pltpu.VMEM((members * extra, LANES), jnp.bfloat16),
        in_specs=[vmem, vmem, vmem],
        out_specs=vmem,
        scratch_shapes=[pltpu.VMEM((members * extra, LANES), jnp.float32)],
        compiler_params=pltpu.CompilerParams(vmem_limit_bytes=16 * 2**20),
        name="finish",
    )(near(swapped), near(deviation), near(mean))
    analysis = analysis.reshape(mem_count, local, extra, LANES)
    analysis = lax.all_to_all(analysis, "mem", split_axis=0, concat_axis=0, tiled=True)
    return pl.pallas_call(
        functools.partial(unpack_kernel, owned),
        out_shape=jax.ShapeDtypeStruct(ens_state.shape, jnp.bfloat16),
        in_specs=[vmem],
        out_specs=vmem,
        compiler_params=pltpu.CompilerParams(vmem_limit_bytes=16 * 2**20),
        name="unpack",
    )(near(analysis))


def solution(mesh):
    placed = (
        P("mem", "grid", None),
        P("mem", "grid", None),
        P("grid", None),
        P("grid", None),
        P("grid"),
        P("grid", None),
        P("grid", None),
    )
    return jax.shard_map(per_device, mesh=mesh, in_specs=placed, out_specs=P("mem", "grid", None), check_vma=False)
```

```python
import functools
import math

import jax
import jax.numpy as jnp
from jax import lax
from jax.experimental import pallas as pl
from jax.experimental.pallas import tpu as pltpu
from jax.sharding import PartitionSpec as P

NSIT = 3
LOCR = 8
LANES = 128
COUNT = 127
UNIT = 4
TURN = 28
ROOM = 256
SPAN = 16
PITCH = 49

inflation = 1.1


def swap(value, crossing):
    mem_count = lax.axis_size("mem")
    grid_count = lax.axis_size("grid")
    pairs = []
    for m in range(mem_count):
        for g in range(grid_count):
            if crossing:
                other = m ^ 1, (g + 1 if g % 2 else g - 1) % grid_count
            else:
                other = m, g ^ 1
            pairs.append((m * grid_count + g, other[0] * grid_count + other[1]))
    return lax.ppermute(value, ("mem", "grid"), pairs)


def pack_kernel(parts, size, owned, src_ref, state_all, out_ref, stage_ref, state_ref, rows_ref, sems, last):
    local = state_all.shape[0]
    pieces = state_all.shape[2] // LANES
    inward = [
        pltpu.make_async_copy(src_ref.at[:, m * size : (m + 1) * size, :], stage_ref.at[m], sems.at[0, m])
        for m in range(parts)
    ]
    outward = [
        pltpu.make_async_copy(stage_ref.at[m], out_ref.at[m, :, 0:size, :], sems.at[1, m])
        for m in range(parts)
    ]
    state_in = pltpu.make_async_copy(state_all, state_ref, last.at[0])
    state_out = pltpu.make_async_copy(rows_ref, out_ref.at[:, :, size:, :], last.at[1])
    state_in.start()
    for copy in inward:
        copy.start()
    state_in.wait()
    for i in range(local):
        value = state_ref[i].astype(jnp.float32)
        for m in range(parts):
            rows = value[m * owned : (m + 1) * owned]
            rows = jnp.concatenate(
                [rows[:, q * LANES : (q + 1) * LANES] for q in range(pieces)], axis=0
            )
            rows_ref[m, i] = rows.astype(rows_ref.dtype)
    for m in range(parts):
        inward[m].wait()
        outward[m].start()
    state_out.start()
    for copy in outward:
        copy.wait()
    state_out.wait()


def weight_kernel(nb_total, obs, len_ref, cross_ref, mid_ref, chip_ref, prec_all, pos_all, value_all, out_ref, aux_ref, list_ref, item_ref, prec_ref, pos_ref, table_ref, sems):
    place = lax.axis_index("mem")
    grid_pos = lax.axis_index("grid")
    grid_count = lax.axis_size("grid")
    obs_blocks = prec_all.shape[0]
    blocks_dev = mid_ref.shape[0]
    mine = pl.ds(pl.multiple_of(place * obs, 8), obs)
    copies = [
        pltpu.make_async_copy(prec_all.at[mine], prec_ref, sems.at[0]),
        pltpu.make_async_copy(pos_all.at[mine], pos_ref, sems.at[1]),
        pltpu.make_async_copy(value_all.at[mine], aux_ref.at[obs : 2 * obs], sems.at[2]),
    ]
    for copy in copies:
        copy.start()
    row = lax.broadcasted_iota(jnp.int32, (obs, LANES), 0)
    count = jnp.zeros((obs, LANES), jnp.int32)
    for o in range(obs):
        count = jnp.where(row == o, len_ref[place * obs + o], count)
    lane = lax.broadcasted_iota(jnp.int32, (obs, LANES), 1)
    aux_ref[0:obs, :] = jnp.where(lane < count, 1.0, 0.0)
    base = grid_pos * obs_blocks + place * obs
    even = jnp.broadcast_to(lax.rem(grid_pos, 2), mid_ref.shape) == 0
    low = jnp.where(even, cross_ref[...], chip_ref[...])
    high = jnp.where(even, chip_ref[...], cross_ref[...])
    pairs = jnp.concatenate([low, mid_ref[...], high], axis=0) - base
    index = lax.broadcasted_iota(jnp.int32, (blocks_dev, LANES), 0)
    centers = jnp.concatenate(
        [
            index + lax.rem(grid_pos + grid_count + step, grid_count) * blocks_dev
            for step in (-1, 0, 1)
        ],
        axis=0,
    ).astype(jnp.float32) + 0.5
    for copy in copies:
        copy.wait()
    blocks = 3 * blocks_dev
    slot = lax.broadcasted_iota(jnp.int32, (blocks, LANES), 1)
    found = jnp.zeros((blocks, LANES), jnp.int32)
    chosen = jnp.full((blocks, LANES), obs, jnp.int32)
    for o in range(obs):
        hit = jnp.max(jnp.where(pairs == o, 1.0, 0.0), axis=1, keepdims=True)
        hit = jnp.broadcast_to(hit, (blocks, LANES)).astype(jnp.int32)
        chosen = jnp.where(slot == jnp.where(hit > 0, found, -1), o, chosen)
        found = found + hit
        gap = jnp.abs(pos_ref[o : o + 1, :] - centers)
        distance = jnp.minimum(gap, nb_total - gap)
        relative = distance * (1.0 / LOCR)
        weight = prec_ref[o : o + 1, :] * jnp.exp(-0.5 * relative * relative)
        out_ref[pl.ds(o, blocks, stride=obs), :] = weight
    out_ref[blocks * obs :, :] = jnp.zeros((out_ref.shape[0] - blocks * obs, LANES), jnp.float32)
    table_ref[0:blocks] = jnp.where(slot == COUNT, found, chosen)
    table_ref[blocks:] = jnp.full((table_ref.shape[0] - blocks, LANES), obs, jnp.int32)
    copy = pltpu.make_async_copy(table_ref, list_ref, sems.at[3])
    copy.start()
    copy.wait()
    most = -(-obs // UNIT)
    for group in range(3):
        at = 0
        for b in range(group * blocks_dev, (group + 1) * blocks_dev):
            for k in range(most):
                item_ref[group, at + k] = b * SPAN + k
            at = at + lax.shift_right_logical(list_ref[b, COUNT] + UNIT - 1, 2)
        for k in range(TURN):
            item_ref[group, at + k] = (group + 1) * blocks_dev * SPAN + most
        item_ref[group, ROOM - 1] = at


def early_chip(place):
    last = lax.axis_size("grid") - 1
    return (place == 0) | ((lax.rem(place, 2) == 1) & (place != last))


def accumulate(members, obs, group, blocks, list_ref, item_ref, d_ref, w_ref, acc_ref):
    rows = d_ref.shape[1]
    acc_ref[...] = jnp.zeros(acc_ref.shape, jnp.float32)

    def step(turn, carry):
        for u in range(TURN):
            item = item_ref[group, turn * TURN + u]
            b = lax.shift_right_logical(item, 4)
            first = lax.bitwise_and(item, SPAN - 1) * UNIT
            full, scaled = [], []
            for k in range(UNIT):
                o = list_ref[b, first + k]
                d = d_ref[o]
                row = w_ref[pl.ds(b * obs + o, 1), :]
                w = jnp.broadcast_to(row, (16, LANES)).astype(jnp.bfloat16)
                full.append(d)
                scaled.append((d[:members].reshape(members // 16, 16, LANES) * w[None]).reshape(members, LANES))
            at = pl.multiple_of((b - group * blocks) * members, 16)
            acc_ref[pl.ds(at, members), 0:rows] += lax.dot_general(
                jnp.concatenate(scaled, axis=1),
                jnp.concatenate(full, axis=1),
                (((1,), (1,)), ((), ())),
                preferred_element_type=jnp.float32,
            )
        return carry

    lax.fori_loop(0, (item_ref[group, ROOM - 1] + TURN - 1) // TURN, step, 0)


def packed_system(members, blocks, acc_ref, out_ref):
    half = members // 2
    lane = lax.broadcasted_iota(jnp.int32, (half, LANES), 1)
    for b in range(blocks):
        top = acc_ref[b * members : b * members + half, :]
        bottom = acc_ref[b * members + half : (b + 1) * members, :]
        corner = pltpu.roll(bottom, LANES - members, 1)
        force = pltpu.roll(bottom, 2, 1)
        value = jnp.where(lane >= members + 2, force, top)
        value = jnp.where(lane >= LANES - half, corner, value)
        out_ref[b * half : (b + 1) * half, :] = value.astype(out_ref.dtype)


def cross_kernel(members, obs, blocks, list_ref, item_ref, prior_ref, aux_ref, w_ref, d_ref, out_ref, early_ref, dev_ref, acc_ref):
    rows = d_ref.shape[1]
    total = prior_ref[0, 0:obs].astype(jnp.float32)
    for i in range(1, members):
        total = total + prior_ref[i, 0:obs].astype(jnp.float32)
    mean = total / members
    valid = aux_ref[0:obs, :] > 0.0
    for i in range(members):
        dev_ref[i * PITCH : i * PITCH + obs, :] = jnp.where(
            valid, prior_ref[i, 0:obs].astype(jnp.float32) - mean, 0.0
        )
    departure = jnp.where(valid, aux_ref[obs : 2 * obs, :] - mean, 0.0)
    high = departure.astype(jnp.bfloat16).astype(jnp.float32)
    dev_ref[members * PITCH : members * PITCH + obs, :] = high
    dev_ref[(members + 1) * PITCH : (members + 1) * PITCH + obs, :] = departure - high
    dev_ref[(members + 2) * PITCH :, :] = jnp.zeros(((rows - members - 2) * PITCH, LANES), jnp.float32)
    for o in range(obs):
        d_ref[o] = dev_ref[pl.ds(o, rows, stride=PITCH), :].astype(jnp.bfloat16)
    d_ref[obs] = jnp.zeros((rows, LANES), jnp.bfloat16)
    place = lax.axis_index("grid")
    group = 2 * lax.rem(place, 2)
    accumulate(members, obs, group, blocks, list_ref, item_ref, d_ref, w_ref, acc_ref)
    packed_system(members, blocks, acc_ref, out_ref)

    @pl.when(early_chip(place))
    def _():
        accumulate(members, obs, 2 - group, blocks, list_ref, item_ref, d_ref, w_ref, acc_ref)
        packed_system(members, blocks, acc_ref, early_ref)


def chip_kernel(members, obs, blocks, list_ref, item_ref, d_ref, w_ref, early_ref, out_ref, acc_ref):
    place = lax.axis_index("grid")

    @pl.when(early_chip(place))
    def _():
        out_ref[...] = early_ref[...]

    @pl.when(jnp.logical_not(early_chip(place)))
    def _():
        group = 2 - 2 * lax.rem(place, 2)
        accumulate(members, obs, group, blocks, list_ref, item_ref, d_ref, w_ref, acc_ref)
        packed_system(members, blocks, acc_ref, out_ref)


def own_kernel(members, obs, blocks, list_ref, item_ref, d_ref, w_ref, out_ref, acc_ref):
    accumulate(members, obs, 1, blocks, list_ref, item_ref, d_ref, w_ref, acc_ref)
    packed_system(members, blocks, acc_ref, out_ref)


def state_kernel(members, part_ref, dev_ref, mean_ref, wide_ref):
    rows = mean_ref.shape[0]
    first = part_ref.shape[1] - rows
    total = part_ref[0, first:].astype(jnp.float32)
    for i in range(1, members):
        total = total + part_ref[i, first:].astype(jnp.float32)
    mean = total / members
    mean_ref[...] = mean
    for i in range(members):
        wide_ref[i * rows : (i + 1) * rows, :] = part_ref[i, first:].astype(jnp.float32) - mean
    for k in range(rows):
        dev_ref[:, k * LANES : (k + 1) * LANES] = wide_ref[pl.ds(k, members, stride=rows), :].astype(jnp.bfloat16)


def merge_kernel(own_ref, low_ref, high_ref, out_ref):
    total = own_ref[...] + low_ref[...].astype(jnp.float32) + high_ref[...].astype(jnp.float32)
    out_ref[...] = total.astype(jnp.bfloat16)


def finish_kernel(members, owned, parts, system_ref, dev_ref, mean_ref, out_ref, wide_ref):
    half = members // 2
    rows_out = mean_ref.shape[0]
    total = system_ref[0].astype(jnp.float32)
    for m in range(1, parts):
        total = total + system_ref[m].astype(jnp.float32)
    rows = lax.broadcasted_iota(jnp.int32, (members, members), 0)
    cols = lax.broadcasted_iota(jnp.int32, (members, members), 1)
    identity = jnp.where(rows == cols, 1.0, 0.0)
    lane = lax.broadcasted_iota(jnp.int32, (half, LANES), 1)

    def split(value):
        top = value.astype(jnp.bfloat16)
        return top, (value - top.astype(jnp.float32)).astype(jnp.bfloat16)

    def dot(a, b):
        (a_top, a_low), (b_top, b_low) = split(a), split(b)

        def one(x, y):
            return jnp.dot(x, y, preferred_element_type=jnp.float32)

        return one(a_top, b_top) + (one(a_top, b_low) + one(a_low, b_top))

    y_iter, z_iter, bound, force = [], [], [], []
    for r in range(owned):
        part = total[r * half : (r + 1) * half]
        square = jnp.concatenate([part, jnp.zeros((LANES - half, LANES), jnp.float32)], axis=0)
        below = jnp.transpose(square)[half : 2 * half]
        right = pltpu.roll(part, members, 1)
        bottom = jnp.where(lane < half, below, right)
        system = jnp.concatenate([part, bottom], axis=0)[:, :members]
        system = system + (members - 1) / inflation * identity
        sums = jnp.sum(jnp.abs(system), axis=1, keepdims=True)
        bound.append(jnp.max(sums, axis=0, keepdims=True))
        y_iter.append(system / bound[r])
        turned = jnp.transpose(square)
        sums_hl = turned[members : members + 8] + pltpu.roll(turned[members : members + 8], 7, 0)
        low = jnp.broadcast_to(sums_hl[2:3], (8, LANES))
        row = jnp.broadcast_to(sums_hl[0:1], (8, LANES))
        lane8 = lax.broadcasted_iota(jnp.int32, (8, LANES), 1)
        row = jnp.where(lane8 < half, row, pltpu.roll(low, half, 1))
        force.append(row[:, :members])
    for sweep in range(NSIT):
        if sweep == 0:
            factor = [1.5 * identity - 0.5 * y for y in y_iter]
            z_next = factor
        else:
            factor = [1.5 * identity - 0.5 * dot(z, y) for z, y in zip(z_iter, y_iter)]
            z_next = [dot(f, z) for f, z in zip(factor, z_iter)]
        if sweep + 1 < NSIT:
            y_iter = [dot(y, f) for y, f in zip(y_iter, factor)]
        else:
            before = [dot(row, z) for row, z in zip(force, z_iter)]
            before = [dot(row, f) for row, f in zip(before, factor)]
        z_iter = z_next
    for r in range(owned):
        weight = dot(before[r], z_iter[r])[0:1] / bound[r]
        turned = math.sqrt(members - 1) * (z_iter[r] / jnp.sqrt(bound[r])) + weight
        turned = turned.astype(jnp.bfloat16)
        for k in range(r, rows_out, owned):
            moved = jnp.dot(
                turned, dev_ref[:, k * LANES : (k + 1) * LANES], preferred_element_type=jnp.float32
            )
            wide_ref[pl.ds(k, members, stride=rows_out), :] = mean_ref[k : k + 1, :] + moved
    out_ref[...] = wide_ref[...].astype(jnp.bfloat16)


def unpack_kernel(owned, part_ref, out_ref):
    parts, local, rows, _ = part_ref.shape
    for i in range(local):
        groups = []
        for m in range(parts):
            value = part_ref[m, i].astype(jnp.float32)
            groups.append(
                jnp.concatenate([value[k : k + owned] for k in range(0, rows, owned)], axis=1)
            )
        out_ref[i] = jnp.concatenate(groups, axis=0).astype(out_ref.dtype)


def per_device(ens_state, obs_prior, obs_value, obs_prec, obs_len, pair_block, obs_pos):
    mem_count = lax.axis_size("mem")
    grid_count = lax.axis_size("grid")
    local = ens_state.shape[0]
    members = mem_count * local
    blocks_dev = ens_state.shape[1]
    obs_blocks = obs_prior.shape[1]
    owned = blocks_dev // mem_count
    obs = obs_blocks // mem_count
    half = members // 2
    nb_total = blocks_dev * grid_count
    vmem = pl.BlockSpec(memory_space=pltpu.VMEM)
    anywhere = pl.BlockSpec(memory_space=pl.ANY)
    scalars = pl.BlockSpec(memory_space=pltpu.SMEM)

    pieces = ens_state.shape[2] // LANES

    def near(value):
        return pltpu.with_memory_space_constraint(value, pltpu.VMEM)

    extra = pieces * owned

    def scalar(value):
        return pltpu.with_memory_space_constraint(value, pltpu.SMEM)

    def far(value):
        return pltpu.with_memory_space_constraint(value, pltpu.HBM)

    packed = pl.pallas_call(
        functools.partial(pack_kernel, mem_count, obs, owned),
        out_shape=jax.ShapeDtypeStruct((mem_count, local, obs + extra, LANES), obs_prior.dtype),
        in_specs=[pl.BlockSpec(memory_space=pltpu.HBM), pl.BlockSpec(memory_space=pltpu.HBM)],
        out_specs=pl.BlockSpec(memory_space=pltpu.HBM),
        scratch_shapes=[
            pltpu.VMEM((mem_count, local, obs, LANES), obs_prior.dtype),
            pltpu.VMEM(ens_state.shape, ens_state.dtype),
            pltpu.VMEM((mem_count, local, extra, LANES), ens_state.dtype),
            pltpu.SemaphoreType.DMA((2, mem_count)),
            pltpu.SemaphoreType.DMA((2,)),
        ],
        compiler_params=pltpu.CompilerParams(vmem_limit_bytes=16 * 2**20),
        name="pack",
    )(far(obs_prior), far(ens_state))
    prior = lax.all_to_all(packed, "mem", split_axis=0, concat_axis=0, tiled=True)
    prior = prior.reshape(members, obs + extra, LANES)
    pairs_cross = swap(pair_block, True)
    pairs_chip = swap(pair_block, False)

    blocks = 3 * blocks_dev
    weights, aux, lists, items = pl.pallas_call(
        functools.partial(weight_kernel, float(nb_total), obs),
        out_shape=(
            pltpu.VMEM(((blocks + 1) * obs + 8, LANES), jnp.float32),
            pltpu.VMEM((2 * obs, LANES), jnp.float32),
            pltpu.SMEM((blocks + 8, LANES), jnp.int32),
            pltpu.SMEM((3, ROOM), jnp.int32),
        ),
        in_specs=[pl.BlockSpec(memory_space=pltpu.SMEM), vmem, vmem, vmem, anywhere, anywhere, anywhere],
        out_specs=(vmem, vmem, scalars, scalars),
        scratch_shapes=[
            pltpu.VMEM((obs, LANES), jnp.float32),
            pltpu.VMEM((obs, LANES), jnp.float32),
            pltpu.VMEM((blocks + 8, LANES), jnp.int32),
            pltpu.SemaphoreType.DMA((4,)),
        ],
        compiler_params=pltpu.CompilerParams(vmem_limit_bytes=16 * 2**20),
        name="weights",
    )(obs_len, near(pairs_cross), pair_block, near(pairs_chip), obs_prec, obs_pos, obs_value)

    rows = -(-(members + 2) // 16) * 16
    system = pltpu.VMEM((blocks_dev * half, LANES), jnp.bfloat16)
    d_all, to_cross, early = pl.pallas_call(
        functools.partial(cross_kernel, members, obs, blocks_dev),
        out_shape=(pltpu.VMEM((obs + 1, rows, LANES), jnp.bfloat16), system, system),
        in_specs=[scalars, scalars, vmem, vmem, vmem],
        out_specs=(vmem, vmem, vmem),
        scratch_shapes=[
            pltpu.VMEM((rows * PITCH, LANES), jnp.float32),
            pltpu.VMEM(((blocks_dev + 1) * members, LANES), jnp.float32),
        ],
        compiler_params=pltpu.CompilerParams(vmem_limit_bytes=16 * 2**20),
        name="cross",
    )(scalar(lists), scalar(items), near(prior), near(aux), near(weights))
    from_cross = swap(to_cross, True)

    def later(kernel, more, dtype):
        return pl.pallas_call(
            functools.partial(kernel, members, obs, blocks_dev),
            out_shape=pltpu.VMEM((blocks_dev * half, LANES), dtype),
            in_specs=[scalars, scalars, vmem, vmem] + [vmem] * len(more),
            out_specs=vmem,
            scratch_shapes=[pltpu.VMEM(((blocks_dev + 1) * members, LANES), jnp.float32)],
            compiler_params=pltpu.CompilerParams(vmem_limit_bytes=16 * 2**20),
        )(scalar(lists), scalar(items), near(d_all), near(weights), *(near(value) for value in more))

    to_chip = later(chip_kernel, (early,), jnp.bfloat16)
    from_chip = swap(to_chip, False)
    own = later(own_kernel, (), jnp.float32)
    partial = pl.pallas_call(
        merge_kernel,
        out_shape=pltpu.VMEM((blocks_dev * half, LANES), jnp.bfloat16),
        in_specs=[vmem, vmem, vmem],
        out_specs=vmem,
        compiler_params=pltpu.CompilerParams(vmem_limit_bytes=16 * 2**20),
        name="merge",
    )(near(own), near(from_cross), near(from_chip))
    partial = partial.reshape(mem_count, owned * half, LANES)
    swapped = lax.all_to_all(partial, "mem", split_axis=0, concat_axis=0, tiled=True)
    deviation, mean = pl.pallas_call(
        functools.partial(state_kernel, members),
        out_shape=(
            pltpu.VMEM((members, extra * LANES), jnp.bfloat16),
            pltpu.VMEM((extra, LANES), jnp.float32),
        ),
        in_specs=[vmem],
        out_specs=(vmem, vmem),
        scratch_shapes=[pltpu.VMEM((members * extra, LANES), jnp.float32)],
        compiler_params=pltpu.CompilerParams(vmem_limit_bytes=16 * 2**20),
        name="state",
    )(near(prior))
    analysis = pl.pallas_call(
        functools.partial(finish_kernel, members, owned, mem_count),
        out_shape=pltpu.VMEM((members * extra, LANES), jnp.bfloat16),
        in_specs=[vmem, vmem, vmem],
        out_specs=vmem,
        scratch_shapes=[pltpu.VMEM((members * extra, LANES), jnp.float32)],
        compiler_params=pltpu.CompilerParams(vmem_limit_bytes=16 * 2**20),
        name="finish",
    )(near(swapped), near(deviation), near(mean))
    analysis = analysis.reshape(mem_count, local, extra, LANES)
    analysis = lax.all_to_all(analysis, "mem", split_axis=0, concat_axis=0, tiled=True)
    return pl.pallas_call(
        functools.partial(unpack_kernel, owned),
        out_shape=jax.ShapeDtypeStruct(ens_state.shape, jnp.bfloat16),
        in_specs=[vmem],
        out_specs=vmem,
        compiler_params=pltpu.CompilerParams(vmem_limit_bytes=16 * 2**20),
        name="unpack",
    )(near(analysis))


def solution(mesh):
    placed = (
        P("mem", "grid", None),
        P("mem", "grid", None),
        P("grid", None),
        P("grid", None),
        P("grid"),
        P("grid", None),
        P("grid", None),
    )
    return jax.shard_map(per_device, mesh=mesh, in_specs=placed, out_specs=P("mem", "grid", None), check_vma=False)
```

```python
import functools
import math

import jax
import jax.numpy as jnp
from jax import lax
from jax.experimental import pallas as pl
from jax.experimental.pallas import tpu as pltpu
from jax.sharding import PartitionSpec as P

NSIT = 3
LOCR = 8
LANES = 128
COUNT = 127
UNIT = 4
TURN = 28
ROOM = 256
SPAN = 16
PITCH = 49

inflation = 1.1


def swap(value, crossing):
    mem_count = lax.axis_size("mem")
    grid_count = lax.axis_size("grid")
    pairs = []
    for m in range(mem_count):
        for g in range(grid_count):
            if crossing:
                other = m ^ 1, (g + 1 if g % 2 else g - 1) % grid_count
            else:
                other = m, g ^ 1
            pairs.append((m * grid_count + g, other[0] * grid_count + other[1]))
    return lax.ppermute(value, ("mem", "grid"), pairs)


def pack_kernel(parts, size, owned, src_ref, state_all, out_ref, stage_ref, state_ref, rows_ref, sems, last):
    local = state_all.shape[0]
    pieces = state_all.shape[2] // LANES
    inward = [
        pltpu.make_async_copy(src_ref.at[:, m * size : (m + 1) * size, :], stage_ref.at[m], sems.at[0, m])
        for m in range(parts)
    ]
    outward = [
        pltpu.make_async_copy(stage_ref.at[m], out_ref.at[m, :, 0:size, :], sems.at[1, m])
        for m in range(parts)
    ]
    state_in = pltpu.make_async_copy(state_all, state_ref, last.at[0])
    state_out = pltpu.make_async_copy(rows_ref, out_ref.at[:, :, size:, :], last.at[1])
    state_in.start()
    for copy in inward:
        copy.start()
    state_in.wait()
    for i in range(local):
        value = state_ref[i].astype(jnp.float32)
        for m in range(parts):
            rows = value[m * owned : (m + 1) * owned]
            rows = jnp.concatenate(
                [rows[:, q * LANES : (q + 1) * LANES] for q in range(pieces)], axis=0
            )
            rows_ref[m, i] = rows.astype(rows_ref.dtype)
    for m in range(parts):
        inward[m].wait()
        outward[m].start()
    state_out.start()
    for copy in outward:
        copy.wait()
    state_out.wait()


def weight_kernel(nb_total, obs, len_ref, cross_ref, mid_ref, chip_ref, prec_all, pos_all, value_all, out_ref, aux_ref, list_ref, item_ref, prec_ref, pos_ref, table_ref, sems):
    place = lax.axis_index("mem")
    grid_pos = lax.axis_index("grid")
    grid_count = lax.axis_size("grid")
    obs_blocks = prec_all.shape[0]
    blocks_dev = mid_ref.shape[0]
    mine = pl.ds(pl.multiple_of(place * obs, 8), obs)
    copies = [
        pltpu.make_async_copy(prec_all.at[mine], prec_ref, sems.at[0]),
        pltpu.make_async_copy(pos_all.at[mine], pos_ref, sems.at[1]),
        pltpu.make_async_copy(value_all.at[mine], aux_ref.at[obs : 2 * obs], sems.at[2]),
    ]
    for copy in copies:
        copy.start()
    row = lax.broadcasted_iota(jnp.int32, (obs, LANES), 0)
    count = jnp.zeros((obs, LANES), jnp.int32)
    for o in range(obs):
        count = jnp.where(row == o, len_ref[place * obs + o], count)
    lane = lax.broadcasted_iota(jnp.int32, (obs, LANES), 1)
    aux_ref[0:obs, :] = jnp.where(lane < count, 1.0, 0.0)
    base = grid_pos * obs_blocks + place * obs
    even = jnp.broadcast_to(lax.rem(grid_pos, 2), mid_ref.shape) == 0
    low = jnp.where(even, cross_ref[...], chip_ref[...])
    high = jnp.where(even, chip_ref[...], cross_ref[...])
    pairs = jnp.concatenate([low, mid_ref[...], high], axis=0) - base
    index = lax.broadcasted_iota(jnp.int32, (blocks_dev, LANES), 0)
    centers = jnp.concatenate(
        [
            index + lax.rem(grid_pos + grid_count + step, grid_count) * blocks_dev
            for step in (-1, 0, 1)
        ],
        axis=0,
    ).astype(jnp.float32) + 0.5
    for copy in copies:
        copy.wait()
    blocks = 3 * blocks_dev
    slot = lax.broadcasted_iota(jnp.int32, (blocks, LANES), 1)
    found = jnp.zeros((blocks, LANES), jnp.int32)
    chosen = jnp.full((blocks, LANES), obs, jnp.int32)
    for o in range(obs):
        hit = jnp.max(jnp.where(pairs == o, 1.0, 0.0), axis=1, keepdims=True)
        hit = jnp.broadcast_to(hit, (blocks, LANES)).astype(jnp.int32)
        chosen = jnp.where(slot == jnp.where(hit > 0, found, -1), o, chosen)
        found = found + hit
        gap = jnp.abs(pos_ref[o : o + 1, :] - centers)
        distance = jnp.minimum(gap, nb_total - gap)
        relative = distance * (1.0 / LOCR)
        weight = prec_ref[o : o + 1, :] * jnp.exp(-0.5 * relative * relative)
        out_ref[pl.ds(o, blocks, stride=obs), :] = weight
    out_ref[blocks * obs :, :] = jnp.zeros((out_ref.shape[0] - blocks * obs, LANES), jnp.float32)
    table_ref[0:blocks] = jnp.where(slot == COUNT, found, chosen)
    table_ref[blocks:] = jnp.full((table_ref.shape[0] - blocks, LANES), obs, jnp.int32)
    copy = pltpu.make_async_copy(table_ref, list_ref, sems.at[3])
    copy.start()
    copy.wait()
    most = -(-obs // UNIT)
    for group in range(3):
        at = 0
        for b in range(group * blocks_dev, (group + 1) * blocks_dev):
            for k in range(most):
                item_ref[group, at + k] = b * SPAN + k
            at = at + lax.shift_right_logical(list_ref[b, COUNT] + UNIT - 1, 2)
        for k in range(TURN):
            item_ref[group, at + k] = (group + 1) * blocks_dev * SPAN + most
        item_ref[group, ROOM - 1] = at


def early_chip(place):
    last = lax.axis_size("grid") - 1
    return place != last


def accumulate(members, obs, group, blocks, list_ref, item_ref, d_ref, w_ref, acc_ref):
    rows = d_ref.shape[1]
    acc_ref[...] = jnp.zeros(acc_ref.shape, jnp.float32)

    def step(turn, carry):
        for u in range(TURN):
            item = item_ref[group, turn * TURN + u]
            b = lax.shift_right_logical(item, 4)
            first = lax.bitwise_and(item, SPAN - 1) * UNIT
            full, scaled = [], []
            for k in range(UNIT):
                o = list_ref[b, first + k]
                d = d_ref[o]
                row = w_ref[pl.ds(b * obs + o, 1), :]
                w = jnp.broadcast_to(row, (16, LANES)).astype(jnp.bfloat16)
                full.append(d)
                scaled.append((d[:members].reshape(members // 16, 16, LANES) * w[None]).reshape(members, LANES))
            at = pl.multiple_of((b - group * blocks) * members, 16)
            acc_ref[pl.ds(at, members), 0:rows] += lax.dot_general(
                jnp.concatenate(scaled, axis=1),
                jnp.concatenate(full, axis=1),
                (((1,), (1,)), ((), ())),
                preferred_element_type=jnp.float32,
            )
        return carry

    lax.fori_loop(0, (item_ref[group, ROOM - 1] + TURN - 1) // TURN, step, 0)


def packed_system(members, blocks, acc_ref, out_ref):
    half = members // 2
    lane = lax.broadcasted_iota(jnp.int32, (half, LANES), 1)
    for b in range(blocks):
        top = acc_ref[b * members : b * members + half, :]
        bottom = acc_ref[b * members + half : (b + 1) * members, :]
        corner = pltpu.roll(bottom, LANES - members, 1)
        force = pltpu.roll(bottom, 2, 1)
        value = jnp.where(lane >= members + 2, force, top)
        value = jnp.where(lane >= LANES - half, corner, value)
        out_ref[b * half : (b + 1) * half, :] = value.astype(out_ref.dtype)


def cross_kernel(members, obs, blocks, list_ref, item_ref, prior_ref, aux_ref, w_ref, d_ref, out_ref, early_ref, dev_ref, acc_ref):
    rows = d_ref.shape[1]
    total = prior_ref[0, 0:obs].astype(jnp.float32)
    for i in range(1, members):
        total = total + prior_ref[i, 0:obs].astype(jnp.float32)
    mean = total / members
    valid = aux_ref[0:obs, :] > 0.0
    for i in range(members):
        dev_ref[i * PITCH : i * PITCH + obs, :] = jnp.where(
            valid, prior_ref[i, 0:obs].astype(jnp.float32) - mean, 0.0
        )
    departure = jnp.where(valid, aux_ref[obs : 2 * obs, :] - mean, 0.0)
    high = departure.astype(jnp.bfloat16).astype(jnp.float32)
    dev_ref[members * PITCH : members * PITCH + obs, :] = high
    dev_ref[(members + 1) * PITCH : (members + 1) * PITCH + obs, :] = departure - high
    dev_ref[(members + 2) * PITCH :, :] = jnp.zeros((dev_ref.shape[0] - (members + 2) * PITCH, LANES), jnp.float32)
    for o in range(obs):
        d_ref[o] = dev_ref[pl.ds(o, rows, stride=PITCH), :].astype(jnp.bfloat16)
    d_ref[obs] = jnp.zeros((rows, LANES), jnp.bfloat16)
    place = lax.axis_index("grid")
    group = 2 * lax.rem(place, 2)
    accumulate(members, obs, group, blocks, list_ref, item_ref, d_ref, w_ref, acc_ref)
    packed_system(members, blocks, acc_ref, out_ref)

    @pl.when(early_chip(place))
    def _():
        accumulate(members, obs, 2 - group, blocks, list_ref, item_ref, d_ref, w_ref, acc_ref)
        packed_system(members, blocks, acc_ref, early_ref)


def chip_kernel(members, obs, blocks, list_ref, item_ref, d_ref, w_ref, early_ref, out_ref, acc_ref):
    place = lax.axis_index("grid")

    @pl.when(early_chip(place))
    def _():
        out_ref[...] = early_ref[...]

    @pl.when(jnp.logical_not(early_chip(place)))
    def _():
        group = 2 - 2 * lax.rem(place, 2)
        accumulate(members, obs, group, blocks, list_ref, item_ref, d_ref, w_ref, acc_ref)
        packed_system(members, blocks, acc_ref, out_ref)


def own_kernel(members, obs, blocks, list_ref, item_ref, d_ref, w_ref, out_ref, acc_ref):
    accumulate(members, obs, 1, blocks, list_ref, item_ref, d_ref, w_ref, acc_ref)
    packed_system(members, blocks, acc_ref, out_ref)


def state_kernel(members, part_ref, dev_ref, mean_ref, wide_ref):
    rows = mean_ref.shape[0]
    first = part_ref.shape[1] - rows
    total = part_ref[0, first:].astype(jnp.float32)
    for i in range(1, members):
        total = total + part_ref[i, first:].astype(jnp.float32)
    mean = total / members
    mean_ref[...] = mean
    for i in range(members):
        wide_ref[i * rows : (i + 1) * rows, :] = part_ref[i, first:].astype(jnp.float32) - mean
    for k in range(rows):
        dev_ref[:, k * LANES : (k + 1) * LANES] = wide_ref[pl.ds(k, members, stride=rows), :].astype(jnp.bfloat16)


def merge_kernel(own_ref, low_ref, high_ref, out_ref):
    total = own_ref[...] + low_ref[...].astype(jnp.float32) + high_ref[...].astype(jnp.float32)
    out_ref[...] = total.astype(jnp.bfloat16)


def finish_kernel(members, owned, parts, system_ref, dev_ref, mean_ref, out_ref, wide_ref):
    half = members // 2
    rows_out = mean_ref.shape[0]
    total = system_ref[0].astype(jnp.float32)
    for m in range(1, parts):
        total = total + system_ref[m].astype(jnp.float32)
    rows = lax.broadcasted_iota(jnp.int32, (members, members), 0)
    cols = lax.broadcasted_iota(jnp.int32, (members, members), 1)
    identity = jnp.where(rows == cols, 1.0, 0.0)
    lane = lax.broadcasted_iota(jnp.int32, (half, LANES), 1)

    def split(value):
        top = value.astype(jnp.bfloat16)
        return top, (value - top.astype(jnp.float32)).astype(jnp.bfloat16)

    def dot(a, b):
        (a_top, a_low), (b_top, b_low) = split(a), split(b)

        def one(x, y):
            return jnp.dot(x, y, preferred_element_type=jnp.float32)

        return one(a_top, b_top) + (one(a_top, b_low) + one(a_low, b_top))

    y_iter, z_iter, bound, force = [], [], [], []
    for r in range(owned):
        part = total[r * half : (r + 1) * half]
        square = jnp.concatenate([part, jnp.zeros((LANES - half, LANES), jnp.float32)], axis=0)
        below = jnp.transpose(square)[half : 2 * half]
        right = pltpu.roll(part, members, 1)
        bottom = jnp.where(lane < half, below, right)
        system = jnp.concatenate([part, bottom], axis=0)[:, :members]
        system = system + (members - 1) / inflation * identity
        sums = jnp.sum(jnp.abs(system), axis=1, keepdims=True)
        bound.append(jnp.max(sums, axis=0, keepdims=True))
        y_iter.append(system / bound[r])
        turned = jnp.transpose(square)
        sums_hl = turned[members : members + 8] + pltpu.roll(turned[members : members + 8], 7, 0)
        low = jnp.broadcast_to(sums_hl[2:3], (8, LANES))
        row = jnp.broadcast_to(sums_hl[0:1], (8, LANES))
        lane8 = lax.broadcasted_iota(jnp.int32, (8, LANES), 1)
        row = jnp.where(lane8 < half, row, pltpu.roll(low, half, 1))
        force.append(row[:, :members])
    for sweep in range(NSIT):
        if sweep == 0:
            factor = [1.5 * identity - 0.5 * y for y in y_iter]
            z_next = factor
        else:
            factor = [1.5 * identity - 0.5 * dot(z, y) for z, y in zip(z_iter, y_iter)]
            z_next = [dot(f, z) for f, z in zip(factor, z_iter)]
        if sweep + 1 < NSIT:
            y_iter = [dot(y, f) for y, f in zip(y_iter, factor)]
        else:
            before = [dot(row, z) for row, z in zip(force, z_iter)]
            before = [dot(row, f) for row, f in zip(before, factor)]
        z_iter = z_next
    for r in range(owned):
        weight = dot(before[r], z_iter[r])[0:1] / bound[r]
        turned = math.sqrt(members - 1) * (z_iter[r] / jnp.sqrt(bound[r])) + weight
        turned = turned.astype(jnp.bfloat16)
        for k in range(r, rows_out, owned):
            moved = jnp.dot(
                turned, dev_ref[:, k * LANES : (k + 1) * LANES], preferred_element_type=jnp.float32
            )
            wide_ref[pl.ds(k, members, stride=rows_out), :] = mean_ref[k : k + 1, :] + moved
    out_ref[...] = wide_ref[0 : out_ref.shape[0], :].astype(jnp.bfloat16)


def unpack_kernel(owned, part_ref, out_ref):
    parts, local, rows, _ = part_ref.shape
    for i in range(local):
        groups = []
        for m in range(parts):
            value = part_ref[m, i].astype(jnp.float32)
            groups.append(
                jnp.concatenate([value[k : k + owned] for k in range(0, rows, owned)], axis=1)
            )
        out_ref[i] = jnp.concatenate(groups, axis=0).astype(out_ref.dtype)


def per_device(ens_state, obs_prior, obs_value, obs_prec, obs_len, pair_block, obs_pos):
    mem_count = lax.axis_size("mem")
    grid_count = lax.axis_size("grid")
    local = ens_state.shape[0]
    members = mem_count * local
    blocks_dev = ens_state.shape[1]
    obs_blocks = obs_prior.shape[1]
    owned = blocks_dev // mem_count
    obs = obs_blocks // mem_count
    half = members // 2
    nb_total = blocks_dev * grid_count
    vmem = pl.BlockSpec(memory_space=pltpu.VMEM)
    anywhere = pl.BlockSpec(memory_space=pl.ANY)
    scalars = pl.BlockSpec(memory_space=pltpu.SMEM)

    pieces = ens_state.shape[2] // LANES

    def near(value):
        return pltpu.with_memory_space_constraint(value, pltpu.VMEM)

    extra = pieces * owned

    def scalar(value):
        return pltpu.with_memory_space_constraint(value, pltpu.SMEM)

    def far(value):
        return pltpu.with_memory_space_constraint(value, pltpu.HBM)

    packed = pl.pallas_call(
        functools.partial(pack_kernel, mem_count, obs, owned),
        out_shape=jax.ShapeDtypeStruct((mem_count, local, obs + extra, LANES), obs_prior.dtype),
        in_specs=[pl.BlockSpec(memory_space=pltpu.HBM), pl.BlockSpec(memory_space=pltpu.HBM)],
        out_specs=pl.BlockSpec(memory_space=pltpu.HBM),
        scratch_shapes=[
            pltpu.VMEM((mem_count, local, obs, LANES), obs_prior.dtype),
            pltpu.VMEM(ens_state.shape, ens_state.dtype),
            pltpu.VMEM((mem_count, local, extra, LANES), ens_state.dtype),
            pltpu.SemaphoreType.DMA((2, mem_count)),
            pltpu.SemaphoreType.DMA((2,)),
        ],
        compiler_params=pltpu.CompilerParams(vmem_limit_bytes=16 * 2**20),
        name="pack",
    )(far(obs_prior), far(ens_state))
    prior = lax.all_to_all(packed, "mem", split_axis=0, concat_axis=0, tiled=True)
    prior = prior.reshape(members, obs + extra, LANES)
    pairs_cross = swap(pair_block, True)
    pairs_chip = swap(pair_block, False)

    blocks = 3 * blocks_dev
    weights, aux, lists, items = pl.pallas_call(
        functools.partial(weight_kernel, float(nb_total), obs),
        out_shape=(
            pltpu.VMEM(((blocks + 1) * obs + 8, LANES), jnp.float32),
            pltpu.VMEM((2 * obs, LANES), jnp.float32),
            pltpu.SMEM((blocks + 8, LANES), jnp.int32),
            pltpu.SMEM((3, ROOM), jnp.int32),
        ),
        in_specs=[pl.BlockSpec(memory_space=pltpu.SMEM), vmem, vmem, vmem, anywhere, anywhere, anywhere],
        out_specs=(vmem, vmem, scalars, scalars),
        scratch_shapes=[
            pltpu.VMEM((obs, LANES), jnp.float32),
            pltpu.VMEM((obs, LANES), jnp.float32),
            pltpu.VMEM((blocks + 8, LANES), jnp.int32),
            pltpu.SemaphoreType.DMA((4,)),
        ],
        compiler_params=pltpu.CompilerParams(vmem_limit_bytes=16 * 2**20),
        name="weights",
    )(obs_len, near(pairs_cross), pair_block, near(pairs_chip), obs_prec, obs_pos, obs_value)

    rows = -(-(members + 2) // 16) * 16
    system = pltpu.VMEM((blocks_dev * half, LANES), jnp.bfloat16)
    d_all, to_cross, early = pl.pallas_call(
        functools.partial(cross_kernel, members, obs, blocks_dev),
        out_shape=(pltpu.VMEM((obs + 1, rows, LANES), jnp.bfloat16), system, system),
        in_specs=[scalars, scalars, vmem, vmem, vmem],
        out_specs=(vmem, vmem, vmem),
        scratch_shapes=[
            pltpu.VMEM((rows * PITCH + 56, LANES), jnp.float32),
            pltpu.VMEM(((blocks_dev + 1) * members, LANES), jnp.float32),
        ],
        compiler_params=pltpu.CompilerParams(vmem_limit_bytes=16 * 2**20),
        name="cross",
    )(scalar(lists), scalar(items), near(prior), near(aux), near(weights))
    from_cross = swap(to_cross, True)

    def later(kernel, more, dtype):
        return pl.pallas_call(
            functools.partial(kernel, members, obs, blocks_dev),
            out_shape=pltpu.VMEM((blocks_dev * half, LANES), dtype),
            in_specs=[scalars, scalars, vmem, vmem] + [vmem] * len(more),
            out_specs=vmem,
            scratch_shapes=[pltpu.VMEM(((blocks_dev + 1) * members, LANES), jnp.float32)],
            compiler_params=pltpu.CompilerParams(vmem_limit_bytes=16 * 2**20),
        )(scalar(lists), scalar(items), near(d_all), near(weights), *(near(value) for value in more))

    to_chip = later(chip_kernel, (early,), jnp.bfloat16)
    from_chip = swap(to_chip, False)
    own = later(own_kernel, (), jnp.float32)
    partial = pl.pallas_call(
        merge_kernel,
        out_shape=pltpu.VMEM((blocks_dev * half, LANES), jnp.bfloat16),
        in_specs=[vmem, vmem, vmem],
        out_specs=vmem,
        compiler_params=pltpu.CompilerParams(vmem_limit_bytes=16 * 2**20),
        name="merge",
    )(near(own), near(from_cross), near(from_chip))
    partial = partial.reshape(mem_count, owned * half, LANES)
    swapped = lax.all_to_all(partial, "mem", split_axis=0, concat_axis=0, tiled=True)
    deviation, mean = pl.pallas_call(
        functools.partial(state_kernel, members),
        out_shape=(
            pltpu.VMEM((members, extra * LANES), jnp.bfloat16),
            pltpu.VMEM((extra, LANES), jnp.float32),
        ),
        in_specs=[vmem],
        out_specs=(vmem, vmem),
        scratch_shapes=[pltpu.VMEM((members * extra + extra, LANES), jnp.float32)],
        compiler_params=pltpu.CompilerParams(vmem_limit_bytes=16 * 2**20),
        name="state",
    )(near(prior))
    analysis = pl.pallas_call(
        functools.partial(finish_kernel, members, owned, mem_count),
        out_shape=pltpu.VMEM((members * extra, LANES), jnp.bfloat16),
        in_specs=[vmem, vmem, vmem],
        out_specs=vmem,
        scratch_shapes=[pltpu.VMEM((members * extra + extra, LANES), jnp.float32)],
        compiler_params=pltpu.CompilerParams(vmem_limit_bytes=16 * 2**20),
        name="finish",
    )(near(swapped), near(deviation), near(mean))
    analysis = analysis.reshape(mem_count, local, extra, LANES)
    analysis = lax.all_to_all(analysis, "mem", split_axis=0, concat_axis=0, tiled=True)
    return pl.pallas_call(
        functools.partial(unpack_kernel, owned),
        out_shape=jax.ShapeDtypeStruct(ens_state.shape, jnp.bfloat16),
        in_specs=[vmem],
        out_specs=vmem,
        compiler_params=pltpu.CompilerParams(vmem_limit_bytes=16 * 2**20),
        name="unpack",
    )(near(analysis))


def solution(mesh):
    placed = (
        P("mem", "grid", None),
        P("mem", "grid", None),
        P("grid", None),
        P("grid", None),
        P("grid"),
        P("grid", None),
        P("grid", None),
    )
    return jax.shard_map(per_device, mesh=mesh, in_specs=placed, out_specs=P("mem", "grid", None), check_vma=False)
```
